32 devices in a mesh: groups: 1, col: 8 (over y, x, core), row: 4 (over z).
Axes of the slice: x: 2, y: 2, z: 4, core: 2. Of those that a mesh axis runs over, the one named last changes fastest.
Arguments:
- features: bfloat16 [16384, 128], P(('groups', 'row', 'col')), may hold values from -6 to 6
- adjacency: bfloat16 [256, 64, 5632], P(('groups', 'col'), None, 'row'), may hold values from -0.125 to 0.125
- tile_cols: int32 [256, 88], P(('groups', 'col'), 'row'), may hold values from 0 to 63
- row_counts: int32 [256, 4], P(('groups', 'col'), 'row'), may hold values from 1 to 22, as said below
- weight: bfloat16 [128, 128], replicated, may hold values from -0.5 to 0.5
- bias: float32 [128], replicated, may hold values from -3 to 3
- out_grad: bfloat16 [16384, 128], P(('groups', 'col', 'row')), may hold values from -6 to 6
Outputs:
- activations: bfloat16 [16384, 128], P(('groups', 'col', 'row'))
- feature_grad: bfloat16 [16384, 128], P(('groups', 'row', 'col'))
- weight_grad: float32 [128, 128], P('groups')
- bias_grad: float32 [128], P('groups')
The draws below stay inside these ranges and needn't reach their ends.
Inputs may be any that keep to these rules, and one draw needn't show every extreme that they name: `row_counts`: live slots of a block row come first among its 22 slots on each row index; at least one entry equals 22. `tile_cols`: block column within the source range of row index s // 22.
All inputs are finite; a program needn't handle non-finite values.
Results may differ from the reference program's by a relative error of at most 0.006.
Values may be sent and summed in bfloat16 or wider, within the bound.
A program may use at most 128 MiB of HBM per device.

```python
import math
import jax
import jax.numpy as jnp
from jax import lax

F = 128
TILE = 64
PER_ROW = 22
NODES = 16384
BLOCKS = 256
ROW_BLKS = 32
COL_BLKS = 64
SLOTS = 88
N_COL = 8
N_ROW = 4


def draw_row_counts(key, part):
    key_cap = jax.random.fold_in(key, 11)
    key_count = jax.random.fold_in(key, 12)
    key_full = jax.random.fold_in(key, 13)
    shape_all = (N_COL, ROW_BLKS, N_ROW)
    caps = jax.random.randint(key_cap, (N_COL, 1, N_ROW), max(PER_ROW // 2, 1), PER_ROW + 1)
    counts = jax.random.randint(key_count, shape_all, 1, caps + 1)
    total = N_COL * ROW_BLKS * N_ROW
    chosen = jax.random.randint(key_full, (), 0, total)
    position = jnp.arange(total, dtype=jnp.int32).reshape(shape_all)
    counts = jnp.where(position == chosen, PER_ROW, counts)
    return counts.reshape(N_COL * ROW_BLKS, N_ROW).astype(jnp.int32)


def place_ends(result, key, least, top_value):
    dims = result.shape
    index_at = [jax.random.randint(jax.random.fold_in(key, axis), (), 0, dims[axis]) for axis in range(len(dims))]
    result = result.at[tuple(index_at)].set(least)
    longest = dims.index(max(dims))
    index_at[longest] = (index_at[longest] + 1) % dims[longest]
    return result.at[tuple(index_at)].set(top_value)


def steps_of(key, extent, cuts, least, top_value):
    loudness, own = 1.0, jax.random.fold_in(key, 6)
    for dim, shards_of in cuts:
        heights = jnp.exp(jax.random.uniform(jax.random.fold_in(own, dim), (shards_of,), jnp.float32, least / len(cuts), top_value / len(cuts)))
        loudness = loudness * jnp.repeat(heights, extent[dim] // shards_of).reshape([-1 if axis == dim else 1 for axis in range(len(extent))])
    return loudness


def normal_values(stream_key, shape, deviation, reach, cuts=(), held_as=jnp.bfloat16):
    result = deviation * jax.random.normal(stream_key, shape, jnp.float32)
    if cuts:
        result = result * steps_of(stream_key, shape, cuts, -0.22, 0.18)
    return jnp.clip(result, -reach, reach).astype(held_as)


def setup_inputs(seed: int = 0, part: int = 0) -> dict:
    arg_keys = jax.random.split(jax.random.key(seed), 8)
    part_keys = jax.random.split(jax.random.fold_in(arg_keys[7], part), 8)
    features = normal_values(part_keys[0], (NODES, F), 1.0, 6.0, ((0, 32),))
    adjacency = normal_values(part_keys[1], (BLOCKS, TILE, SLOTS * TILE), (TILE * SLOTS * 2 // 5) ** -0.5, 0.125, ((0, 8), (2, 4)))
    tile_cols = place_ends(jax.random.randint(part_keys[2], (BLOCKS, SLOTS), 0, COL_BLKS), jax.random.fold_in(part_keys[2], 1), 0, COL_BLKS - 1).astype(jnp.int32)
    row_counts = draw_row_counts(jax.random.fold_in(jax.random.fold_in(arg_keys[7], part), 71), part)
    weight = normal_values(arg_keys[4], (F, F), F ** -0.5, 0.5)
    bias = normal_values(arg_keys[5], (F,), 0.5, 3.0, (), jnp.float32)
    out_grad = normal_values(part_keys[6], (NODES, F), 1.0, 6.0, ((0, 32),))
    return dict(features=features, adjacency=adjacency, tile_cols=tile_cols, row_counts=row_counts, weight=weight, bias=bias, out_grad=out_grad)


def silu_slope(preact):
    sigmoid_z = jax.nn.sigmoid(preact)
    return sigmoid_z * (1.0 + preact * (1.0 - sigmoid_z))

def reference(features, adjacency, tile_cols, row_counts, weight, bias, out_grad):
    group = math.gcd(BLOCKS, 16)
    steps_count = BLOCKS // group
    slot_ids = jnp.arange(SLOTS, dtype=jnp.int32)
    source_block = (tile_cols + (slot_ids // PER_ROW * COL_BLKS)[None, :]).astype(jnp.int32)
    slot_counts = jnp.repeat(row_counts, PER_ROW, axis=1)
    is_live = (slot_ids % PER_ROW)[None, :] < slot_counts
    feature_blocks = features.reshape(BLOCKS, TILE, F)
    tile_groups = adjacency.reshape(steps_count, group, TILE, SLOTS, TILE)
    source_groups = source_block.reshape(steps_count, group, SLOTS)
    live_groups = is_live.reshape(steps_count, group, SLOTS)

    def forward_group(packed):
        tile_part, col_part, live_part = packed
        picked = jnp.where(live_part[:, :, None, None], feature_blocks[col_part], jnp.zeros((), features.dtype))
        return jnp.einsum('bisj,bsjf->bif', tile_part.astype(jnp.float32), picked.astype(jnp.float32))
    summed = lax.map(forward_group, (tile_groups, source_groups, live_groups))
    hidden = summed.reshape(NODES, F).astype(jnp.bfloat16)
    preact = jnp.dot(hidden, weight, preferred_element_type=jnp.float32) + bias
    activations = jax.nn.silu(preact).astype(jnp.bfloat16)
    pre_grad = out_grad.astype(jnp.float32) * silu_slope(preact)
    pre_grad_half = pre_grad.astype(jnp.bfloat16)
    scale = 1.0 / math.sqrt(NODES)
    weight_grad = jnp.dot(hidden.T, pre_grad_half, preferred_element_type=jnp.float32) * scale
    bias_grad = lax.optimization_barrier(jnp.sum(pre_grad, axis=0)) * scale
    dest_grad = jnp.dot(pre_grad_half, weight.T, preferred_element_type=jnp.float32).astype(jnp.bfloat16)
    grad_groups = dest_grad.reshape(steps_count, group, TILE, F)

    def backward_group(accum, packed):
        tile_part, col_part, live_part, grad_part = packed
        contrib = jnp.einsum('bisj,bif->bsjf', tile_part.astype(jnp.float32), grad_part.astype(jnp.float32))
        contrib = jnp.where(live_part[:, :, None, None], contrib, jnp.zeros((), contrib.dtype))
        accum = accum.at[col_part.reshape(-1)].add(contrib.reshape(-1, TILE, F))
        return (accum, None)
    start = jnp.zeros((BLOCKS, TILE, F), jnp.float32)
    accum, unused = lax.scan(backward_group, start, (tile_groups, source_groups, live_groups, grad_groups))
    feature_grad = accum.reshape(NODES, F).astype(jnp.bfloat16)
    return (activations, feature_grad, weight_grad, bias_grad)
```

```python
import functools
import math

import jax
import jax.numpy as jnp
from jax import lax
from jax.experimental import pallas as pl
from jax.experimental.pallas import tpu as pltpu
from jax.sharding import PartitionSpec as P

MESH = pl.DeviceIdType.MESH
F32, BF16 = jnp.float32, jnp.bfloat16
MIB = 1024 * 1024


def col_peers(nc):
    c = lax.axis_index("col")
    outer, core, n_out = c // 2, c % 2, nc // 2
    partner = outer * 2 + (1 - core)
    ahead = [lax.rem(outer + d, n_out) * 2 + core for d in range(n_out)]
    behind = [lax.rem(outer - d + n_out, n_out) * 2 + core for d in range(n_out)]
    return c, partner, ahead, behind


def send(src, dst, send_sem, recv_sem, where):
    return pltpu.make_async_remote_copy(
        src_ref=src, dst_ref=dst, send_sem=send_sem, recv_sem=recv_sem,
        device_id=where, device_id_type=MESH,
    )


def enter(nc, nr):
    c, r = lax.axis_index("col"), lax.axis_index("row")
    barrier = pltpu.get_barrier_semaphore()
    for d in range(1, nc):
        pl.semaphore_signal(barrier, inc=1, device_id={"col": lax.rem(c + d, nc)}, device_id_type=MESH)
    for e in range(1, nr):
        pl.semaphore_signal(barrier, inc=1, device_id={"row": lax.rem(r + e, nr)}, device_id_type=MESH)
    pl.semaphore_wait(barrier, nc - 1 + nr - 1)


def forward_kernel(
    nc, nr, scale, cols_ref, counts_ref, feat_hbm, adj_hbm, weight_hbm, bias_hbm, og_hbm,
    grads_ref, wb_ref,
    xg, adj, weight_ref, bias_ref, og_ref, own, part, rbuf, gg, w_out, w_in, w_all,
    in_sem, a_sem, f_send, f_recv, p_send, p_recv, r_send, r_recv, g_send, g_recv, w_send, w_recv, wa_send, wa_recv,
):
    blocks, tile, slot_width = adj.shape
    per_row = slot_width // tile
    chunk = blocks // nr
    rows = chunk * tile
    n_out = nc // 2
    own_blocks = feat_hbm.shape[0]
    c, partner, ahead, behind = col_peers(nc)
    r = lax.axis_index("row")
    row_at = [lax.rem(r + e, nr) for e in range(nr)]

    mine = xg.at[pl.ds(c * own_blocks, own_blocks)]
    first = pltpu.make_async_copy(feat_hbm, mine, in_sem.at[0])
    first.start()
    loads = []
    for e in range(nr):
        t = row_at[(e + 1) % nr]
        cut = pl.ds(t * chunk, chunk)
        load = pltpu.make_async_copy(adj_hbm.at[cut], adj.at[cut], a_sem.at[e])
        load.start()
        loads.append(load)
    small = []
    for n, (src, dst) in enumerate(((weight_hbm, weight_ref), (bias_hbm, bias_ref), (og_hbm, og_ref))):
        load = pltpu.make_async_copy(src, dst, in_sem.at[n + 1])
        load.start()
        small.append(load)

    def blocks_of(col):
        return xg.at[pl.ds(col * own_blocks, own_blocks)]

    xg[nc * own_blocks] = jnp.zeros(xg.shape[1:], xg.dtype)
    first.wait()
    enter(nc, nr)

    copies = []
    for d in range(1, n_out):
        copy = send(blocks_of(c), blocks_of(c), f_send.at[d], f_recv.at[d], {"col": ahead[d]})
        copy.start()
        copies.append(copy)
    pair = []
    copy = send(blocks_of(c), blocks_of(c), p_send.at[0], p_recv.at[0], {"col": partner})
    copy.start()
    pair.append(copy)
    for d in range(1, n_out):
        copies[d - 1].wait_recv()
        came = blocks_of(behind[d])
        copy = send(came, came, p_send.at[d], p_recv.at[d], {"col": partner})
        copy.start()
        pair.append(copy)
    for copy in pair:
        copy.wait_recv()
    for copy in copies + pair:
        copy.wait_send()

    pace = math.gcd(chunk, 4)
    row_copies = []
    for e in range(nr):
        far = (e + 1) % nr
        t = row_at[far]
        loads[e].wait()

        def block_rows(n, carry, t=t, far=far):
            for i in range(pace):
                i = n * pace + i
                b = t * chunk + i
                count = counts_ref[0, b]
                picked = [
                    xg[jnp.where(s < count, cols_ref[s, b], nc * own_blocks)] for s in range(per_row)
                ]
                got = jnp.dot(adj[b], jnp.concatenate(picked, axis=0), preferred_element_type=F32)
                cut = pl.ds(pl.multiple_of(i * tile, tile), tile)
                if far:
                    part[far - 1, cut, :] = got.astype(BF16)
                else:
                    own[cut, :] = got
            return carry

        lax.fori_loop(0, chunk // pace, block_rows, 0)
        if far:
            copy = send(
                part.at[far - 1], rbuf.at[far - 1], r_send.at[far - 1], r_recv.at[far - 1], {"row": t}
            )
            copy.start()
            row_copies.append(copy)
    summed = own[...]
    for copy in row_copies:
        copy.wait_recv()
    for e in range(nr - 1):
        summed = summed + rbuf[e].astype(F32)
    hidden = summed.astype(BF16)
    for load in small:
        load.wait()
    preact = jnp.dot(hidden, weight_ref[...], preferred_element_type=F32) + bias_ref[...]
    sig = jax.nn.sigmoid(preact)
    pre_grad = og_ref[...].astype(F32) * (sig * (1.0 + preact * (1.0 - sig)))
    half = pre_grad.astype(BF16)
    dest = lax.dot_general(
        half, weight_ref[...], (((1,), (1,)), ((), ())), preferred_element_type=F32
    )
    gg[r] = dest.astype(BF16)

    def hop(t, step):
        way = 0 if step > 0 else 1
        return send(gg.at[t], gg.at[t], g_send.at[way, t], g_recv.at[t], {"row": r + step})

    for step in (1, -1):
        @pl.when((r + step >= 0) & (r + step < nr))
        def start_chain(step=step):
            hop(r, step).start()
    grads_ref[pl.ds(nr * rows, rows), :] = (preact * sig).astype(BF16)
    feat = hidden.shape[1]
    cut = feat // nc
    w_out[:, pl.ds(0, cut), :] = scale * lax.dot_general(
        hidden, half, (((0,), (0,)), ((), ())), preferred_element_type=F32
    ).reshape(nc, cut, feat)
    w_out[:, pl.ds(cut, 8), :] = jnp.broadcast_to(
        scale * jnp.sum(pre_grad, axis=0, keepdims=True), (nc, 8, feat)
    )
    w_copies = []
    for d in range(1, nc):
        there = lax.rem(c + d, nc)
        copy = send(w_out.at[there], w_in.at[d - 1], w_send.at[d - 1], w_recv.at[d - 1], {"col": there})
        copy.start()
        w_copies.append(copy)
    for k in range(1, nr):
        if k == min(2, nr - 1):
            total = w_out[c]
            for d in range(1, nc):
                w_copies[d - 1].wait_recv()
                total = total + w_in[d - 1]
            w_all[c] = total
            for d in range(1, nc):
                there = lax.rem(c + d, nc)
                copy = send(w_all.at[c], w_all.at[c], wa_send.at[d - 1], wa_recv.at[d - 1], {"col": there})
                copy.start()
                w_copies.append(copy)
        for step in (1, -1):
            t = r - k * step
            came = (t >= 0) & (t < nr)

            @pl.when(came)
            def arrive(t=t, step=step):
                hop(t, step).wait_recv()

            @pl.when(came & (r + step >= 0) & (r + step < nr))
            def pass_on(t=t, step=step):
                hop(t, step).start()
    for k in range(nr):
        for step in (1, -1):
            t = r - k * step

            @pl.when((t >= 0) & (t < nr) & (r + step >= 0) & (r + step < nr))
            def sent(t=t, step=step):
                hop(t, step).wait_send()
    for copy in w_copies[nc - 1 :]:
        copy.wait_recv()
    for n in range(nc):
        wb_ref[pl.ds(n * cut, cut), :] = w_all[n, pl.ds(0, cut), :]
    wb_ref[pl.ds(feat, 8), :] = w_all[0, pl.ds(cut, 8), :]
    grads_ref[pl.ds(0, nr * rows), :] = gg[...].reshape(nr * rows, feat)
    for copy in row_copies + w_copies:
        copy.wait_send()


def backward_kernel(cols_ref, counts_ref, adj_ref, grad_ref, out_ref, act_out, sem, *accs):
    blocks, tile, slot_width = adj_ref.shape
    per_row = slot_width // tile
    dead = out_ref.shape[0]
    hand_out = pltpu.make_async_copy(grad_ref.at[pl.ds(blocks * tile, act_out.shape[0])], act_out, sem)
    hand_out.start()
    for acc in accs:
        acc[...] = jnp.zeros_like(acc)

    pace = math.gcd(blocks, 4)

    def block_rows(n, carry):
        contribs = []
        for i in range(pace):
            b = n * pace + i
            contribs.append(lax.dot_general(
                adj_ref[b], grad_ref[pl.ds(pl.multiple_of(b * tile, tile), tile), :],
                (((0,), (0,)), ((), ())), preferred_element_type=F32,
            ))
        for s in range(per_row):
            for i in range(pace):
                b = n * pace + i
                acc = accs[i]
                j = jnp.where(s < counts_ref[0, b], cols_ref[s, b], dead)
                acc[j] = acc[j] + contribs[i][s * tile : (s + 1) * tile]
        return carry

    lax.fori_loop(0, blocks // pace, block_rows, 0)
    total = accs[0][pl.ds(0, dead)]
    for acc in accs[1:]:
        total = total + acc[pl.ds(0, dead)]
    out_ref[...] = total.astype(BF16)
    hand_out.wait()


def scatter_kernel(
    nc, nr, part_ref, wb_ref, out_ref, wg_ref, bg_ref,
    from_pair, send_buf, from_chip, w_row,
    p_send, p_recv, s_send, s_recv, wr_send, wr_recv,
):
    n_out = nc // 2
    c, partner, ahead, behind = col_peers(nc)
    r = lax.axis_index("row")
    row_at = [lax.rem(r + e, nr) for e in range(nr)]
    partner_ahead = [x + partner - c for x in ahead]
    enter(nc, nr)

    started = []

    def go(*args):
        copy = send(*args)
        copy.start()
        started.append(copy)
        return copy

    order = list(range(1, n_out)) + [0]
    pair = {}
    for d in order:
        pair[d] = go(part_ref.at[partner_ahead[d]], from_pair.at[d], p_send.at[d], p_recv.at[d], {"col": partner})
    w_row[r] = wb_ref[...]
    w_copies = [
        go(w_row.at[r], w_row.at[r], wr_send.at[e - 1], wr_recv.at[e - 1], {"row": row_at[e]})
        for e in range(1, nr)
    ]
    copies = []
    for d in order:
        pair[d].wait_recv()
        both = part_ref[ahead[d]].astype(F32) + from_pair[d].astype(F32)
        if d:
            send_buf[d - 1] = both.astype(BF16)
            copies.append(go(
                send_buf.at[d - 1], from_chip.at[d - 1], s_send.at[d - 1], s_recv.at[d - 1], {"col": ahead[d]}
            ))
    for copy in copies:
        copy.wait_recv()
    for d in range(1, n_out):
        both = both + from_chip[d - 1].astype(F32)
    out_ref[...] = both.astype(BF16)
    for copy in w_copies:
        copy.wait_recv()
    total = w_row[0]
    for n in range(1, nr):
        total = total + w_row[n]
    feat = wg_ref.shape[0]
    wg_ref[...] = total[:feat]
    bg_ref[...] = total[feat : feat + 1]
    for copy in started:
        copy.wait_send()


def on_device(mesh, features, adjacency, tile_cols, row_counts, weight, bias, out_grad):
    blocks, tile, slot_width = adjacency.shape
    own_rows, feat = features.shape
    nc, nr = mesh.shape["col"], mesh.shape["row"]
    n_out = nc // 2
    col_blocks = nc * own_rows // tile
    scale = 1.0 / math.sqrt(own_rows * nc * nr)
    cut = feat // nc

    vmem = pl.BlockSpec(memory_space=pltpu.VMEM)
    smem = pl.BlockSpec(memory_space=pltpu.SMEM)
    hbm = pl.BlockSpec(memory_space=pltpu.HBM)
    dma = pltpu.SemaphoreType.DMA
    rows = blocks * tile // nr
    tile_flops = 2 * blocks * tile * slot_width * feat
    grads, wb = pl.pallas_call(
        functools.partial(forward_kernel, nc, nr, scale),
        out_shape=(
            jax.ShapeDtypeStruct((blocks * tile + rows, feat), BF16),
            jax.ShapeDtypeStruct((feat + 8, feat), F32),
        ),
        in_specs=[smem, smem, hbm, hbm, hbm, hbm, hbm],
        out_specs=(vmem, vmem),
        scratch_shapes=[
            pltpu.VMEM((col_blocks + 1, tile, feat), BF16),
            pltpu.VMEM(adjacency.shape, BF16),
            pltpu.VMEM((feat, feat), BF16),
            pltpu.VMEM((1, feat), F32),
            pltpu.VMEM((rows, feat), BF16),
            pltpu.VMEM((rows, feat), F32),
            pltpu.VMEM((nr - 1, rows, feat), BF16),
            pltpu.VMEM((nr - 1, rows, feat), BF16),
            pltpu.VMEM((nr, rows, feat), BF16),
            pltpu.VMEM((nc, cut + 8, feat), F32),
            pltpu.VMEM((nc - 1, cut + 8, feat), F32),
            pltpu.VMEM((nc, cut + 8, feat), F32),
            dma((4,)), dma((nr,)), dma((n_out,)), dma((n_out,)), dma((n_out,)), dma((n_out,)),
            dma((nr - 1,)), dma((nr - 1,)), dma((2, nr)), dma((nr,)),
            dma((nc - 1,)), dma((nc - 1,)), dma((nc - 1,)), dma((nc - 1,)),
        ],
        compiler_params=pltpu.CompilerParams(
            collective_id=0, has_side_effects=True, vmem_limit_bytes=56 * MIB
        ),
        cost_estimate=pl.CostEstimate(
            flops=tile_flops, bytes_accessed=adjacency.size * 2, transcendentals=rows * feat
        ),
    )(
        tile_cols.T, row_counts.T, features.reshape(own_rows // tile, tile, feat), adjacency, weight,
        bias.reshape(1, -1), out_grad,
    )

    partial, activations = pl.pallas_call(
        backward_kernel,
        out_shape=(
            jax.ShapeDtypeStruct((col_blocks, tile, feat), BF16),
            jax.ShapeDtypeStruct((rows, feat), BF16),
        ),
        in_specs=[smem, smem, vmem, vmem],
        out_specs=(vmem, hbm),
        scratch_shapes=[dma] + [pltpu.VMEM((col_blocks + 1, tile, feat), F32) for unused in range(4)],
        compiler_params=pltpu.CompilerParams(vmem_limit_bytes=32 * MIB),
        cost_estimate=pl.CostEstimate(
            flops=tile_flops * 8, bytes_accessed=adjacency.size * 2, transcendentals=0
        ),
    )(tile_cols.T, row_counts.T, adjacency, grads)

    feature_grad, weight_grad, bias_grad = pl.pallas_call(
        functools.partial(scatter_kernel, nc, nr),
        out_shape=(
            jax.ShapeDtypeStruct((own_rows, feat), BF16),
            jax.ShapeDtypeStruct((feat, feat), F32),
            jax.ShapeDtypeStruct((1, feat), F32),
        ),
        in_specs=[vmem, vmem],
        out_specs=(vmem, vmem, vmem),
        scratch_shapes=[
            pltpu.VMEM((n_out, own_rows, feat), BF16),
            pltpu.VMEM((n_out - 1, own_rows, feat), BF16),
            pltpu.VMEM((n_out - 1, own_rows, feat), BF16),
            pltpu.VMEM((nr, feat + 8, feat), F32),
            dma((n_out,)), dma((n_out,)), dma((n_out - 1,)), dma((n_out - 1,)),
            dma((nr - 1,)), dma((nr - 1,)),
        ],
        compiler_params=pltpu.CompilerParams(
            collective_id=1, has_side_effects=True, vmem_limit_bytes=20 * MIB
        ),
        cost_estimate=pl.CostEstimate(
            flops=own_rows * nc * feat, bytes_accessed=8 * own_rows * nc * feat, transcendentals=0
        ),
    )(partial.reshape(nc, own_rows, feat), wb)
    return (activations, feature_grad, weight_grad, bias_grad.reshape(-1))


GROUP = 4


def slot_tables(cols_ref, counts_ref, col_blocks, tab_ref):
    per_row, blocks = cols_ref.shape
    slots = per_row * blocks
    groups = pad_groups(slots, col_blocks)

    def iota(shape, axis):
        return lax.broadcasted_iota(jnp.int32, shape, axis)

    def upright(row):
        n = row.shape[1]
        return jnp.sum(jnp.where(iota((n, n), 0) == iota((n, n), 1), row, 0), axis=1, keepdims=True)

    lane = iota((blocks, col_blocks), 1)
    block = iota((blocks, 1), 0)
    counts = upright(counts_ref[...])
    seen = jnp.zeros((blocks, col_blocks), jnp.int32)
    hits, ranks = [], []
    for s in range(per_row):
        hit = jnp.where((upright(cols_ref[pl.ds(s, 1), :]) == lane) & (counts > s), 1, 0)
        hits.append(hit)
        ranks.append(seen)
        seen = seen + hit
    earlier = jnp.zeros((blocks, col_blocks), jnp.int32)
    for b in range(blocks - 1):
        earlier = earlier + jnp.where(block > b, seen[b : b + 1, :], 0)
    sizes = lax.shift_right_logical(jnp.sum(seen, axis=0, keepdims=True) + (GROUP - 1), 2)
    square = (col_blocks, col_blocks)
    starts = jnp.sum(jnp.where(iota(square, 0) < iota(square, 1), upright(sizes), 0), axis=0, keepdims=True)
    place = iota((blocks, GROUP * groups), 1)
    head = iota((blocks, groups), 1) * GROUP
    found = jnp.zeros((blocks, GROUP * groups), jnp.int32)
    fresh = jnp.zeros((blocks, groups), jnp.int32)
    for s in range(per_row):
        rank = jnp.sum(hits[s] * (ranks[s] + earlier), axis=1, keepdims=True)
        at = jnp.sum(hits[s] * (GROUP * starts), axis=1, keepdims=True) + rank
        at = jnp.where(counts > s, at, -1)
        found = found + jnp.where(at == place, slots - (block * per_row + s), 0)
        fresh = fresh + jnp.where((at == head) & (rank == 0), 1, 0)
    found = slots - jnp.sum(found, axis=0, keepdims=True)
    fresh = jnp.sum(fresh, axis=0, keepdims=True)
    last = jnp.where(sizes > 0, starts + sizes - 1, groups)
    n = 0
    for value in (found, fresh):
        for k in range(value.shape[1] // 128):
            tab_ref[pl.ds(n, 1), :] = value[:, k * 128 : (k + 1) * 128]
            n += 1
    tab_ref[pl.ds(n, 1), pl.ds(0, col_blocks)] = last


def pad_groups(slots, col_blocks):
    most = (slots + (GROUP - 1) * min(col_blocks, slots)) // GROUP
    return -(-most // 128) * 128


def layer_kernel(
    nc, nr, scale, cols_hbm, counts_hbm, feat_hbm, adj_hbm, weight_hbm, bias_hbm, og_hbm,
    fg_ref, act_ref, wb_ref,
    cols_s, counts_s, tab_s, cols_v, counts_v, tab_v,
    xg, adj, weight_ref, bias_ref, og_ref, pf, part, near, far, hid, half, gg,
    contrib, runs, pair_out, pair_in, chip_out, chip_in, kept,
    w_out, w_in, w_row, w_all,
    in_sem, a_sem, f_send, f_recv, p_send, p_recv, n_send, n_recv, r_send, r_recv,
    g_send, g_recv, gp_send, gp_recv, gc_send, gc_recv,
    w_send, w_recv, wr_send, wr_recv, wa_send, wa_recv,
):
    blocks, tile, slot_width = adj.shape
    per_row = slot_width // tile
    slots = blocks * per_row
    chunk = blocks // nr
    rows = chunk * tile
    n_out = nc // 2
    own_blocks = feat_hbm.shape[0]
    col_blocks = nc * own_blocks
    feat = weight_ref.shape[0]
    groups = runs.shape[0] - 1
    cuts = 2
    step = rows // cuts
    c, partner, ahead, behind = col_peers(nc)
    r = lax.axis_index("row")

    barrier = pltpu.get_barrier_semaphore()
    for d in range(1, nc):
        pl.semaphore_signal(barrier, inc=1, device_id={"col": lax.rem(c + d, nc)}, device_id_type=MESH)
    for e in range(1, nr):
        pl.semaphore_signal(barrier, inc=1, device_id={"row": lax.rem(r + e, nr)}, device_id_type=MESH)

    def blocks_of(col):
        return xg.at[pl.ds(col * own_blocks, own_blocks)]

    loads = {}
    for n, (name, src, dst) in enumerate((
        ("feat", feat_hbm, blocks_of(c)), ("cols_s", cols_hbm, cols_s), ("counts_s", counts_hbm, counts_s),
        ("cols_v", cols_hbm, cols_v), ("counts_v", counts_hbm, counts_v),
        ("weight", weight_hbm, weight_ref), ("bias", bias_hbm, bias_ref), ("og", og_hbm, og_ref),
    )):
        loads[name] = pltpu.make_async_copy(src, dst, in_sem.at[n])
        loads[name].start()

    mirrored = r >= 2
    inner = (r == 1) | (r == 2)
    outer = (r == 0) | (r == 3)

    def place(d):
        return jnp.where(mirrored, 3 - d, d)

    mate = jnp.where(r % 2 == 0, r + 1, r - 1)
    targets = [place(3), place(2), mate, r]
    for e in range(nr):
        cut = pl.ds(targets[e] * chunk, chunk)
        load = pltpu.make_async_copy(adj_hbm.at[cut], adj.at[cut], a_sem.at[e])
        load.start()
        loads[e] = load

    xg[col_blocks] = jnp.zeros(xg.shape[1:], xg.dtype)
    contrib[slots] = jnp.zeros(contrib.shape[1:], F32)
    runs[groups] = jnp.zeros(runs.shape[1:], F32)
    loads["feat"].wait()
    pl.semaphore_wait(barrier, nc - 1 + nr - 1)

    done = []
    copies = []
    for d in range(1, n_out):
        copy = send(blocks_of(c), blocks_of(c), f_send.at[d], f_recv.at[d], {"col": ahead[d]})
        copy.start()
        copies.append(copy)
    pair = []
    copy = send(blocks_of(c), blocks_of(c), p_send.at[0], p_recv.at[0], {"col": partner})
    copy.start()
    pair.append(copy)
    loads["cols_v"].wait()
    loads["counts_v"].wait()
    slot_tables(cols_v, counts_v, col_blocks, tab_v)
    table = pltpu.make_async_copy(tab_v, tab_s, in_sem.at[8])
    table.start()
    for d in range(1, n_out):
        copies[d - 1].wait_recv()
        came = blocks_of(behind[d])
        copy = send(came, came, p_send.at[d], p_recv.at[d], {"col": partner})
        copy.start()
        pair.append(copy)
    loads["cols_s"].wait()
    loads["counts_s"].wait()
    table.wait()
    for copy in pair:
        copy.wait_recv()
    done += copies + pair

    def piece(q):
        return pl.ds(q * step, step)

    def to_near(e, q):
        return send(part.at[e, piece(q)], near.at[e, piece(q)], n_send.at[e, q], n_recv.at[e, q], {"row": mate})

    def to_far(e, q):
        return send(part.at[e, piece(q)], far.at[piece(q)], r_send.at[e, q], r_recv.at[q], {"row": targets[e]})

    for e in range(nr):
        t = targets[e]
        loads[e].wait()
        for q in range(cuts):
            def block_rows(n, carry, t=t, e=e, q=q):
                for i in range(2):
                    i = q * (chunk // cuts) + n * 2 + i
                    b = t * chunk + i
                    count = counts_s[0, b]
                    picked = [xg[jnp.where(s < count, cols_s[s, b], col_blocks)] for s in range(per_row)]
                    got = jnp.dot(adj[b], jnp.concatenate(picked, axis=0), preferred_element_type=F32)
                    cut = pl.ds(pl.multiple_of(i * tile, tile), tile)
                    pf[e, cut, :] = got
                    if e < 3:
                        part[e, cut, :] = got.astype(BF16)
                return carry

            lax.fori_loop(0, chunk // cuts // 2, block_rows, 0)
            if e < 2:
                @pl.when(outer)
                def hand_in(e=e, q=q):
                    to_near(e, q).start()
            elif e == 2:
                to_near(e, q).start()
    for e in range(2):
        for q in range(cuts):
            @pl.when(inner)
            def join(e=e, q=q):
                to_near(e, q).wait_recv()
                part[e, piece(q), :] = (pf[e, piece(q), :] + near[e, piece(q), :].astype(F32)).astype(BF16)
                to_far(e, q).start()

    def to_mate(t, q):
        return send(gg.at[t, piece(q)], gg.at[t, piece(q)], g_send.at[0, t, q], g_recv.at[t, q], {"row": mate})

    def to_other(q):
        return send(gg.at[r, piece(q)], gg.at[r, piece(q)], g_send.at[1, r, q], g_recv.at[r, q], {"row": place(2)})

    for name in ("weight", "bias", "og"):
        loads[name].wait()
    bias_part = jnp.zeros((1, feat), F32)
    for q in range(cuts):
        cut = piece(q)
        to_near(2, q).wait_recv()
        to_far(0, q).wait_recv()
        hidden = (pf[3, cut, :] + near[2, cut, :].astype(F32) + far[cut, :].astype(F32)).astype(BF16)
        preact = jnp.dot(hidden, weight_ref[...], preferred_element_type=F32) + bias_ref[...]
        sig = jax.nn.sigmoid(preact)
        pre_grad = og_ref[cut, :].astype(F32) * (sig * (1.0 + preact * (1.0 - sig)))
        small = pre_grad.astype(BF16)
        dest = lax.dot_general(small, weight_ref[...], (((1,), (1,)), ((), ())), preferred_element_type=F32)
        gg[r, cut, :] = dest.astype(BF16)
        to_other(q).start()
        to_mate(r, q).start()
        act_ref[cut, :] = (preact * sig).astype(BF16)
        hid[cut, :] = hidden
        half[cut, :] = small
        bias_part = bias_part + jnp.sum(pre_grad, axis=0, keepdims=True)

    wcut = feat // nc
    w_out[:, pl.ds(0, wcut), :] = scale * lax.dot_general(
        hid[...], half[...], (((0,), (0,)), ((), ())), preferred_element_type=F32
    ).reshape(nc, wcut, feat)
    w_out[:, pl.ds(wcut, 8), :] = jnp.broadcast_to(scale * bias_part, (nc, 8, feat))
    w_copies = []
    for d in range(1, nc):
        there = lax.rem(c + d, nc)
        copy = send(w_out.at[there], w_in.at[d - 1], w_send.at[d - 1], w_recv.at[d - 1], {"col": there})
        copy.start()
        w_copies.append(copy)
    done += w_copies

    def contribute(t, q):
        def pairs(n, carry):
            b = t * chunk + q * (chunk // cuts) + n * 2
            lhs = adj[pl.ds(b, 2)].reshape(2 * tile, slot_width)
            g = gg[t, pl.ds(pl.multiple_of(q * step + n * 2 * tile, 2 * tile), 2 * tile), :]
            upper = lax.broadcasted_iota(jnp.int32, g.shape, 0) < tile
            zero = jnp.zeros_like(g)
            rhs = jnp.concatenate([jnp.where(upper, g, zero), jnp.where(upper, zero, g)], axis=1)
            got = lax.dot_general(lhs, rhs, (((0,), (0,)), ((), ())), preferred_element_type=F32)
            contrib[pl.ds(b * per_row, per_row)] = got[:, :feat].reshape(per_row, tile, feat)
            contrib[pl.ds(b * per_row + per_row, per_row)] = got[:, feat:].reshape(per_row, tile, feat)
            return carry

        lax.fori_loop(0, chunk // cuts // 2, pairs, 0)

    for q in range(cuts):
        contribute(r, q)
    from_in = [(place(2), 0), (mate, 0), (place(3), 0), (place(2), 1), (mate, 1), (place(3), 1)]
    from_out = [(mate, 0), (mate, 1), (place(2), 0), (place(3), 0), (place(2), 1), (place(3), 1)]
    row_copies, all_copies = [], []
    for k in range(6):
        t = jnp.where(inner, from_in[k][0], from_out[k][0])
        q = jnp.where(inner, from_in[k][1], from_out[k][1])
        to_mate(t, q).wait_recv()
        if k % 3 != 1:
            @pl.when(inner)
            def pass_on(t=t, q=q):
                to_mate(t, q).start()
        contribute(t, q)
        if k == 1:
            total = w_out[c]
            for copy in w_copies:
                copy.wait_recv()
            for d in range(1, nc):
                total = total + w_in[d - 1]
            w_row[r] = total
            for e in range(1, nr):
                copy = send(
                    w_row.at[r], w_row.at[r], wr_send.at[e - 1], wr_recv.at[e - 1], {"row": lax.rem(r + e, nr)}
                )
                copy.start()
                row_copies.append(copy)
        if k == 4:
            for copy in row_copies:
                copy.wait_recv()
            total = w_row[0]
            for n in range(1, nr):
                total = total + w_row[n]
            w_all[c] = total
            for d in range(1, nc):
                there = lax.rem(c + d, nc)
                copy = send(w_all.at[c], w_all.at[c], wa_send.at[d - 1], wa_recv.at[d - 1], {"col": there})
                copy.start()
                all_copies.append(copy)
    done += row_copies + all_copies

    hrows = tile // 2
    order = list(range(1, n_out)) + [0]

    def gather(h):
        def add_up(n, acc):
            for u in range(8):
                first = n * 32 + u * GROUP
                line, spot = first // 128, first % 128
                terms = [contrib[tab_s[line, spot + k], pl.ds(h * hrows, hrows), :] for k in range(GROUP)]
                new = tab_s[GROUP * groups // 128 + n // 16, (n % 16) * 8 + u]
                acc = jnp.where(new > 0, 0.0, acc) + ((terms[0] + terms[1]) + (terms[2] + terms[3]))
                runs[n * 8 + u, pl.ds(h * hrows, hrows), :] = acc
            return acc

        used = -(-(slots + (GROUP - 1) * min(col_blocks, slots)) // GROUP)
        lax.fori_loop(0, -(-used // 8), add_up, jnp.zeros((hrows, feat), F32))

    def total_of(j, h):
        return runs[tab_s[GROUP * groups // 128 + groups // 128, j], pl.ds(h * hrows, hrows), :]

    def to_pair(h, d):
        return send(pair_out.at[h, d], pair_in.at[h, d], gp_send.at[h, d], gp_recv.at[h, d], {"col": partner})

    def to_chip(h, d):
        return send(
            chip_out.at[h, d - 1], chip_in.at[h, d - 1], gc_send.at[h, d - 1], gc_recv.at[h, d - 1], {"col": ahead[d]}
        )

    def hand_over(h):
        for d in order:
            def fill(n, carry, d=d):
                there = (ahead[d] + partner - c) * own_blocks + n
                pair_out[h, d, pl.ds(pl.multiple_of(n * hrows, hrows), hrows), :] = total_of(there, h).astype(BF16)
                return carry

            for n in range(own_blocks):
                fill(n, 0)
            to_pair(h, d).start()

    def combine(h):
        for d in order:
            to_pair(h, d).wait_recv()
            for n in range(own_blocks):
                cut = pl.ds(n * hrows, hrows)
                both = total_of(ahead[d] * own_blocks + n, h) + pair_in[h, d, cut, :].astype(F32)
                if d:
                    chip_out[h, d - 1, cut, :] = both.astype(BF16)
                else:
                    kept[h, cut, :] = both
            if d:
                to_chip(h, d).start()

    gather(0)
    hand_over(0)
    gather(1)
    hand_over(1)
    combine(0)
    combine(1)
    for copy in all_copies:
        copy.wait_recv()
    for n in range(nc):
        wb_ref[pl.ds(n * wcut, wcut), :] = w_all[n, pl.ds(0, wcut), :]
    wb_ref[pl.ds(feat, 8), :] = w_all[0, pl.ds(wcut, 8), :]
    for h in range(2):
        for d in range(1, n_out):
            to_chip(h, d).wait_recv()
        for n in range(own_blocks):
            cut = pl.ds(n * hrows, hrows)
            both = kept[h, cut, :]
            for d in range(1, n_out):
                both = both + chip_in[h, d - 1, cut, :].astype(F32)
            fg_ref[pl.ds(n * tile + h * hrows, hrows), :] = both.astype(BF16)
    for copy in done:
        copy.wait_send()
    for q in range(cuts):
        to_near(2, q).wait_send()
        to_other(q).wait_send()
        to_mate(r, q).wait_send()

    @pl.when(outer)
    def outer_sent():
        for e in range(2):
            for q in range(cuts):
                to_near(e, q).wait_send()

    @pl.when(inner)
    def inner_sent():
        for e in range(2):
            for q in range(cuts):
                to_far(e, q).wait_send()
                to_mate(targets[e], q).wait_send()

    for h in range(2):
        for d in range(n_out):
            to_pair(h, d).wait_send()
            if d:
                to_chip(h, d).wait_send()


def finish_kernel(fg_in, act_in, wb_in, act_out, fg_out, wg_out, bg_out, sem):
    feat = wg_out.shape[0]
    copies = []
    for n, (src, dst) in enumerate((
        (fg_in, fg_out), (act_in, act_out), (wb_in.at[pl.ds(0, feat)], wg_out), (wb_in.at[pl.ds(feat, 1)], bg_out),
    )):
        copy = pltpu.make_async_copy(src, dst, sem.at[n])
        copy.start()
        copies.append(copy)
    for copy in copies:
        copy.wait()


def whole_layer(mesh, features, adjacency, tile_cols, row_counts, weight, bias, out_grad):
    blocks, tile, slot_width = adjacency.shape
    own_rows, feat = features.shape
    nc, nr = mesh.shape["col"], mesh.shape["row"]
    n_out = nc // 2
    own_blocks = own_rows // tile
    col_blocks = nc * own_blocks
    per_row = slot_width // tile
    slots = blocks * per_row
    scale = 1.0 / math.sqrt(own_rows * nc * nr)
    cut = feat // nc
    rows = blocks * tile // nr
    groups = pad_groups(slots, col_blocks)
    table_rows = GROUP * groups // 128 + groups // 128 + 1
    table_rows = -(-table_rows // 8) * 8

    vmem = pl.BlockSpec(memory_space=pltpu.VMEM)
    hbm = pl.BlockSpec(memory_space=pltpu.HBM)
    dma = pltpu.SemaphoreType.DMA
    tile_flops = 2 * blocks * tile * slot_width * feat
    fg, act, wb = pl.pallas_call(
        functools.partial(layer_kernel, nc, nr, scale),
        out_shape=(
            jax.ShapeDtypeStruct((own_rows, feat), BF16),
            jax.ShapeDtypeStruct((rows, feat), BF16),
            jax.ShapeDtypeStruct((feat + 8, feat), F32),
        ),
        in_specs=[hbm] * 7,
        out_specs=(vmem, vmem, vmem),
        scratch_shapes=[
            pltpu.SMEM((per_row, blocks), jnp.int32),
            pltpu.SMEM((1, blocks), jnp.int32),
            pltpu.SMEM((table_rows, 128), jnp.int32),
            pltpu.VMEM((per_row, blocks), jnp.int32),
            pltpu.VMEM((1, blocks), jnp.int32),
            pltpu.VMEM((table_rows, 128), jnp.int32),
            pltpu.VMEM((col_blocks + 1, tile, feat), BF16),
            pltpu.VMEM(adjacency.shape, BF16),
            pltpu.VMEM((feat, feat), BF16),
            pltpu.VMEM((1, feat), F32),
            pltpu.VMEM((rows, feat), BF16),
            pltpu.VMEM((nr, rows, feat), F32),
            pltpu.VMEM((3, rows, feat), BF16),
            pltpu.VMEM((3, rows, feat), BF16),
            pltpu.VMEM((rows, feat), BF16),
            pltpu.VMEM((rows, feat), BF16),
            pltpu.VMEM((rows, feat), BF16),
            pltpu.VMEM((nr, rows, feat), BF16),
            pltpu.VMEM((slots + 1, tile, feat), F32),
            pltpu.VMEM((groups + 1, tile, feat), F32),
            pltpu.VMEM((2, n_out, own_rows // 2, feat), BF16),
            pltpu.VMEM((2, n_out, own_rows // 2, feat), BF16),
            pltpu.VMEM((2, n_out - 1, own_rows // 2, feat), BF16),
            pltpu.VMEM((2, n_out - 1, own_rows // 2, feat), BF16),
            pltpu.VMEM((2, own_rows // 2, feat), F32),
            pltpu.VMEM((nc, cut + 8, feat), F32),
            pltpu.VMEM((nc - 1, cut + 8, feat), F32),
            pltpu.VMEM((nr, cut + 8, feat), F32),
            pltpu.VMEM((nc, cut + 8, feat), F32),
            dma((9,)), dma((nr,)), dma((n_out,)), dma((n_out,)), dma((n_out,)), dma((n_out,)),
            dma((3, 2)), dma((3, 2)), dma((2, 2)), dma((2,)),
            dma((2, nr, 2)), dma((nr, 2)),
            dma((2, n_out)), dma((2, n_out)), dma((2, n_out - 1)), dma((2, n_out - 1)),
            dma((nc - 1,)), dma((nc - 1,)), dma((nr - 1,)), dma((nr - 1,)), dma((nc - 1,)), dma((nc - 1,)),
        ],
        compiler_params=pltpu.CompilerParams(
            collective_id=0, has_side_effects=True, vmem_limit_bytes=56 * MIB
        ),
        cost_estimate=pl.CostEstimate(
            flops=2 * tile_flops, bytes_accessed=adjacency.size * 2, transcendentals=rows * feat
        ),
    )(
        tile_cols.T, row_counts.T, features.reshape(own_blocks, tile, feat), adjacency, weight,
        bias.reshape(1, -1), out_grad,
    )
    activations, feature_grad, weight_grad, bias_grad = pl.pallas_call(
        finish_kernel,
        out_shape=(
            jax.ShapeDtypeStruct((rows, feat), BF16),
            jax.ShapeDtypeStruct((own_rows, feat), BF16),
            jax.ShapeDtypeStruct((feat, feat), F32),
            jax.ShapeDtypeStruct((1, feat), F32),
        ),
        in_specs=[vmem] * 3,
        out_specs=(hbm,) * 4,
        scratch_shapes=[dma((4,))],
    )(fg, act, wb)
    return (activations, feature_grad, weight_grad, bias_grad.reshape(-1))


def solution(mesh):
    small = mesh.shape["row"] == 4 and mesh.shape["col"] == 8
    placed = (
        P(("groups", "row", "col"), None),
        P(("groups", "col"), None, "row"),
        P(("groups", "col"), "row"),
        P(("groups", "col"), "row"),
        P(),
        P(),
        P(("groups", "col", "row"), None),
    )
    return jax.shard_map(
        functools.partial(whole_layer if small else on_device, mesh),
        mesh=mesh,
        in_specs=placed,
        out_specs=(
            P(("groups", "col", "row"), None),
            P(("groups", "row", "col"), None),
            P("groups", None),
            P("groups"),
        ),
        check_vma=False,
    )
```

```python
import functools
import math

import jax
import jax.numpy as jnp
from jax import lax
from jax.experimental import pallas as pl
from jax.experimental.pallas import tpu as pltpu
from jax.sharding import PartitionSpec as P

MESH = pl.DeviceIdType.MESH
F32, BF16 = jnp.float32, jnp.bfloat16
MIB = 1024 * 1024


def col_peers(nc):
    c = lax.axis_index("col")
    outer, core, n_out = c // 2, c % 2, nc // 2
    partner = outer * 2 + (1 - core)
    ahead = [lax.rem(outer + d, n_out) * 2 + core for d in range(n_out)]
    behind = [lax.rem(outer - d + n_out, n_out) * 2 + core for d in range(n_out)]
    return c, partner, ahead, behind


def send(src, dst, send_sem, recv_sem, where):
    return pltpu.make_async_remote_copy(
        src_ref=src, dst_ref=dst, send_sem=send_sem, recv_sem=recv_sem,
        device_id=where, device_id_type=MESH,
    )


def enter(nc, nr):
    c, r = lax.axis_index("col"), lax.axis_index("row")
    barrier = pltpu.get_barrier_semaphore()
    for d in range(1, nc):
        pl.semaphore_signal(barrier, inc=1, device_id={"col": lax.rem(c + d, nc)}, device_id_type=MESH)
    for e in range(1, nr):
        pl.semaphore_signal(barrier, inc=1, device_id={"row": lax.rem(r + e, nr)}, device_id_type=MESH)
    pl.semaphore_wait(barrier, nc - 1 + nr - 1)


def forward_kernel(
    nc, nr, scale, cols_ref, counts_ref, feat_hbm, adj_hbm, weight_hbm, bias_hbm, og_hbm,
    grads_ref, wb_ref,
    xg, adj, weight_ref, bias_ref, og_ref, own, part, rbuf, gg, w_out, w_in, w_all,
    in_sem, a_sem, f_send, f_recv, p_send, p_recv, r_send, r_recv, g_send, g_recv, w_send, w_recv, wa_send, wa_recv,
):
    blocks, tile, slot_width = adj.shape
    per_row = slot_width // tile
    chunk = blocks // nr
    rows = chunk * tile
    n_out = nc // 2
    own_blocks = feat_hbm.shape[0]
    c, partner, ahead, behind = col_peers(nc)
    r = lax.axis_index("row")
    row_at = [lax.rem(r + e, nr) for e in range(nr)]

    mine = xg.at[pl.ds(c * own_blocks, own_blocks)]
    first = pltpu.make_async_copy(feat_hbm, mine, in_sem.at[0])
    first.start()
    loads = []
    for e in range(nr):
        t = row_at[(e + 1) % nr]
        cut = pl.ds(t * chunk, chunk)
        load = pltpu.make_async_copy(adj_hbm.at[cut], adj.at[cut], a_sem.at[e])
        load.start()
        loads.append(load)
    small = []
    for n, (src, dst) in enumerate(((weight_hbm, weight_ref), (bias_hbm, bias_ref), (og_hbm, og_ref))):
        load = pltpu.make_async_copy(src, dst, in_sem.at[n + 1])
        load.start()
        small.append(load)

    def blocks_of(col):
        return xg.at[pl.ds(col * own_blocks, own_blocks)]

    xg[nc * own_blocks] = jnp.zeros(xg.shape[1:], xg.dtype)
    first.wait()
    enter(nc, nr)

    copies = []
    for d in range(1, n_out):
        copy = send(blocks_of(c), blocks_of(c), f_send.at[d], f_recv.at[d], {"col": ahead[d]})
        copy.start()
        copies.append(copy)
    pair = []
    copy = send(blocks_of(c), blocks_of(c), p_send.at[0], p_recv.at[0], {"col": partner})
    copy.start()
    pair.append(copy)
    for d in range(1, n_out):
        copies[d - 1].wait_recv()
        came = blocks_of(behind[d])
        copy = send(came, came, p_send.at[d], p_recv.at[d], {"col": partner})
        copy.start()
        pair.append(copy)
    for copy in pair:
        copy.wait_recv()
    for copy in copies + pair:
        copy.wait_send()

    pace = math.gcd(chunk, 4)
    row_copies = []
    for e in range(nr):
        far = (e + 1) % nr
        t = row_at[far]
        loads[e].wait()

        def block_rows(n, carry, t=t, far=far):
            for i in range(pace):
                i = n * pace + i
                b = t * chunk + i
                count = counts_ref[0, b]
                picked = [
                    xg[jnp.where(s < count, cols_ref[s, b], nc * own_blocks)] for s in range(per_row)
                ]
                got = jnp.dot(adj[b], jnp.concatenate(picked, axis=0), preferred_element_type=F32)
                cut = pl.ds(pl.multiple_of(i * tile, tile), tile)
                if far:
                    part[far - 1, cut, :] = got.astype(BF16)
                else:
                    own[cut, :] = got
            return carry

        lax.fori_loop(0, chunk // pace, block_rows, 0)
        if far:
            copy = send(
                part.at[far - 1], rbuf.at[far - 1], r_send.at[far - 1], r_recv.at[far - 1], {"row": t}
            )
            copy.start()
            row_copies.append(copy)
    summed = own[...]
    for copy in row_copies:
        copy.wait_recv()
    for e in range(nr - 1):
        summed = summed + rbuf[e].astype(F32)
    hidden = summed.astype(BF16)
    for load in small:
        load.wait()
    preact = jnp.dot(hidden, weight_ref[...], preferred_element_type=F32) + bias_ref[...]
    sig = jax.nn.sigmoid(preact)
    pre_grad = og_ref[...].astype(F32) * (sig * (1.0 + preact * (1.0 - sig)))
    half = pre_grad.astype(BF16)
    dest = lax.dot_general(
        half, weight_ref[...], (((1,), (1,)), ((), ())), preferred_element_type=F32
    )
    gg[r] = dest.astype(BF16)

    def hop(t, step):
        way = 0 if step > 0 else 1
        return send(gg.at[t], gg.at[t], g_send.at[way, t], g_recv.at[t], {"row": r + step})

    for step in (1, -1):
        @pl.when((r + step >= 0) & (r + step < nr))
        def start_chain(step=step):
            hop(r, step).start()
    grads_ref[pl.ds(nr * rows, rows), :] = (preact * sig).astype(BF16)
    feat = hidden.shape[1]
    cut = feat // nc
    w_out[:, pl.ds(0, cut), :] = scale * lax.dot_general(
        hidden, half, (((0,), (0,)), ((), ())), preferred_element_type=F32
    ).reshape(nc, cut, feat)
    w_out[:, pl.ds(cut, 8), :] = jnp.broadcast_to(
        scale * jnp.sum(pre_grad, axis=0, keepdims=True), (nc, 8, feat)
    )
    w_copies = []
    for d in range(1, nc):
        there = lax.rem(c + d, nc)
        copy = send(w_out.at[there], w_in.at[d - 1], w_send.at[d - 1], w_recv.at[d - 1], {"col": there})
        copy.start()
        w_copies.append(copy)
    for k in range(1, nr):
        if k == min(2, nr - 1):
            total = w_out[c]
            for d in range(1, nc):
                w_copies[d - 1].wait_recv()
                total = total + w_in[d - 1]
            w_all[c] = total
            for d in range(1, nc):
                there = lax.rem(c + d, nc)
                copy = send(w_all.at[c], w_all.at[c], wa_send.at[d - 1], wa_recv.at[d - 1], {"col": there})
                copy.start()
                w_copies.append(copy)
        for step in (1, -1):
            t = r - k * step
            came = (t >= 0) & (t < nr)

            @pl.when(came)
            def arrive(t=t, step=step):
                hop(t, step).wait_recv()

            @pl.when(came & (r + step >= 0) & (r + step < nr))
            def pass_on(t=t, step=step):
                hop(t, step).start()
    for k in range(nr):
        for step in (1, -1):
            t = r - k * step

            @pl.when((t >= 0) & (t < nr) & (r + step >= 0) & (r + step < nr))
            def sent(t=t, step=step):
                hop(t, step).wait_send()
    for copy in w_copies[nc - 1 :]:
        copy.wait_recv()
    for n in range(nc):
        wb_ref[pl.ds(n * cut, cut), :] = w_all[n, pl.ds(0, cut), :]
    wb_ref[pl.ds(feat, 8), :] = w_all[0, pl.ds(cut, 8), :]
    grads_ref[pl.ds(0, nr * rows), :] = gg[...].reshape(nr * rows, feat)
    for copy in row_copies + w_copies:
        copy.wait_send()


def backward_kernel(cols_ref, counts_ref, adj_ref, grad_ref, out_ref, act_out, sem, *accs):
    blocks, tile, slot_width = adj_ref.shape
    per_row = slot_width // tile
    dead = out_ref.shape[0]
    hand_out = pltpu.make_async_copy(grad_ref.at[pl.ds(blocks * tile, act_out.shape[0])], act_out, sem)
    hand_out.start()
    for acc in accs:
        acc[...] = jnp.zeros_like(acc)

    pace = math.gcd(blocks, 4)

    def block_rows(n, carry):
        contribs = []
        for i in range(pace):
            b = n * pace + i
            contribs.append(lax.dot_general(
                adj_ref[b], grad_ref[pl.ds(pl.multiple_of(b * tile, tile), tile), :],
                (((0,), (0,)), ((), ())), preferred_element_type=F32,
            ))
        for s in range(per_row):
            for i in range(pace):
                b = n * pace + i
                acc = accs[i]
                j = jnp.where(s < counts_ref[0, b], cols_ref[s, b], dead)
                acc[j] = acc[j] + contribs[i][s * tile : (s + 1) * tile]
        return carry

    lax.fori_loop(0, blocks // pace, block_rows, 0)
    total = accs[0][pl.ds(0, dead)]
    for acc in accs[1:]:
        total = total + acc[pl.ds(0, dead)]
    out_ref[...] = total.astype(BF16)
    hand_out.wait()


def scatter_kernel(
    nc, nr, part_ref, wb_ref, out_ref, wg_ref, bg_ref,
    from_pair, send_buf, from_chip, w_row,
    p_send, p_recv, s_send, s_recv, wr_send, wr_recv,
):
    n_out = nc // 2
    c, partner, ahead, behind = col_peers(nc)
    r = lax.axis_index("row")
    row_at = [lax.rem(r + e, nr) for e in range(nr)]
    partner_ahead = [x + partner - c for x in ahead]
    enter(nc, nr)

    started = []

    def go(*args):
        copy = send(*args)
        copy.start()
        started.append(copy)
        return copy

    order = list(range(1, n_out)) + [0]
    pair = {}
    for d in order:
        pair[d] = go(part_ref.at[partner_ahead[d]], from_pair.at[d], p_send.at[d], p_recv.at[d], {"col": partner})
    w_row[r] = wb_ref[...]
    w_copies = [
        go(w_row.at[r], w_row.at[r], wr_send.at[e - 1], wr_recv.at[e - 1], {"row": row_at[e]})
        for e in range(1, nr)
    ]
    copies = []
    for d in order:
        pair[d].wait_recv()
        both = part_ref[ahead[d]].astype(F32) + from_pair[d].astype(F32)
        if d:
            send_buf[d - 1] = both.astype(BF16)
            copies.append(go(
                send_buf.at[d - 1], from_chip.at[d - 1], s_send.at[d - 1], s_recv.at[d - 1], {"col": ahead[d]}
            ))
    for copy in copies:
        copy.wait_recv()
    for d in range(1, n_out):
        both = both + from_chip[d - 1].astype(F32)
    out_ref[...] = both.astype(BF16)
    for copy in w_copies:
        copy.wait_recv()
    total = w_row[0]
    for n in range(1, nr):
        total = total + w_row[n]
    feat = wg_ref.shape[0]
    wg_ref[...] = total[:feat]
    bg_ref[...] = total[feat : feat + 1]
    for copy in started:
        copy.wait_send()


def on_device(mesh, features, adjacency, tile_cols, row_counts, weight, bias, out_grad):
    blocks, tile, slot_width = adjacency.shape
    own_rows, feat = features.shape
    nc, nr = mesh.shape["col"], mesh.shape["row"]
    n_out = nc // 2
    col_blocks = nc * own_rows // tile
    scale = 1.0 / math.sqrt(own_rows * nc * nr)
    cut = feat // nc

    vmem = pl.BlockSpec(memory_space=pltpu.VMEM)
    smem = pl.BlockSpec(memory_space=pltpu.SMEM)
    hbm = pl.BlockSpec(memory_space=pltpu.HBM)
    dma = pltpu.SemaphoreType.DMA
    rows = blocks * tile // nr
    tile_flops = 2 * blocks * tile * slot_width * feat
    grads, wb = pl.pallas_call(
        functools.partial(forward_kernel, nc, nr, scale),
        out_shape=(
            jax.ShapeDtypeStruct((blocks * tile + rows, feat), BF16),
            jax.ShapeDtypeStruct((feat + 8, feat), F32),
        ),
        in_specs=[smem, smem, hbm, hbm, hbm, hbm, hbm],
        out_specs=(vmem, vmem),
        scratch_shapes=[
            pltpu.VMEM((col_blocks + 1, tile, feat), BF16),
            pltpu.VMEM(adjacency.shape, BF16),
            pltpu.VMEM((feat, feat), BF16),
            pltpu.VMEM((1, feat), F32),
            pltpu.VMEM((rows, feat), BF16),
            pltpu.VMEM((rows, feat), F32),
            pltpu.VMEM((nr - 1, rows, feat), BF16),
            pltpu.VMEM((nr - 1, rows, feat), BF16),
            pltpu.VMEM((nr, rows, feat), BF16),
            pltpu.VMEM((nc, cut + 8, feat), F32),
            pltpu.VMEM((nc - 1, cut + 8, feat), F32),
            pltpu.VMEM((nc, cut + 8, feat), F32),
            dma((4,)), dma((nr,)), dma((n_out,)), dma((n_out,)), dma((n_out,)), dma((n_out,)),
            dma((nr - 1,)), dma((nr - 1,)), dma((2, nr)), dma((nr,)),
            dma((nc - 1,)), dma((nc - 1,)), dma((nc - 1,)), dma((nc - 1,)),
        ],
        compiler_params=pltpu.CompilerParams(
            collective_id=0, has_side_effects=True, vmem_limit_bytes=56 * MIB
        ),
        cost_estimate=pl.CostEstimate(
            flops=tile_flops, bytes_accessed=adjacency.size * 2, transcendentals=rows * feat
        ),
    )(
        tile_cols.T, row_counts.T, features.reshape(own_rows // tile, tile, feat), adjacency, weight,
        bias.reshape(1, -1), out_grad,
    )

    partial, activations = pl.pallas_call(
        backward_kernel,
        out_shape=(
            jax.ShapeDtypeStruct((col_blocks, tile, feat), BF16),
            jax.ShapeDtypeStruct((rows, feat), BF16),
        ),
        in_specs=[smem, smem, vmem, vmem],
        out_specs=(vmem, hbm),
        scratch_shapes=[dma] + [pltpu.VMEM((col_blocks + 1, tile, feat), F32) for unused in range(4)],
        compiler_params=pltpu.CompilerParams(vmem_limit_bytes=32 * MIB),
        cost_estimate=pl.CostEstimate(
            flops=tile_flops * 8, bytes_accessed=adjacency.size * 2, transcendentals=0
        ),
    )(tile_cols.T, row_counts.T, adjacency, grads)

    feature_grad, weight_grad, bias_grad = pl.pallas_call(
        functools.partial(scatter_kernel, nc, nr),
        out_shape=(
            jax.ShapeDtypeStruct((own_rows, feat), BF16),
            jax.ShapeDtypeStruct((feat, feat), F32),
            jax.ShapeDtypeStruct((1, feat), F32),
        ),
        in_specs=[vmem, vmem],
        out_specs=(vmem, vmem, vmem),
        scratch_shapes=[
            pltpu.VMEM((n_out, own_rows, feat), BF16),
            pltpu.VMEM((n_out - 1, own_rows, feat), BF16),
            pltpu.VMEM((n_out - 1, own_rows, feat), BF16),
            pltpu.VMEM((nr, feat + 8, feat), F32),
            dma((n_out,)), dma((n_out,)), dma((n_out - 1,)), dma((n_out - 1,)),
            dma((nr - 1,)), dma((nr - 1,)),
        ],
        compiler_params=pltpu.CompilerParams(
            collective_id=1, has_side_effects=True, vmem_limit_bytes=20 * MIB
        ),
        cost_estimate=pl.CostEstimate(
            flops=own_rows * nc * feat, bytes_accessed=8 * own_rows * nc * feat, transcendentals=0
        ),
    )(partial.reshape(nc, own_rows, feat), wb)
    return (activations, feature_grad, weight_grad, bias_grad.reshape(-1))


GROUP = 4


def slot_tables(cols_ref, counts_ref, col_blocks, mine, tab_ref):
    per_row, blocks = cols_ref.shape
    slots = per_row * blocks
    groups = half_groups(slots, col_blocks)
    keys = 2 * col_blocks

    def iota(shape, axis):
        return lax.broadcasted_iota(jnp.int32, shape, axis)

    def upright(row):
        n = row.shape[1]
        return jnp.sum(jnp.where(iota((n, n), 0) == iota((n, n), 1), row, 0), axis=1, keepdims=True)

    lane = iota((blocks, keys), 1)
    block = iota((blocks, 1), 0)
    late = jnp.where((block >= mine) & (block < mine + blocks // 2), 0, col_blocks)
    counts = upright(counts_ref[...])
    seen = jnp.zeros((blocks, keys), jnp.int32)
    hits, ranks = [], []
    for s in range(per_row):
        hit = jnp.where((upright(cols_ref[pl.ds(s, 1), :]) + late == lane) & (counts > s), 1, 0)
        hits.append(hit)
        ranks.append(seen)
        seen = seen + hit
    earlier = jnp.zeros((blocks, keys), jnp.int32)
    for b in range(blocks - 1):
        earlier = earlier + jnp.where(block > b, seen[b : b + 1, :], 0)
    sizes = lax.shift_right_logical(jnp.sum(seen, axis=0, keepdims=True) + (GROUP - 1), 2)
    square = (keys, keys)
    first, second = iota(square, 0), iota(square, 1)
    lower = (first < second) & ((first < col_blocks) == (second < col_blocks))
    starts = jnp.sum(jnp.where(lower, upright(sizes), 0), axis=0, keepdims=True)
    starts = starts + jnp.where(iota((1, keys), 1) < col_blocks, 0, groups)
    places = -(-2 * GROUP * groups // 128) * 128
    heads = -(-2 * groups // 128) * 128
    place = iota((blocks, places), 1)
    head = iota((blocks, heads), 1) * GROUP
    found = jnp.zeros((blocks, places), jnp.int32)
    fresh = jnp.zeros((blocks, heads), jnp.int32)
    for s in range(per_row):
        rank = jnp.sum(hits[s] * (ranks[s] + earlier), axis=1, keepdims=True)
        at = jnp.sum(hits[s] * (GROUP * starts), axis=1, keepdims=True) + rank
        at = jnp.where(counts > s, at, -1)
        found = found + jnp.where(at == place, slots - (block * per_row + s), 0)
        fresh = fresh + jnp.where((at == head) & (rank == 0), 1, 0)
    found = slots - jnp.sum(found, axis=0, keepdims=True)
    fresh = jnp.sum(fresh, axis=0, keepdims=True)
    last = jnp.where(sizes > 0, starts + sizes - 1, 2 * groups)
    n = 0
    for value in (found, fresh):
        for k in range(value.shape[1] // 128):
            tab_ref[pl.ds(n, 1), :] = value[:, k * 128 : (k + 1) * 128]
            n += 1
    tab_ref[pl.ds(n, 1), pl.ds(0, keys)] = last


def half_groups(slots, col_blocks):
    most = (slots // 2 + (GROUP - 1) * min(col_blocks, slots // 2)) // GROUP
    return -(-most // 8) * 8


def layer_kernel(
    nc, nr, scale, cols_hbm, counts_hbm, feat_hbm, adj_hbm, weight_hbm, bias_hbm, og_hbm,
    fg_ref, act_ref, wb_ref,
    cols_s, counts_s, tab_s, cols_v, counts_v, tab_v,
    xg, adj, weight_ref, bias_ref, og_ref, pf, part, near, far, hid, half, gg,
    contrib, runs, pair_out, pair_in, chip_out, chip_in, kept,
    w_out, w_in, w_row, w_all,
    in_sem, a_sem, f_send, f_recv, p_send, p_recv, n_send, n_recv, r_send, r_recv,
    g_send, g_recv, gp_send, gp_recv, gc_send, gc_recv,
    w_send, w_recv, wr_send, wr_recv, wa_send, wa_recv,
):
    blocks, tile, slot_width = adj.shape
    per_row = slot_width // tile
    slots = blocks * per_row
    chunk = blocks // nr
    rows = chunk * tile
    n_out = nc // 2
    own_blocks = feat_hbm.shape[0]
    col_blocks = nc * own_blocks
    feat = weight_ref.shape[0]
    groups = half_groups(slots, col_blocks)
    cuts = 4
    fresh_at = -(-2 * GROUP * groups // 128)
    last_at = fresh_at + -(-2 * groups // 128)
    step = rows // cuts
    c, partner, ahead, behind = col_peers(nc)
    r = lax.axis_index("row")

    barrier = pltpu.get_barrier_semaphore()
    for d in range(1, nc):
        pl.semaphore_signal(barrier, inc=1, device_id={"col": lax.rem(c + d, nc)}, device_id_type=MESH)
    for e in range(1, nr):
        pl.semaphore_signal(barrier, inc=1, device_id={"row": lax.rem(r + e, nr)}, device_id_type=MESH)

    def blocks_of(col):
        return xg.at[pl.ds(col * own_blocks, own_blocks)]

    loads = {}
    for n, (name, src, dst) in enumerate((
        ("feat", feat_hbm, blocks_of(c)), ("cols_s", cols_hbm, cols_s), ("counts_s", counts_hbm, counts_s),
        ("cols_v", cols_hbm, cols_v), ("counts_v", counts_hbm, counts_v),
        ("weight", weight_hbm, weight_ref), ("bias", bias_hbm, bias_ref), ("og", og_hbm, og_ref),
    )):
        loads[name] = pltpu.make_async_copy(src, dst, in_sem.at[n])
        loads[name].start()

    mirrored = r >= 2
    inner = (r == 1) | (r == 2)
    outer = (r == 0) | (r == 3)

    def place(d):
        return jnp.where(mirrored, 3 - d, d)

    mate = jnp.where(r % 2 == 0, r + 1, r - 1)
    targets = [place(3), place(2), mate, r]
    for e in range(nr):
        cut = pl.ds(targets[e] * chunk, chunk)
        load = pltpu.make_async_copy(adj_hbm.at[cut], adj.at[cut], a_sem.at[e])
        load.start()
        loads[e] = load

    xg[col_blocks] = jnp.zeros(xg.shape[1:], xg.dtype)
    contrib[slots] = jnp.zeros(contrib.shape[1:], F32)
    runs[2 * groups] = jnp.zeros(runs.shape[1:], F32)
    loads["feat"].wait()
    pl.semaphore_wait(barrier, nc - 1 + nr - 1)

    done = []
    copies = []
    for d in range(1, n_out):
        copy = send(blocks_of(c), blocks_of(c), f_send.at[d], f_recv.at[d], {"col": ahead[d]})
        copy.start()
        copies.append(copy)
    pair = []
    copy = send(blocks_of(c), blocks_of(c), p_send.at[0], p_recv.at[0], {"col": partner})
    copy.start()
    pair.append(copy)
    loads["cols_v"].wait()
    loads["counts_v"].wait()
    slot_tables(cols_v, counts_v, col_blocks, r // 2 * (blocks // 2), tab_v)
    table = pltpu.make_async_copy(tab_v, tab_s, in_sem.at[8])
    table.start()
    for d in range(1, n_out):
        copies[d - 1].wait_recv()
        came = blocks_of(behind[d])
        copy = send(came, came, p_send.at[d], p_recv.at[d], {"col": partner})
        copy.start()
        pair.append(copy)
    loads["cols_s"].wait()
    loads["counts_s"].wait()
    table.wait()
    for copy in pair:
        copy.wait_recv()
    done += copies + pair

    def piece(q):
        return pl.ds(q * step, step)

    def to_near(e, q):
        return send(part.at[e, piece(q)], near.at[e, piece(q)], n_send.at[e, q], n_recv.at[e, q], {"row": mate})

    def to_far(e, q):
        return send(part.at[e, piece(q)], far.at[piece(q)], r_send.at[e, q], r_recv.at[q], {"row": targets[e]})

    for e in range(nr):
        t = targets[e]
        loads[e].wait()
        for q in range(cuts):
            def block_rows(n, carry, t=t, e=e, q=q):
                for i in range(2):
                    i = q * (chunk // cuts) + n * 2 + i
                    b = t * chunk + i
                    count = counts_s[0, b]
                    picked = [xg[jnp.where(s < count, cols_s[s, b], col_blocks)] for s in range(per_row)]
                    got = jnp.dot(adj[b], jnp.concatenate(picked, axis=0), preferred_element_type=F32)
                    cut = pl.ds(pl.multiple_of(i * tile, tile), tile)
                    pf[e, cut, :] = got
                    if e < 3:
                        part[e, cut, :] = got.astype(BF16)
                return carry

            lax.fori_loop(0, chunk // cuts // 2, block_rows, 0)
            if e < 2:
                @pl.when(outer)
                def hand_in(e=e, q=q):
                    to_near(e, q).start()
            elif e == 2:
                to_near(e, q).start()
    for e in range(2):
        for q in range(cuts):
            @pl.when(inner)
            def join(e=e, q=q):
                to_near(e, q).wait_recv()
                part[e, piece(q), :] = (pf[e, piece(q), :] + near[e, piece(q), :].astype(F32)).astype(BF16)
                to_far(e, q).start()

    def to_mate(t, q):
        return send(gg.at[t, piece(q)], gg.at[t, piece(q)], g_send.at[0, t, q], g_recv.at[t, q], {"row": mate})

    def to_other(q):
        return send(gg.at[r, piece(q)], gg.at[r, piece(q)], g_send.at[1, r, q], g_recv.at[r, q], {"row": place(2)})

    for name in ("weight", "bias", "og"):
        loads[name].wait()
    bias_part = jnp.zeros((1, feat), F32)
    for q in range(cuts):
        cut = piece(q)
        to_near(2, q).wait_recv()
        to_far(0, q).wait_recv()
        hidden = (pf[3, cut, :] + near[2, cut, :].astype(F32) + far[cut, :].astype(F32)).astype(BF16)
        preact = jnp.dot(hidden, weight_ref[...], preferred_element_type=F32) + bias_ref[...]
        sig = jax.nn.sigmoid(preact)
        pre_grad = og_ref[cut, :].astype(F32) * (sig * (1.0 + preact * (1.0 - sig)))
        small = pre_grad.astype(BF16)
        dest = lax.dot_general(small, weight_ref[...], (((1,), (1,)), ((), ())), preferred_element_type=F32)
        gg[r, cut, :] = dest.astype(BF16)
        to_other(q).start()
        to_mate(r, q).start()
        act_ref[cut, :] = (preact * sig).astype(BF16)
        hid[cut, :] = hidden
        half[cut, :] = small
        bias_part = bias_part + jnp.sum(pre_grad, axis=0, keepdims=True)

    wcut = feat // nc
    w_out[:, pl.ds(0, wcut), :] = scale * lax.dot_general(
        hid[...], half[...], (((0,), (0,)), ((), ())), preferred_element_type=F32
    ).reshape(nc, wcut, feat)
    w_out[:, pl.ds(wcut, 8), :] = jnp.broadcast_to(scale * bias_part, (nc, 8, feat))
    w_copies = []
    for d in range(1, nc):
        there = lax.rem(c + d, nc)
        copy = send(w_out.at[there], w_in.at[d - 1], w_send.at[d - 1], w_recv.at[d - 1], {"col": there})
        copy.start()
        w_copies.append(copy)
    done += w_copies

    def contribute(t, q):
        def pairs(n, carry):
            b = t * chunk + q * (chunk // cuts) + n * 2
            lhs = adj[pl.ds(b, 2)].reshape(2 * tile, slot_width)
            g = gg[t, pl.ds(pl.multiple_of(q * step + n * 2 * tile, 2 * tile), 2 * tile), :]
            upper = lax.broadcasted_iota(jnp.int32, g.shape, 0) < tile
            zero = jnp.zeros_like(g)
            rhs = jnp.concatenate([jnp.where(upper, g, zero), jnp.where(upper, zero, g)], axis=1)
            got = lax.dot_general(lhs, rhs, (((0,), (0,)), ((), ())), preferred_element_type=F32)
            contrib[pl.ds(b * per_row, per_row)] = got[:, :feat].reshape(per_row, tile, feat)
            contrib[pl.ds(b * per_row + per_row, per_row)] = got[:, feat:].reshape(per_row, tile, feat)
            return carry

        lax.fori_loop(0, chunk // cuts // 2, pairs, 0)

    def gather(part_of):
        def add_up(n, acc):
            spot = part_of * GROUP * groups + n * 8 * GROUP
            head = part_of * groups + n * 8
            for u in range(8):
                terms = [contrib[tab_s[spot // 128, spot % 128 + u * GROUP + k]] for k in range(GROUP)]
                new = tab_s[fresh_at + head // 128, head % 128 + u]
                acc = jnp.where(new > 0, 0.0, acc) + ((terms[0] + terms[1]) + (terms[2] + terms[3]))
                runs[head + u] = acc
            return acc

        lax.fori_loop(0, groups // 8, add_up, jnp.zeros((tile, feat), F32))

    for q in range(cuts):
        contribute(r, q)
    from_in, from_out = [], [(mate, q) for q in range(cuts)]
    for q in range(cuts):
        from_in += [(place(2), q), (mate, q), (place(3), q)]
        from_out += [(place(2), q), (place(3), q)]
    row_copies, all_copies = [], []
    for k in range(3 * cuts):
        t = jnp.where(inner, from_in[k][0], from_out[k][0])
        q = jnp.where(inner, from_in[k][1], from_out[k][1])
        to_mate(t, q).wait_recv()
        if k % 3 != 1:
            @pl.when(inner)
            def pass_on(t=t, q=q):
                to_mate(t, q).start()
        contribute(t, q)
        if k == cuts - 1:
            @pl.when(outer)
            def early():
                gather(0)

            total = w_out[c]
            for copy in w_copies:
                copy.wait_recv()
            for d in range(1, nc):
                total = total + w_in[d - 1]
            w_row[r] = total
            for e in range(1, nr):
                copy = send(
                    w_row.at[r], w_row.at[r], wr_send.at[e - 1], wr_recv.at[e - 1], {"row": lax.rem(r + e, nr)}
                )
                copy.start()
                row_copies.append(copy)
        if k == 3 * cuts - 2:
            for copy in row_copies:
                copy.wait_recv()
            total = w_row[0]
            for n in range(1, nr):
                total = total + w_row[n]
            w_all[c] = total
            for d in range(1, nc):
                there = lax.rem(c + d, nc)
                copy = send(w_all.at[c], w_all.at[c], wa_send.at[d - 1], wa_recv.at[d - 1], {"col": there})
                copy.start()
                all_copies.append(copy)
    done += row_copies + all_copies

    hrows = tile // 2
    order = list(range(1, n_out)) + [0]

    def total_of(j, h):
        cut = pl.ds(h * hrows, hrows)
        return runs[tab_s[last_at, j], cut, :] + runs[tab_s[last_at, col_blocks + j], cut, :]

    def to_pair(h, d):
        return send(pair_out.at[h, d], pair_in.at[h, d], gp_send.at[h, d], gp_recv.at[h, d], {"col": partner})

    def to_chip(h, d):
        return send(
            chip_out.at[h, d - 1], chip_in.at[h, d - 1], gc_send.at[h, d - 1], gc_recv.at[h, d - 1], {"col": ahead[d]}
        )

    def hand_over(h):
        for d in order:
            def fill(n, carry, d=d):
                there = (ahead[d] + partner - c) * own_blocks + n
                pair_out[h, d, pl.ds(pl.multiple_of(n * hrows, hrows), hrows), :] = total_of(there, h).astype(BF16)
                return carry

            for n in range(own_blocks):
                fill(n, 0)
            to_pair(h, d).start()

    def combine(h):
        for d in order:
            to_pair(h, d).wait_recv()
            for n in range(own_blocks):
                cut = pl.ds(n * hrows, hrows)
                both = total_of(ahead[d] * own_blocks + n, h) + pair_in[h, d, cut, :].astype(F32)
                if d:
                    chip_out[h, d - 1, cut, :] = both.astype(BF16)
                else:
                    kept[h, cut, :] = both
            if d:
                to_chip(h, d).start()

    @pl.when(inner)
    def late():
        gather(0)

    gather(1)
    hand_over(0)
    hand_over(1)
    combine(0)
    combine(1)
    for copy in all_copies:
        copy.wait_recv()
    for n in range(nc):
        wb_ref[pl.ds(n * wcut, wcut), :] = w_all[n, pl.ds(0, wcut), :]
    wb_ref[pl.ds(feat, 8), :] = w_all[0, pl.ds(wcut, 8), :]
    for h in range(2):
        for d in range(1, n_out):
            to_chip(h, d).wait_recv()
        for n in range(own_blocks):
            cut = pl.ds(n * hrows, hrows)
            both = kept[h, cut, :]
            for d in range(1, n_out):
                both = both + chip_in[h, d - 1, cut, :].astype(F32)
            fg_ref[pl.ds(n * tile + h * hrows, hrows), :] = both.astype(BF16)
    for copy in done:
        copy.wait_send()
    for q in range(cuts):
        to_near(2, q).wait_send()
        to_other(q).wait_send()
        to_mate(r, q).wait_send()

    @pl.when(outer)
    def outer_sent():
        for e in range(2):
            for q in range(cuts):
                to_near(e, q).wait_send()

    @pl.when(inner)
    def inner_sent():
        for e in range(2):
            for q in range(cuts):
                to_far(e, q).wait_send()
                to_mate(targets[e], q).wait_send()

    for h in range(2):
        for d in range(n_out):
            to_pair(h, d).wait_send()
            if d:
                to_chip(h, d).wait_send()


def finish_kernel(fg_in, act_in, wb_in, act_out, fg_out, wg_out, bg_out, sem):
    feat = wg_out.shape[0]
    copies = []
    for n, (src, dst) in enumerate((
        (fg_in, fg_out), (act_in, act_out), (wb_in.at[pl.ds(0, feat)], wg_out), (wb_in.at[pl.ds(feat, 1)], bg_out),
    )):
        copy = pltpu.make_async_copy(src, dst, sem.at[n])
        copy.start()
        copies.append(copy)
    for copy in copies:
        copy.wait()


def whole_layer(mesh, features, adjacency, tile_cols, row_counts, weight, bias, out_grad):
    blocks, tile, slot_width = adjacency.shape
    own_rows, feat = features.shape
    nc, nr = mesh.shape["col"], mesh.shape["row"]
    n_out = nc // 2
    own_blocks = own_rows // tile
    col_blocks = nc * own_blocks
    per_row = slot_width // tile
    slots = blocks * per_row
    scale = 1.0 / math.sqrt(own_rows * nc * nr)
    cut = feat // nc
    rows = blocks * tile // nr
    groups = half_groups(slots, col_blocks)
    table_rows = -(-2 * GROUP * groups // 128) + -(-2 * groups // 128) + 1
    table_rows = -(-table_rows // 8) * 8

    vmem = pl.BlockSpec(memory_space=pltpu.VMEM)
    hbm = pl.BlockSpec(memory_space=pltpu.HBM)
    dma = pltpu.SemaphoreType.DMA
    tile_flops = 2 * blocks * tile * slot_width * feat
    fg, act, wb = pl.pallas_call(
        functools.partial(layer_kernel, nc, nr, scale),
        out_shape=(
            jax.ShapeDtypeStruct((own_rows, feat), BF16),
            jax.ShapeDtypeStruct((rows, feat), BF16),
            jax.ShapeDtypeStruct((feat + 8, feat), F32),
        ),
        in_specs=[hbm] * 7,
        out_specs=(vmem, vmem, vmem),
        scratch_shapes=[
            pltpu.SMEM((per_row, blocks), jnp.int32),
            pltpu.SMEM((1, blocks), jnp.int32),
            pltpu.SMEM((table_rows, 128), jnp.int32),
            pltpu.VMEM((per_row, blocks), jnp.int32),
            pltpu.VMEM((1, blocks), jnp.int32),
            pltpu.VMEM((table_rows, 128), jnp.int32),
            pltpu.VMEM((col_blocks + 1, tile, feat), BF16),
            pltpu.VMEM(adjacency.shape, BF16),
            pltpu.VMEM((feat, feat), BF16),
            pltpu.VMEM((1, feat), F32),
            pltpu.VMEM((rows, feat), BF16),
            pltpu.VMEM((nr, rows, feat), F32),
            pltpu.VMEM((3, rows, feat), BF16),
            pltpu.VMEM((3, rows, feat), BF16),
            pltpu.VMEM((rows, feat), BF16),
            pltpu.VMEM((rows, feat), BF16),
            pltpu.VMEM((rows, feat), BF16),
            pltpu.VMEM((nr, rows, feat), BF16),
            pltpu.VMEM((slots + 1, tile, feat), F32),
            pltpu.VMEM((2 * groups + 1, tile, feat), F32),
            pltpu.VMEM((2, n_out, own_rows // 2, feat), BF16),
            pltpu.VMEM((2, n_out, own_rows // 2, feat), BF16),
            pltpu.VMEM((2, n_out - 1, own_rows // 2, feat), BF16),
            pltpu.VMEM((2, n_out - 1, own_rows // 2, feat), BF16),
            pltpu.VMEM((2, own_rows // 2, feat), F32),
            pltpu.VMEM((nc, cut + 8, feat), F32),
            pltpu.VMEM((nc - 1, cut + 8, feat), F32),
            pltpu.VMEM((nr, cut + 8, feat), F32),
            pltpu.VMEM((nc, cut + 8, feat), F32),
            dma((9,)), dma((nr,)), dma((n_out,)), dma((n_out,)), dma((n_out,)), dma((n_out,)),
            dma((3, 4)), dma((3, 4)), dma((2, 4)), dma((4,)),
            dma((2, nr, 4)), dma((nr, 4)),
            dma((2, n_out)), dma((2, n_out)), dma((2, n_out - 1)), dma((2, n_out - 1)),
            dma((nc - 1,)), dma((nc - 1,)), dma((nr - 1,)), dma((nr - 1,)), dma((nc - 1,)), dma((nc - 1,)),
        ],
        compiler_params=pltpu.CompilerParams(
            collective_id=0, has_side_effects=True, vmem_limit_bytes=56 * MIB
        ),
        cost_estimate=pl.CostEstimate(
            flops=2 * tile_flops, bytes_accessed=adjacency.size * 2, transcendentals=rows * feat
        ),
    )(
        tile_cols.T, row_counts.T, features.reshape(own_blocks, tile, feat), adjacency, weight,
        bias.reshape(1, -1), out_grad,
    )
    activations, feature_grad, weight_grad, bias_grad = pl.pallas_call(
        finish_kernel,
        out_shape=(
            jax.ShapeDtypeStruct((rows, feat), BF16),
            jax.ShapeDtypeStruct((own_rows, feat), BF16),
            jax.ShapeDtypeStruct((feat, feat), F32),
            jax.ShapeDtypeStruct((1, feat), F32),
        ),
        in_specs=[vmem] * 3,
        out_specs=(hbm,) * 4,
        scratch_shapes=[dma((4,))],
    )(fg, act, wb)
    return (activations, feature_grad, weight_grad, bias_grad.reshape(-1))


def solution(mesh):
    small = mesh.shape["row"] == 4 and mesh.shape["col"] == 8
    placed = (
        P(("groups", "row", "col"), None),
        P(("groups", "col"), None, "row"),
        P(("groups", "col"), "row"),
        P(("groups", "col"), "row"),
        P(),
        P(),
        P(("groups", "col", "row"), None),
    )
    return jax.shard_map(
        functools.partial(whole_layer if small else on_device, mesh),
        mesh=mesh,
        in_specs=placed,
        out_specs=(
            P(("groups", "col", "row"), None),
            P(("groups", "row", "col"), None),
            P("groups", None),
            P("groups"),
        ),
        check_vma=False,
    )
```

```python
import functools
import math

import jax
import jax.numpy as jnp
from jax import lax
from jax.experimental import pallas as pl
from jax.experimental.pallas import tpu as pltpu
from jax.sharding import PartitionSpec as P

MESH = pl.DeviceIdType.MESH
F32, BF16 = jnp.float32, jnp.bfloat16
MIB = 1024 * 1024


def col_peers(nc):
    c = lax.axis_index("col")
    outer, core, n_out = c // 2, c % 2, nc // 2
    partner = outer * 2 + (1 - core)
    ahead = [lax.rem(outer + d, n_out) * 2 + core for d in range(n_out)]
    behind = [lax.rem(outer - d + n_out, n_out) * 2 + core for d in range(n_out)]
    return c, partner, ahead, behind


def send(src, dst, send_sem, recv_sem, where):
    return pltpu.make_async_remote_copy(
        src_ref=src, dst_ref=dst, send_sem=send_sem, recv_sem=recv_sem,
        device_id=where, device_id_type=MESH,
    )


def enter(nc, nr):
    c, r = lax.axis_index("col"), lax.axis_index("row")
    barrier = pltpu.get_barrier_semaphore()
    for d in range(1, nc):
        pl.semaphore_signal(barrier, inc=1, device_id={"col": lax.rem(c + d, nc)}, device_id_type=MESH)
    for e in range(1, nr):
        pl.semaphore_signal(barrier, inc=1, device_id={"row": lax.rem(r + e, nr)}, device_id_type=MESH)
    pl.semaphore_wait(barrier, nc - 1 + nr - 1)


def forward_kernel(
    nc, nr, scale, cols_ref, counts_ref, feat_hbm, adj_hbm, weight_hbm, bias_hbm, og_hbm,
    grads_ref, wb_ref,
    xg, adj, weight_ref, bias_ref, og_ref, own, part, rbuf, gg, w_out, w_in, w_all,
    in_sem, a_sem, f_send, f_recv, p_send, p_recv, r_send, r_recv, g_send, g_recv, w_send, w_recv, wa_send, wa_recv,
):
    blocks, tile, slot_width = adj.shape
    per_row = slot_width // tile
    chunk = blocks // nr
    rows = chunk * tile
    n_out = nc // 2
    own_blocks = feat_hbm.shape[0]
    c, partner, ahead, behind = col_peers(nc)
    r = lax.axis_index("row")
    row_at = [lax.rem(r + e, nr) for e in range(nr)]

    mine = xg.at[pl.ds(c * own_blocks, own_blocks)]
    first = pltpu.make_async_copy(feat_hbm, mine, in_sem.at[0])
    first.start()
    loads = []
    for e in range(nr):
        t = row_at[(e + 1) % nr]
        cut = pl.ds(t * chunk, chunk)
        load = pltpu.make_async_copy(adj_hbm.at[cut], adj.at[cut], a_sem.at[e])
        load.start()
        loads.append(load)
    small = []
    for n, (src, dst) in enumerate(((weight_hbm, weight_ref), (bias_hbm, bias_ref), (og_hbm, og_ref))):
        load = pltpu.make_async_copy(src, dst, in_sem.at[n + 1])
        load.start()
        small.append(load)

    def blocks_of(col):
        return xg.at[pl.ds(col * own_blocks, own_blocks)]

    xg[nc * own_blocks] = jnp.zeros(xg.shape[1:], xg.dtype)
    first.wait()
    enter(nc, nr)

    copies = []
    for d in range(1, n_out):
        copy = send(blocks_of(c), blocks_of(c), f_send.at[d], f_recv.at[d], {"col": ahead[d]})
        copy.start()
        copies.append(copy)
    pair = []
    copy = send(blocks_of(c), blocks_of(c), p_send.at[0], p_recv.at[0], {"col": partner})
    copy.start()
    pair.append(copy)
    for d in range(1, n_out):
        copies[d - 1].wait_recv()
        came = blocks_of(behind[d])
        copy = send(came, came, p_send.at[d], p_recv.at[d], {"col": partner})
        copy.start()
        pair.append(copy)
    for copy in pair:
        copy.wait_recv()
    for copy in copies + pair:
        copy.wait_send()

    pace = math.gcd(chunk, 4)
    row_copies = []
    for e in range(nr):
        far = (e + 1) % nr
        t = row_at[far]
        loads[e].wait()

        def block_rows(n, carry, t=t, far=far):
            for i in range(pace):
                i = n * pace + i
                b = t * chunk + i
                count = counts_ref[0, b]
                picked = [
                    xg[jnp.where(s < count, cols_ref[s, b], nc * own_blocks)] for s in range(per_row)
                ]
                got = jnp.dot(adj[b], jnp.concatenate(picked, axis=0), preferred_element_type=F32)
                cut = pl.ds(pl.multiple_of(i * tile, tile), tile)
                if far:
                    part[far - 1, cut, :] = got.astype(BF16)
                else:
                    own[cut, :] = got
            return carry

        lax.fori_loop(0, chunk // pace, block_rows, 0)
        if far:
            copy = send(
                part.at[far - 1], rbuf.at[far - 1], r_send.at[far - 1], r_recv.at[far - 1], {"row": t}
            )
            copy.start()
            row_copies.append(copy)
    summed = own[...]
    for copy in row_copies:
        copy.wait_recv()
    for e in range(nr - 1):
        summed = summed + rbuf[e].astype(F32)
    hidden = summed.astype(BF16)
    for load in small:
        load.wait()
    preact = jnp.dot(hidden, weight_ref[...], preferred_element_type=F32) + bias_ref[...]
    sig = jax.nn.sigmoid(preact)
    pre_grad = og_ref[...].astype(F32) * (sig * (1.0 + preact * (1.0 - sig)))
    half = pre_grad.astype(BF16)
    dest = lax.dot_general(
        half, weight_ref[...], (((1,), (1,)), ((), ())), preferred_element_type=F32
    )
    gg[r] = dest.astype(BF16)

    def hop(t, step):
        way = 0 if step > 0 else 1
        return send(gg.at[t], gg.at[t], g_send.at[way, t], g_recv.at[t], {"row": r + step})

    for step in (1, -1):
        @pl.when((r + step >= 0) & (r + step < nr))
        def start_chain(step=step):
            hop(r, step).start()
    grads_ref[pl.ds(nr * rows, rows), :] = (preact * sig).astype(BF16)
    feat = hidden.shape[1]
    cut = feat // nc
    w_out[:, pl.ds(0, cut), :] = scale * lax.dot_general(
        hidden, half, (((0,), (0,)), ((), ())), preferred_element_type=F32
    ).reshape(nc, cut, feat)
    w_out[:, pl.ds(cut, 8), :] = jnp.broadcast_to(
        scale * jnp.sum(pre_grad, axis=0, keepdims=True), (nc, 8, feat)
    )
    w_copies = []
    for d in range(1, nc):
        there = lax.rem(c + d, nc)
        copy = send(w_out.at[there], w_in.at[d - 1], w_send.at[d - 1], w_recv.at[d - 1], {"col": there})
        copy.start()
        w_copies.append(copy)
    for k in range(1, nr):
        if k == min(2, nr - 1):
            total = w_out[c]
            for d in range(1, nc):
                w_copies[d - 1].wait_recv()
                total = total + w_in[d - 1]
            w_all[c] = total
            for d in range(1, nc):
                there = lax.rem(c + d, nc)
                copy = send(w_all.at[c], w_all.at[c], wa_send.at[d - 1], wa_recv.at[d - 1], {"col": there})
                copy.start()
                w_copies.append(copy)
        for step in (1, -1):
            t = r - k * step
            came = (t >= 0) & (t < nr)

            @pl.when(came)
            def arrive(t=t, step=step):
                hop(t, step).wait_recv()

            @pl.when(came & (r + step >= 0) & (r + step < nr))
            def pass_on(t=t, step=step):
                hop(t, step).start()
    for k in range(nr):
        for step in (1, -1):
            t = r - k * step

            @pl.when((t >= 0) & (t < nr) & (r + step >= 0) & (r + step < nr))
            def sent(t=t, step=step):
                hop(t, step).wait_send()
    for copy in w_copies[nc - 1 :]:
        copy.wait_recv()
    for n in range(nc):
        wb_ref[pl.ds(n * cut, cut), :] = w_all[n, pl.ds(0, cut), :]
    wb_ref[pl.ds(feat, 8), :] = w_all[0, pl.ds(cut, 8), :]
    grads_ref[pl.ds(0, nr * rows), :] = gg[...].reshape(nr * rows, feat)
    for copy in row_copies + w_copies:
        copy.wait_send()


def backward_kernel(cols_ref, counts_ref, adj_ref, grad_ref, out_ref, act_out, sem, *accs):
    blocks, tile, slot_width = adj_ref.shape
    per_row = slot_width // tile
    dead = out_ref.shape[0]
    hand_out = pltpu.make_async_copy(grad_ref.at[pl.ds(blocks * tile, act_out.shape[0])], act_out, sem)
    hand_out.start()
    for acc in accs:
        acc[...] = jnp.zeros_like(acc)

    pace = math.gcd(blocks, 4)

    def block_rows(n, carry):
        contribs = []
        for i in range(pace):
            b = n * pace + i
            contribs.append(lax.dot_general(
                adj_ref[b], grad_ref[pl.ds(pl.multiple_of(b * tile, tile), tile), :],
                (((0,), (0,)), ((), ())), preferred_element_type=F32,
            ))
        for s in range(per_row):
            for i in range(pace):
                b = n * pace + i
                acc = accs[i]
                j = jnp.where(s < counts_ref[0, b], cols_ref[s, b], dead)
                acc[j] = acc[j] + contribs[i][s * tile : (s + 1) * tile]
        return carry

    lax.fori_loop(0, blocks // pace, block_rows, 0)
    total = accs[0][pl.ds(0, dead)]
    for acc in accs[1:]:
        total = total + acc[pl.ds(0, dead)]
    out_ref[...] = total.astype(BF16)
    hand_out.wait()


def scatter_kernel(
    nc, nr, part_ref, wb_ref, out_ref, wg_ref, bg_ref,
    from_pair, send_buf, from_chip, w_row,
    p_send, p_recv, s_send, s_recv, wr_send, wr_recv,
):
    n_out = nc // 2
    c, partner, ahead, behind = col_peers(nc)
    r = lax.axis_index("row")
    row_at = [lax.rem(r + e, nr) for e in range(nr)]
    partner_ahead = [x + partner - c for x in ahead]
    enter(nc, nr)

    started = []

    def go(*args):
        copy = send(*args)
        copy.start()
        started.append(copy)
        return copy

    order = list(range(1, n_out)) + [0]
    pair = {}
    for d in order:
        pair[d] = go(part_ref.at[partner_ahead[d]], from_pair.at[d], p_send.at[d], p_recv.at[d], {"col": partner})
    w_row[r] = wb_ref[...]
    w_copies = [
        go(w_row.at[r], w_row.at[r], wr_send.at[e - 1], wr_recv.at[e - 1], {"row": row_at[e]})
        for e in range(1, nr)
    ]
    copies = []
    for d in order:
        pair[d].wait_recv()
        both = part_ref[ahead[d]].astype(F32) + from_pair[d].astype(F32)
        if d:
            send_buf[d - 1] = both.astype(BF16)
            copies.append(go(
                send_buf.at[d - 1], from_chip.at[d - 1], s_send.at[d - 1], s_recv.at[d - 1], {"col": ahead[d]}
            ))
    for copy in copies:
        copy.wait_recv()
    for d in range(1, n_out):
        both = both + from_chip[d - 1].astype(F32)
    out_ref[...] = both.astype(BF16)
    for copy in w_copies:
        copy.wait_recv()
    total = w_row[0]
    for n in range(1, nr):
        total = total + w_row[n]
    feat = wg_ref.shape[0]
    wg_ref[...] = total[:feat]
    bg_ref[...] = total[feat : feat + 1]
    for copy in started:
        copy.wait_send()


def on_device(mesh, features, adjacency, tile_cols, row_counts, weight, bias, out_grad):
    blocks, tile, slot_width = adjacency.shape
    own_rows, feat = features.shape
    nc, nr = mesh.shape["col"], mesh.shape["row"]
    n_out = nc // 2
    col_blocks = nc * own_rows // tile
    scale = 1.0 / math.sqrt(own_rows * nc * nr)
    cut = feat // nc

    vmem = pl.BlockSpec(memory_space=pltpu.VMEM)
    smem = pl.BlockSpec(memory_space=pltpu.SMEM)
    hbm = pl.BlockSpec(memory_space=pltpu.HBM)
    dma = pltpu.SemaphoreType.DMA
    rows = blocks * tile // nr
    tile_flops = 2 * blocks * tile * slot_width * feat
    grads, wb = pl.pallas_call(
        functools.partial(forward_kernel, nc, nr, scale),
        out_shape=(
            jax.ShapeDtypeStruct((blocks * tile + rows, feat), BF16),
            jax.ShapeDtypeStruct((feat + 8, feat), F32),
        ),
        in_specs=[smem, smem, hbm, hbm, hbm, hbm, hbm],
        out_specs=(vmem, vmem),
        scratch_shapes=[
            pltpu.VMEM((col_blocks + 1, tile, feat), BF16),
            pltpu.VMEM(adjacency.shape, BF16),
            pltpu.VMEM((feat, feat), BF16),
            pltpu.VMEM((1, feat), F32),
            pltpu.VMEM((rows, feat), BF16),
            pltpu.VMEM((rows, feat), F32),
            pltpu.VMEM((nr - 1, rows, feat), BF16),
            pltpu.VMEM((nr - 1, rows, feat), BF16),
            pltpu.VMEM((nr, rows, feat), BF16),
            pltpu.VMEM((nc, cut + 8, feat), F32),
            pltpu.VMEM((nc - 1, cut + 8, feat), F32),
            pltpu.VMEM((nc, cut + 8, feat), F32),
            dma((4,)), dma((nr,)), dma((n_out,)), dma((n_out,)), dma((n_out,)), dma((n_out,)),
            dma((nr - 1,)), dma((nr - 1,)), dma((2, nr)), dma((nr,)),
            dma((nc - 1,)), dma((nc - 1,)), dma((nc - 1,)), dma((nc - 1,)),
        ],
        compiler_params=pltpu.CompilerParams(
            collective_id=0, has_side_effects=True, vmem_limit_bytes=56 * MIB
        ),
        cost_estimate=pl.CostEstimate(
            flops=tile_flops, bytes_accessed=adjacency.size * 2, transcendentals=rows * feat
        ),
    )(
        tile_cols.T, row_counts.T, features.reshape(own_rows // tile, tile, feat), adjacency, weight,
        bias.reshape(1, -1), out_grad,
    )

    partial, activations = pl.pallas_call(
        backward_kernel,
        out_shape=(
            jax.ShapeDtypeStruct((col_blocks, tile, feat), BF16),
            jax.ShapeDtypeStruct((rows, feat), BF16),
        ),
        in_specs=[smem, smem, vmem, vmem],
        out_specs=(vmem, hbm),
        scratch_shapes=[dma] + [pltpu.VMEM((col_blocks + 1, tile, feat), F32) for unused in range(4)],
        compiler_params=pltpu.CompilerParams(vmem_limit_bytes=32 * MIB),
        cost_estimate=pl.CostEstimate(
            flops=tile_flops * 8, bytes_accessed=adjacency.size * 2, transcendentals=0
        ),
    )(tile_cols.T, row_counts.T, adjacency, grads)

    feature_grad, weight_grad, bias_grad = pl.pallas_call(
        functools.partial(scatter_kernel, nc, nr),
        out_shape=(
            jax.ShapeDtypeStruct((own_rows, feat), BF16),
            jax.ShapeDtypeStruct((feat, feat), F32),
            jax.ShapeDtypeStruct((1, feat), F32),
        ),
        in_specs=[vmem, vmem],
        out_specs=(vmem, vmem, vmem),
        scratch_shapes=[
            pltpu.VMEM((n_out, own_rows, feat), BF16),
            pltpu.VMEM((n_out - 1, own_rows, feat), BF16),
            pltpu.VMEM((n_out - 1, own_rows, feat), BF16),
            pltpu.VMEM((nr, feat + 8, feat), F32),
            dma((n_out,)), dma((n_out,)), dma((n_out - 1,)), dma((n_out - 1,)),
            dma((nr - 1,)), dma((nr - 1,)),
        ],
        compiler_params=pltpu.CompilerParams(
            collective_id=1, has_side_effects=True, vmem_limit_bytes=20 * MIB
        ),
        cost_estimate=pl.CostEstimate(
            flops=own_rows * nc * feat, bytes_accessed=8 * own_rows * nc * feat, transcendentals=0
        ),
    )(partial.reshape(nc, own_rows, feat), wb)
    return (activations, feature_grad, weight_grad, bias_grad.reshape(-1))


GROUP = 4


def slot_tables(cols_ref, counts_ref, col_blocks, mine, tab_ref):
    per_row, blocks = cols_ref.shape
    slots = per_row * blocks
    groups = half_groups(slots, col_blocks)
    keys = 2 * col_blocks

    def iota(shape, axis):
        return lax.broadcasted_iota(jnp.int32, shape, axis)

    def upright(row):
        n = row.shape[1]
        return jnp.sum(jnp.where(iota((n, n), 0) == iota((n, n), 1), row, 0), axis=1, keepdims=True)

    lane = iota((blocks, keys), 1)
    block = iota((blocks, 1), 0)
    late = jnp.where((block >= mine) & (block < mine + blocks // 2), 0, col_blocks)
    counts = upright(counts_ref[...])
    seen = jnp.zeros((blocks, keys), jnp.int32)
    hits, ranks = [], []
    for s in range(per_row):
        hit = jnp.where((upright(cols_ref[pl.ds(s, 1), :]) + late == lane) & (counts > s), 1, 0)
        hits.append(hit)
        ranks.append(seen)
        seen = seen + hit
    earlier = jnp.zeros((blocks, keys), jnp.int32)
    for b in range(blocks - 1):
        earlier = earlier + jnp.where(block > b, seen[b : b + 1, :], 0)
    sizes = lax.shift_right_logical(jnp.sum(seen, axis=0, keepdims=True) + (GROUP - 1), 2)
    square = (keys, keys)
    first, second = iota(square, 0), iota(square, 1)
    lower = (first < second) & ((first < col_blocks) == (second < col_blocks))
    starts = jnp.sum(jnp.where(lower, upright(sizes), 0), axis=0, keepdims=True)
    starts = starts + jnp.where(iota((1, keys), 1) < col_blocks, 0, groups)
    places = -(-2 * GROUP * groups // 128) * 128
    heads = -(-2 * groups // 128) * 128
    place = iota((blocks, places), 1)
    head = iota((blocks, heads), 1) * GROUP
    found = jnp.zeros((blocks, places), jnp.int32)
    fresh = jnp.zeros((blocks, heads), jnp.int32)
    for s in range(per_row):
        rank = jnp.sum(hits[s] * (ranks[s] + earlier), axis=1, keepdims=True)
        at = jnp.sum(hits[s] * (GROUP * starts), axis=1, keepdims=True) + rank
        at = jnp.where(counts > s, at, -1)
        found = found + jnp.where(at == place, slots - (block * per_row + s), 0)
        fresh = fresh + jnp.where((at == head) & (rank == 0), 1, 0)
    found = slots - jnp.sum(found, axis=0, keepdims=True)
    fresh = jnp.sum(fresh, axis=0, keepdims=True)
    last = jnp.where(sizes > 0, starts + sizes - 1, 2 * groups)
    n = 0
    for value in (found, fresh):
        for k in range(value.shape[1] // 128):
            tab_ref[pl.ds(n, 1), :] = value[:, k * 128 : (k + 1) * 128]
            n += 1
    tab_ref[pl.ds(n, 1), pl.ds(0, keys)] = last


def square_peers():
    c = lax.axis_index("col")
    y, x, core = c // 4, c // 2 % 2, c % 2

    def at(dy, dx):
        return (y + dy) % 2 * 4 + (x + dx) % 2 * 2 + core

    return c, c + 1 - 2 * core, [c, at(1, 1), at(0, 1), at(1, 0)]


def half_groups(slots, col_blocks):
    most = (slots // 2 + (GROUP - 1) * min(col_blocks, slots // 2)) // GROUP
    return -(-most // 8) * 8


def layer_kernel(
    nc, nr, scale, cols_hbm, counts_hbm, feat_hbm, adj_hbm, weight_hbm, bias_hbm, og_hbm,
    fg_ref, act_ref, wb_ref,
    cols_s, counts_s, tab_s, cols_v, counts_v, tab_v,
    xg, adj, weight_ref, bias_ref, og_ref, pf, part, near, far, hid, half, bias_sum, gg,
    contrib, runs, pair_out, pair_in, chip_out, chip_in, kept,
    w_out, w_in, w_row, w_all,
    in_sem, a_sem, f_send, f_recv, n_send, n_recv, r_send, r_recv,
    g_send, g_recv, gp_send, gp_recv, gc_send, gc_recv,
    w_send, w_recv, wr_send, wr_recv, wa_send, wa_recv,
):
    blocks, tile, slot_width = adj.shape
    per_row = slot_width // tile
    slots = blocks * per_row
    chunk = blocks // nr
    rows = chunk * tile
    n_out = nc // 2
    own_blocks = feat_hbm.shape[0]
    col_blocks = nc * own_blocks
    feat = weight_ref.shape[0]
    groups = half_groups(slots, col_blocks)
    cuts = 4
    fresh_at = -(-2 * GROUP * groups // 128)
    last_at = fresh_at + -(-2 * groups // 128)
    step = rows // cuts
    c, partner, ahead = square_peers()
    r = lax.axis_index("row")

    barrier = pltpu.get_barrier_semaphore()
    for d in range(1, nc):
        pl.semaphore_signal(barrier, inc=1, device_id={"col": lax.rem(c + d, nc)}, device_id_type=MESH)
    for e in range(1, nr):
        pl.semaphore_signal(barrier, inc=1, device_id={"row": lax.rem(r + e, nr)}, device_id_type=MESH)

    half_blocks = own_blocks // 2
    odd, even = c % 2 == 1, c % 2 == 0
    chip_x, chip_y, chip_d = [ahead[n] - c % 2 for n in (2, 3, 1)]

    def feat_part(col, h):
        return xg.at[pl.ds(col * own_blocks + h * half_blocks, half_blocks)]

    def give(slot, src, col, h, there):
        return send(src, feat_part(col, h), f_send.at[slot], f_recv.at[col, h], {"col": there})

    first = []
    for h in range(2):
        mine = feat_hbm.at[pl.ds(h * half_blocks, half_blocks)]
        first.append((h, give(h, mine, c, h, chip_x + 1)))
        first.append((1 - h, give(2 + h, mine, c, h, chip_y + 1)))
        first.append((2 + h, give(4 + h, mine, c, h, partner)))
    first = [copy for unused, copy in sorted(first, key=lambda pair: pair[0])]

    relays, keeps, last_ones = [], [], []
    for k in (1, 0):
        relays.append((chip_x + k, 0, chip_y + 1))
        relays.append((chip_y + k, 1, chip_x + 1))
        keeps += [(chip_x + k, 1), (chip_y + k, 0)]
        last_ones += [(chip_d + k, 0), (chip_d + k, 1)]
    inside = [(col, h) for col, h, unused in relays] + keeps + last_ones
    relays = [give(6 + n, feat_part(col, h), col, h, there) for n, (col, h, there) in enumerate(relays)]
    inside = [give(10 + n, feat_part(col, h), col, h, partner) for n, (col, h) in enumerate(inside)]

    pl.semaphore_wait(barrier, nc - 1 + nr - 1)
    for copy in first:
        copy.start()

    loads = {}
    for n, (name, src, dst) in enumerate((
        ("cols_v", cols_hbm, cols_v), ("counts_v", counts_hbm, counts_v),
        ("feat", feat_hbm, xg.at[pl.ds(c * own_blocks, own_blocks)]), ("cols_s", cols_hbm, cols_s),
        ("counts_s", counts_hbm, counts_s),
        ("weight", weight_hbm, weight_ref), ("bias", bias_hbm, bias_ref), ("og", og_hbm, og_ref),
    )):
        loads[name] = pltpu.make_async_copy(src, dst, in_sem.at[n])
        loads[name].start()

    mirrored = r >= 2
    inner = (r == 1) | (r == 2)
    outer = (r == 0) | (r == 3)

    def place(d):
        return jnp.where(mirrored, 3 - d, d)

    mate = jnp.where(r % 2 == 0, r + 1, r - 1)
    targets = [place(3), place(2), mate, r]
    for e in range(nr):
        cut = pl.ds(targets[e] * chunk, chunk)
        load = pltpu.make_async_copy(adj_hbm.at[cut], adj.at[cut], a_sem.at[e])
        load.start()
        loads[e] = load

    xg[col_blocks] = jnp.zeros(xg.shape[1:], xg.dtype)
    contrib[slots] = jnp.zeros(contrib.shape[1:], F32)
    runs[2 * groups] = jnp.zeros(runs.shape[1:], F32)

    @pl.when(odd)
    def relay():
        for n in range(4):
            inside[n].wait_recv()
            relays[n].start()
            inside[n].start()

    loads["cols_v"].wait()
    loads["counts_v"].wait()
    slot_tables(cols_v, counts_v, col_blocks, r // 2 * (blocks // 2), tab_v)
    table = pltpu.make_async_copy(tab_v, tab_s, in_sem.at[8])
    table.start()

    @pl.when(odd)
    def pass_inside():
        for n in range(4, 12):
            inside[n].wait_recv()
            inside[n].start()

    @pl.when(even)
    def take_inside():
        for n in range(12):
            inside[n].wait_recv()

    for name in ("feat", "cols_s", "counts_s"):
        loads[name].wait()
    table.wait()
    for h in range(2):
        give(4 + h, feat_part(partner, h), partner, h, partner).wait_recv()

    def piece(q):
        return pl.ds(q * step, step)

    def to_near(e, q):
        return send(part.at[e, piece(q)], near.at[e, piece(q)], n_send.at[e, q], n_recv.at[e, q], {"row": mate})

    def to_far(e, q):
        return send(part.at[e, piece(q)], far.at[piece(q)], r_send.at[e, q], r_recv.at[q], {"row": targets[e]})

    def products(e, q):
        def block_rows(n, carry):
            for i in range(2):
                i = q * (chunk // cuts) + n * 2 + i
                b = targets[e] * chunk + i
                count = counts_s[0, b]
                picked = [xg[jnp.where(s < count, cols_s[s, b], col_blocks)] for s in range(per_row)]
                got = jnp.dot(adj[b], jnp.concatenate(picked, axis=0), preferred_element_type=F32)
                cut = pl.ds(pl.multiple_of(i * tile, tile), tile)
                pf[e, cut, :] = got
                if e < 3:
                    part[e, cut, :] = got.astype(BF16)
            return carry

        lax.fori_loop(0, chunk // cuts // 2, block_rows, 0)

    loads[0].wait()
    loads[1].wait()
    for q in range(cuts):
        for e in range(2):
            products(e, q)

            @pl.when(outer)
            def hand_in(e=e, q=q):
                to_near(e, q).start()
    for e in (2, 3):
        loads[e].wait()
        for q in range(cuts):
            products(e, q)
            if e == 2:
                to_near(e, q).start()
    for q in range(cuts):
        for e in range(2):
            @pl.when(inner)
            def join(e=e, q=q):
                to_near(e, q).wait_recv()
                part[e, piece(q), :] = (pf[e, piece(q), :] + near[e, piece(q), :].astype(F32)).astype(BF16)
                to_far(e, q).start()

    def to_mate(t, q):
        return send(gg.at[t, piece(q)], gg.at[t, piece(q)], g_send.at[0, t, q], g_recv.at[t, q], {"row": mate})

    def to_other(q):
        return send(gg.at[r, piece(q)], gg.at[r, piece(q)], g_send.at[1, r, q], g_recv.at[r, q], {"row": place(2)})

    for name in ("weight", "bias", "og"):
        loads[name].wait()
    bias_part = jnp.zeros((1, feat), F32)
    for q in range(cuts):
        cut = piece(q)
        to_near(2, q).wait_recv()
        to_far(0, q).wait_recv()
        hidden = (pf[3, cut, :] + near[2, cut, :].astype(F32) + far[cut, :].astype(F32)).astype(BF16)
        preact = jnp.dot(hidden, weight_ref[...], preferred_element_type=F32) + bias_ref[...]
        sig = jax.nn.sigmoid(preact)
        pre_grad = og_ref[cut, :].astype(F32) * (sig * (1.0 + preact * (1.0 - sig)))
        small = pre_grad.astype(BF16)
        dest = lax.dot_general(small, weight_ref[...], (((1,), (1,)), ((), ())), preferred_element_type=F32)
        gg[r, cut, :] = dest.astype(BF16)
        to_other(q).start()
        to_mate(r, q).start()
        act_ref[cut, :] = (preact * sig).astype(BF16)
        hid[cut, :] = hidden
        half[cut, :] = small
        bias_part = bias_part + jnp.sum(pre_grad, axis=0, keepdims=True)
    bias_sum[...] = bias_part

    wcut = feat // nc

    def to_col(src, dst, sems, d):
        return send(src, dst, sems[0].at[d - 1], sems[1].at[d - 1], {"col": lax.rem(c + d, nc)})

    def w_first(d):
        return to_col(w_out.at[lax.rem(c + d, nc)], w_in.at[d - 1], (w_send, w_recv), d)

    def w_second(e):
        return send(w_row.at[r], w_row.at[r], wr_send.at[e - 1], wr_recv.at[e - 1], {"row": lax.rem(r + e, nr)})

    def w_third(d):
        return to_col(w_all.at[c], w_all.at[c], (wa_send, wa_recv), d)

    def weight_terms():
        w_out[:, pl.ds(0, wcut), :] = scale * lax.dot_general(
            hid[...], half[...], (((0,), (0,)), ((), ())), preferred_element_type=F32
        ).reshape(nc, wcut, feat)
        w_out[:, pl.ds(wcut, 8), :] = jnp.broadcast_to(scale * bias_sum[...], (nc, 8, feat))
        for d in range(1, nc):
            w_first(d).start()

    def weight_rows():
        total = w_out[c]
        for d in range(1, nc):
            w_first(d).wait_recv()
            total = total + w_in[d - 1]
        w_row[r] = total
        for e in range(1, nr):
            w_second(e).start()

    def weight_whole():
        for e in range(1, nr):
            w_second(e).wait_recv()
        total = w_row[0]
        for n in range(1, nr):
            total = total + w_row[n]
        w_all[c] = total
        for d in range(1, nc):
            w_third(d).start()

    def contribute(t, q):
        def pairs(n, carry):
            b = t * chunk + q * (chunk // cuts) + n * 2
            lhs = adj[pl.ds(b, 2)].reshape(2 * tile, slot_width)
            g = gg[t, pl.ds(pl.multiple_of(q * step + n * 2 * tile, 2 * tile), 2 * tile), :]
            upper = lax.broadcasted_iota(jnp.int32, g.shape, 0) < tile
            zero = jnp.zeros_like(g)
            rhs = jnp.concatenate([jnp.where(upper, g, zero), jnp.where(upper, zero, g)], axis=1)
            got = lax.dot_general(lhs, rhs, (((0,), (0,)), ((), ())), preferred_element_type=F32)
            contrib[pl.ds(b * per_row, per_row)] = got[:, :feat].reshape(per_row, tile, feat)
            contrib[pl.ds(b * per_row + per_row, per_row)] = got[:, feat:].reshape(per_row, tile, feat)
            return carry

        lax.fori_loop(0, chunk // cuts // 2, pairs, 0)

    def gather(part_of, low=0, high=tile):
        span = pl.ds(low, high - low)

        def add_up(n, acc):
            spot = part_of * GROUP * groups + n * 8 * GROUP
            head = part_of * groups + n * 8
            for u in range(8):
                terms = [contrib[tab_s[spot // 128, spot % 128 + u * GROUP + k], span, :] for k in range(GROUP)]
                new = tab_s[fresh_at + head // 128, head % 128 + u]
                acc = jnp.where(new > 0, 0.0, acc) + ((terms[0] + terms[1]) + (terms[2] + terms[3]))
                runs[head + u, span, :] = acc
            return acc

        lax.fori_loop(0, groups // 8, add_up, jnp.zeros((high - low, feat), F32))

    near_in, far_in = place(2), place(3)
    from_in = [(r, q) for q in range(cuts)]
    from_out = from_in + [(mate, q) for q in range(cuts)]
    passed = []
    for q in range(cuts):
        from_in += [(mate, q), (near_in, q), (far_in, q)]
        from_out += [(near_in, q), (far_in, q)]
        passed += [(near_in, q), (far_in, q)]
    for k in range(4 * cuts):
        if 2 <= k < 2 + len(passed):
            @pl.when(inner)
            def pass_on(t=passed[k - 2][0], q=passed[k - 2][1]):
                to_mate(t, q).wait_recv()
                to_mate(t, q).start()
        if k == cuts:
            pl.when(outer)(weight_terms)
        if k == 2 + len(passed):
            pl.when(inner)(weight_terms)
        if k == 4 * cuts - 2:
            weight_rows()
        if k == 2 * cuts:
            @pl.when(outer)
            def early():
                gather(0)
        if k >= cuts:
            @pl.when(outer)
            def came(k=k):
                to_mate(*from_out[k]).wait_recv()
        if from_in[k][0] is mate:
            @pl.when(inner)
            def mate_came(k=k):
                to_mate(*from_in[k]).wait_recv()
        contribute(
            jnp.where(inner, from_in[k][0], from_out[k][0]), jnp.where(inner, from_in[k][1], from_out[k][1])
        )

    hrows = tile // 2
    order = list(range(1, n_out)) + [0]

    def total_of(j, h):
        cut = pl.ds(h * hrows, hrows)
        return runs[tab_s[last_at, j], cut, :] + runs[tab_s[last_at, col_blocks + j], cut, :]

    def to_pair(h, d):
        return send(pair_out.at[h, d], pair_in.at[h, d], gp_send.at[h, d], gp_recv.at[h, d], {"col": partner})

    def to_chip(h, d):
        return send(
            chip_out.at[h, d - 1], chip_in.at[h, d - 1], gc_send.at[h, d - 1], gc_recv.at[h, d - 1], {"col": ahead[d]}
        )

    def hand_over(h):
        for d in order:
            def fill(n, carry, d=d):
                there = (ahead[d] + partner - c) * own_blocks + n
                pair_out[h, d, pl.ds(pl.multiple_of(n * hrows, hrows), hrows), :] = total_of(there, h).astype(BF16)
                return carry

            for n in range(own_blocks):
                fill(n, 0)
            to_pair(h, d).start()

    def combine(h):
        for d in order:
            to_pair(h, d).wait_recv()
            for n in range(own_blocks):
                cut = pl.ds(n * hrows, hrows)
                both = total_of(ahead[d] * own_blocks + n, h) + pair_in[h, d, cut, :].astype(F32)
                if d:
                    chip_out[h, d - 1, cut, :] = both.astype(BF16)
                else:
                    kept[h, cut, :] = both
            if d:
                to_chip(h, d).start()

    @pl.when(inner)
    def late():
        gather(0)

    gather(1, 0, hrows)
    hand_over(0)
    weight_whole()
    gather(1, hrows, tile)
    combine(0)
    hand_over(1)
    combine(1)
    for d in range(1, nc):
        w_third(d).wait_recv()
    for n in range(nc):
        wb_ref[pl.ds(n * wcut, wcut), :] = w_all[n, pl.ds(0, wcut), :]
    wb_ref[pl.ds(feat, 8), :] = w_all[0, pl.ds(wcut, 8), :]
    for h in range(2):
        for d in range(1, n_out):
            to_chip(h, d).wait_recv()
        for n in range(own_blocks):
            cut = pl.ds(n * hrows, hrows)
            both = kept[h, cut, :]
            for d in range(1, n_out):
                both = both + chip_in[h, d - 1, cut, :].astype(F32)
            fg_ref[pl.ds(n * tile + h * hrows, hrows), :] = both.astype(BF16)
    for copy in first:
        copy.wait_send()

    @pl.when(odd)
    def odd_sent():
        for copy in relays + inside:
            copy.wait_send()

    for d in range(1, nc):
        w_first(d).wait_send()
        w_third(d).wait_send()
    for e in range(1, nr):
        w_second(e).wait_send()
    for q in range(cuts):
        to_near(2, q).wait_send()
        to_other(q).wait_send()
        to_mate(r, q).wait_send()

    @pl.when(outer)
    def outer_sent():
        for e in range(2):
            for q in range(cuts):
                to_near(e, q).wait_send()

    @pl.when(inner)
    def inner_sent():
        for e in range(2):
            for q in range(cuts):
                to_far(e, q).wait_send()
                to_mate(targets[e], q).wait_send()

    for h in range(2):
        for d in range(n_out):
            to_pair(h, d).wait_send()
            if d:
                to_chip(h, d).wait_send()


def finish_kernel(fg_in, act_in, wb_in, act_out, fg_out, wg_out, bg_out, sem):
    feat = wg_out.shape[0]
    copies = []
    for n, (src, dst) in enumerate((
        (fg_in, fg_out), (act_in, act_out), (wb_in.at[pl.ds(0, feat)], wg_out), (wb_in.at[pl.ds(feat, 1)], bg_out),
    )):
        copy = pltpu.make_async_copy(src, dst, sem.at[n])
        copy.start()
        copies.append(copy)
    for copy in copies:
        copy.wait()


def whole_layer(mesh, features, adjacency, tile_cols, row_counts, weight, bias, out_grad):
    blocks, tile, slot_width = adjacency.shape
    own_rows, feat = features.shape
    nc, nr = mesh.shape["col"], mesh.shape["row"]
    n_out = nc // 2
    own_blocks = own_rows // tile
    col_blocks = nc * own_blocks
    per_row = slot_width // tile
    slots = blocks * per_row
    scale = 1.0 / math.sqrt(own_rows * nc * nr)
    cut = feat // nc
    rows = blocks * tile // nr
    groups = half_groups(slots, col_blocks)
    table_rows = -(-2 * GROUP * groups // 128) + -(-2 * groups // 128) + 1
    table_rows = -(-table_rows // 8) * 8

    vmem = pl.BlockSpec(memory_space=pltpu.VMEM)
    hbm = pl.BlockSpec(memory_space=pltpu.HBM)
    dma = pltpu.SemaphoreType.DMA
    tile_flops = 2 * blocks * tile * slot_width * feat
    fg, act, wb = pl.pallas_call(
        functools.partial(layer_kernel, nc, nr, scale),
        out_shape=(
            pltpu.VMEM((own_rows, feat), BF16),
            pltpu.VMEM((rows, feat), BF16),
            pltpu.VMEM((feat + 8, feat), F32),
        ),
        in_specs=[hbm] * 7,
        out_specs=(vmem, vmem, vmem),
        scratch_shapes=[
            pltpu.SMEM((per_row, blocks), jnp.int32),
            pltpu.SMEM((1, blocks), jnp.int32),
            pltpu.SMEM((table_rows, 128), jnp.int32),
            pltpu.VMEM((per_row, blocks), jnp.int32),
            pltpu.VMEM((1, blocks), jnp.int32),
            pltpu.VMEM((table_rows, 128), jnp.int32),
            pltpu.VMEM((col_blocks + 1, tile, feat), BF16),
            pltpu.VMEM(adjacency.shape, BF16),
            pltpu.VMEM((feat, feat), BF16),
            pltpu.VMEM((1, feat), F32),
            pltpu.VMEM((rows, feat), BF16),
            pltpu.VMEM((nr, rows, feat), F32),
            pltpu.VMEM((3, rows, feat), BF16),
            pltpu.VMEM((3, rows, feat), BF16),
            pltpu.VMEM((rows, feat), BF16),
            pltpu.VMEM((rows, feat), BF16),
            pltpu.VMEM((rows, feat), BF16),
            pltpu.VMEM((1, feat), F32),
            pltpu.VMEM((nr, rows, feat), BF16),
            pltpu.VMEM((slots + 1, tile, feat), F32),
            pltpu.VMEM((2 * groups + 1, tile, feat), F32),
            pltpu.VMEM((2, n_out, own_rows // 2, feat), BF16),
            pltpu.VMEM((2, n_out, own_rows // 2, feat), BF16),
            pltpu.VMEM((2, n_out - 1, own_rows // 2, feat), BF16),
            pltpu.VMEM((2, n_out - 1, own_rows // 2, feat), BF16),
            pltpu.VMEM((2, own_rows // 2, feat), F32),
            pltpu.VMEM((nc, cut + 8, feat), F32),
            pltpu.VMEM((nc - 1, cut + 8, feat), F32),
            pltpu.VMEM((nr, cut + 8, feat), F32),
            pltpu.VMEM((nc, cut + 8, feat), F32),
            dma((9,)), dma((nr,)), dma((22,)), dma((nc, 2)),
            dma((3, 4)), dma((3, 4)), dma((2, 4)), dma((4,)),
            dma((2, nr, 4)), dma((nr, 4)),
            dma((2, n_out)), dma((2, n_out)), dma((2, n_out - 1)), dma((2, n_out - 1)),
            dma((nc - 1,)), dma((nc - 1,)), dma((nr - 1,)), dma((nr - 1,)), dma((nc - 1,)), dma((nc - 1,)),
        ],
        compiler_params=pltpu.CompilerParams(
            collective_id=0, has_side_effects=True, vmem_limit_bytes=56 * MIB
        ),
        cost_estimate=pl.CostEstimate(
            flops=2 * tile_flops, bytes_accessed=adjacency.size * 2, transcendentals=rows * feat
        ),
    )(
        tile_cols.T, row_counts.T, features.reshape(own_blocks, tile, feat), adjacency, weight,
        bias.reshape(1, -1), out_grad,
    )
    activations, feature_grad, weight_grad, bias_grad = pl.pallas_call(
        finish_kernel,
        out_shape=(
            jax.ShapeDtypeStruct((rows, feat), BF16),
            jax.ShapeDtypeStruct((own_rows, feat), BF16),
            jax.ShapeDtypeStruct((feat, feat), F32),
            jax.ShapeDtypeStruct((1, feat), F32),
        ),
        in_specs=[vmem] * 3,
        out_specs=(hbm,) * 4,
        scratch_shapes=[dma((4,))],
        compiler_params=pltpu.CompilerParams(vmem_limit_bytes=2 * MIB),
    )(fg, act, wb)
    return (activations, feature_grad, weight_grad, bias_grad.reshape(-1))


def solution(mesh):
    small = mesh.shape["row"] == 4 and mesh.shape["col"] == 8
    placed = (
        P(("groups", "row", "col"), None),
        P(("groups", "col"), None, "row"),
        P(("groups", "col"), "row"),
        P(("groups", "col"), "row"),
        P(),
        P(),
        P(("groups", "col", "row"), None),
    )
    return jax.shard_map(
        functools.partial(whole_layer if small else on_device, mesh),
        mesh=mesh,
        in_specs=placed,
        out_specs=(
            P(("groups", "col", "row"), None),
            P(("groups", "row", "col"), None),
            P("groups", None),
            P("groups"),
        ),
        check_vma=False,
    )
```

```python
import functools
import math

import jax
import jax.numpy as jnp
from jax import lax
from jax.experimental import pallas as pl
from jax.experimental.pallas import tpu as pltpu
from jax.sharding import PartitionSpec as P

MESH = pl.DeviceIdType.MESH
F32, BF16 = jnp.float32, jnp.bfloat16
MIB = 1024 * 1024


def col_peers(nc):
    c = lax.axis_index("col")
    outer, core, n_out = c // 2, c % 2, nc // 2
    partner = outer * 2 + (1 - core)
    ahead = [lax.rem(outer + d, n_out) * 2 + core for d in range(n_out)]
    behind = [lax.rem(outer - d + n_out, n_out) * 2 + core for d in range(n_out)]
    return c, partner, ahead, behind


def send(src, dst, send_sem, recv_sem, where):
    return pltpu.make_async_remote_copy(
        src_ref=src, dst_ref=dst, send_sem=send_sem, recv_sem=recv_sem,
        device_id=where, device_id_type=MESH,
    )


def enter(nc, nr):
    c, r = lax.axis_index("col"), lax.axis_index("row")
    barrier = pltpu.get_barrier_semaphore()
    for d in range(1, nc):
        pl.semaphore_signal(barrier, inc=1, device_id={"col": lax.rem(c + d, nc)}, device_id_type=MESH)
    for e in range(1, nr):
        pl.semaphore_signal(barrier, inc=1, device_id={"row": lax.rem(r + e, nr)}, device_id_type=MESH)
    pl.semaphore_wait(barrier, nc - 1 + nr - 1)


def forward_kernel(
    nc, nr, scale, cols_ref, counts_ref, feat_hbm, adj_hbm, weight_hbm, bias_hbm, og_hbm,
    grads_ref, wb_ref,
    xg, adj, weight_ref, bias_ref, og_ref, own, part, rbuf, gg, w_out, w_in, w_all,
    in_sem, a_sem, f_send, f_recv, p_send, p_recv, r_send, r_recv, g_send, g_recv, w_send, w_recv, wa_send, wa_recv,
):
    blocks, tile, slot_width = adj.shape
    per_row = slot_width // tile
    chunk = blocks // nr
    rows = chunk * tile
    n_out = nc // 2
    own_blocks = feat_hbm.shape[0]
    c, partner, ahead, behind = col_peers(nc)
    r = lax.axis_index("row")
    row_at = [lax.rem(r + e, nr) for e in range(nr)]

    mine = xg.at[pl.ds(c * own_blocks, own_blocks)]
    first = pltpu.make_async_copy(feat_hbm, mine, in_sem.at[0])
    first.start()
    loads = []
    for e in range(nr):
        t = row_at[(e + 1) % nr]
        cut = pl.ds(t * chunk, chunk)
        load = pltpu.make_async_copy(adj_hbm.at[cut], adj.at[cut], a_sem.at[e])
        load.start()
        loads.append(load)
    small = []
    for n, (src, dst) in enumerate(((weight_hbm, weight_ref), (bias_hbm, bias_ref), (og_hbm, og_ref))):
        load = pltpu.make_async_copy(src, dst, in_sem.at[n + 1])
        load.start()
        small.append(load)

    def blocks_of(col):
        return xg.at[pl.ds(col * own_blocks, own_blocks)]

    xg[nc * own_blocks] = jnp.zeros(xg.shape[1:], xg.dtype)
    first.wait()
    enter(nc, nr)

    copies = []
    for d in range(1, n_out):
        copy = send(blocks_of(c), blocks_of(c), f_send.at[d], f_recv.at[d], {"col": ahead[d]})
        copy.start()
        copies.append(copy)
    pair = []
    copy = send(blocks_of(c), blocks_of(c), p_send.at[0], p_recv.at[0], {"col": partner})
    copy.start()
    pair.append(copy)
    for d in range(1, n_out):
        copies[d - 1].wait_recv()
        came = blocks_of(behind[d])
        copy = send(came, came, p_send.at[d], p_recv.at[d], {"col": partner})
        copy.start()
        pair.append(copy)
    for copy in pair:
        copy.wait_recv()
    for copy in copies + pair:
        copy.wait_send()

    pace = math.gcd(chunk, 4)
    row_copies = []
    for e in range(nr):
        far = (e + 1) % nr
        t = row_at[far]
        loads[e].wait()

        def block_rows(n, carry, t=t, far=far):
            for i in range(pace):
                i = n * pace + i
                b = t * chunk + i
                count = counts_ref[0, b]
                picked = [
                    xg[jnp.where(s < count, cols_ref[s, b], nc * own_blocks)] for s in range(per_row)
                ]
                got = jnp.dot(adj[b], jnp.concatenate(picked, axis=0), preferred_element_type=F32)
                cut = pl.ds(pl.multiple_of(i * tile, tile), tile)
                if far:
                    part[far - 1, cut, :] = got.astype(BF16)
                else:
                    own[cut, :] = got
            return carry

        lax.fori_loop(0, chunk // pace, block_rows, 0)
        if far:
            copy = send(
                part.at[far - 1], rbuf.at[far - 1], r_send.at[far - 1], r_recv.at[far - 1], {"row": t}
            )
            copy.start()
            row_copies.append(copy)
    summed = own[...]
    for copy in row_copies:
        copy.wait_recv()
    for e in range(nr - 1):
        summed = summed + rbuf[e].astype(F32)
    hidden = summed.astype(BF16)
    for load in small:
        load.wait()
    preact = jnp.dot(hidden, weight_ref[...], preferred_element_type=F32) + bias_ref[...]
    sig = jax.nn.sigmoid(preact)
    pre_grad = og_ref[...].astype(F32) * (sig * (1.0 + preact * (1.0 - sig)))
    half = pre_grad.astype(BF16)
    dest = lax.dot_general(
        half, weight_ref[...], (((1,), (1,)), ((), ())), preferred_element_type=F32
    )
    gg[r] = dest.astype(BF16)

    def hop(t, step):
        way = 0 if step > 0 else 1
        return send(gg.at[t], gg.at[t], g_send.at[way, t], g_recv.at[t], {"row": r + step})

    for step in (1, -1):
        @pl.when((r + step >= 0) & (r + step < nr))
        def start_chain(step=step):
            hop(r, step).start()
    grads_ref[pl.ds(nr * rows, rows), :] = (preact * sig).astype(BF16)
    feat = hidden.shape[1]
    cut = feat // nc
    w_out[:, pl.ds(0, cut), :] = scale * lax.dot_general(
        hidden, half, (((0,), (0,)), ((), ())), preferred_element_type=F32
    ).reshape(nc, cut, feat)
    w_out[:, pl.ds(cut, 8), :] = jnp.broadcast_to(
        scale * jnp.sum(pre_grad, axis=0, keepdims=True), (nc, 8, feat)
    )
    w_copies = []
    for d in range(1, nc):
        there = lax.rem(c + d, nc)
        copy = send(w_out.at[there], w_in.at[d - 1], w_send.at[d - 1], w_recv.at[d - 1], {"col": there})
        copy.start()
        w_copies.append(copy)
    for k in range(1, nr):
        if k == min(2, nr - 1):
            total = w_out[c]
            for d in range(1, nc):
                w_copies[d - 1].wait_recv()
                total = total + w_in[d - 1]
            w_all[c] = total
            for d in range(1, nc):
                there = lax.rem(c + d, nc)
                copy = send(w_all.at[c], w_all.at[c], wa_send.at[d - 1], wa_recv.at[d - 1], {"col": there})
                copy.start()
                w_copies.append(copy)
        for step in (1, -1):
            t = r - k * step
            came = (t >= 0) & (t < nr)

            @pl.when(came)
            def arrive(t=t, step=step):
                hop(t, step).wait_recv()

            @pl.when(came & (r + step >= 0) & (r + step < nr))
            def pass_on(t=t, step=step):
                hop(t, step).start()
    for k in range(nr):
        for step in (1, -1):
            t = r - k * step

            @pl.when((t >= 0) & (t < nr) & (r + step >= 0) & (r + step < nr))
            def sent(t=t, step=step):
                hop(t, step).wait_send()
    for copy in w_copies[nc - 1 :]:
        copy.wait_recv()
    for n in range(nc):
        wb_ref[pl.ds(n * cut, cut), :] = w_all[n, pl.ds(0, cut), :]
    wb_ref[pl.ds(feat, 8), :] = w_all[0, pl.ds(cut, 8), :]
    grads_ref[pl.ds(0, nr * rows), :] = gg[...].reshape(nr * rows, feat)
    for copy in row_copies + w_copies:
        copy.wait_send()


def backward_kernel(cols_ref, counts_ref, adj_ref, grad_ref, out_ref, act_out, sem, *accs):
    blocks, tile, slot_width = adj_ref.shape
    per_row = slot_width // tile
    dead = out_ref.shape[0]
    hand_out = pltpu.make_async_copy(grad_ref.at[pl.ds(blocks * tile, act_out.shape[0])], act_out, sem)
    hand_out.start()
    for acc in accs:
        acc[...] = jnp.zeros_like(acc)

    pace = math.gcd(blocks, 4)

    def block_rows(n, carry):
        contribs = []
        for i in range(pace):
            b = n * pace + i
            contribs.append(lax.dot_general(
                adj_ref[b], grad_ref[pl.ds(pl.multiple_of(b * tile, tile), tile), :],
                (((0,), (0,)), ((), ())), preferred_element_type=F32,
            ))
        for s in range(per_row):
            for i in range(pace):
                b = n * pace + i
                acc = accs[i]
                j = jnp.where(s < counts_ref[0, b], cols_ref[s, b], dead)
                acc[j] = acc[j] + contribs[i][s * tile : (s + 1) * tile]
        return carry

    lax.fori_loop(0, blocks // pace, block_rows, 0)
    total = accs[0][pl.ds(0, dead)]
    for acc in accs[1:]:
        total = total + acc[pl.ds(0, dead)]
    out_ref[...] = total.astype(BF16)
    hand_out.wait()


def scatter_kernel(
    nc, nr, part_ref, wb_ref, out_ref, wg_ref, bg_ref,
    from_pair, send_buf, from_chip, w_row,
    p_send, p_recv, s_send, s_recv, wr_send, wr_recv,
):
    n_out = nc // 2
    c, partner, ahead, behind = col_peers(nc)
    r = lax.axis_index("row")
    row_at = [lax.rem(r + e, nr) for e in range(nr)]
    partner_ahead = [x + partner - c for x in ahead]
    enter(nc, nr)

    started = []

    def go(*args):
        copy = send(*args)
        copy.start()
        started.append(copy)
        return copy

    order = list(range(1, n_out)) + [0]
    pair = {}
    for d in order:
        pair[d] = go(part_ref.at[partner_ahead[d]], from_pair.at[d], p_send.at[d], p_recv.at[d], {"col": partner})
    w_row[r] = wb_ref[...]
    w_copies = [
        go(w_row.at[r], w_row.at[r], wr_send.at[e - 1], wr_recv.at[e - 1], {"row": row_at[e]})
        for e in range(1, nr)
    ]
    copies = []
    for d in order:
        pair[d].wait_recv()
        both = part_ref[ahead[d]].astype(F32) + from_pair[d].astype(F32)
        if d:
            send_buf[d - 1] = both.astype(BF16)
            copies.append(go(
                send_buf.at[d - 1], from_chip.at[d - 1], s_send.at[d - 1], s_recv.at[d - 1], {"col": ahead[d]}
            ))
    for copy in copies:
        copy.wait_recv()
    for d in range(1, n_out):
        both = both + from_chip[d - 1].astype(F32)
    out_ref[...] = both.astype(BF16)
    for copy in w_copies:
        copy.wait_recv()
    total = w_row[0]
    for n in range(1, nr):
        total = total + w_row[n]
    feat = wg_ref.shape[0]
    wg_ref[...] = total[:feat]
    bg_ref[...] = total[feat : feat + 1]
    for copy in started:
        copy.wait_send()


def on_device(mesh, features, adjacency, tile_cols, row_counts, weight, bias, out_grad):
    blocks, tile, slot_width = adjacency.shape
    own_rows, feat = features.shape
    nc, nr = mesh.shape["col"], mesh.shape["row"]
    n_out = nc // 2
    col_blocks = nc * own_rows // tile
    scale = 1.0 / math.sqrt(own_rows * nc * nr)
    cut = feat // nc

    vmem = pl.BlockSpec(memory_space=pltpu.VMEM)
    smem = pl.BlockSpec(memory_space=pltpu.SMEM)
    hbm = pl.BlockSpec(memory_space=pltpu.HBM)
    dma = pltpu.SemaphoreType.DMA
    rows = blocks * tile // nr
    tile_flops = 2 * blocks * tile * slot_width * feat
    grads, wb = pl.pallas_call(
        functools.partial(forward_kernel, nc, nr, scale),
        out_shape=(
            jax.ShapeDtypeStruct((blocks * tile + rows, feat), BF16),
            jax.ShapeDtypeStruct((feat + 8, feat), F32),
        ),
        in_specs=[smem, smem, hbm, hbm, hbm, hbm, hbm],
        out_specs=(vmem, vmem),
        scratch_shapes=[
            pltpu.VMEM((col_blocks + 1, tile, feat), BF16),
            pltpu.VMEM(adjacency.shape, BF16),
            pltpu.VMEM((feat, feat), BF16),
            pltpu.VMEM((1, feat), F32),
            pltpu.VMEM((rows, feat), BF16),
            pltpu.VMEM((rows, feat), F32),
            pltpu.VMEM((nr - 1, rows, feat), BF16),
            pltpu.VMEM((nr - 1, rows, feat), BF16),
            pltpu.VMEM((nr, rows, feat), BF16),
            pltpu.VMEM((nc, cut + 8, feat), F32),
            pltpu.VMEM((nc - 1, cut + 8, feat), F32),
            pltpu.VMEM((nc, cut + 8, feat), F32),
            dma((4,)), dma((nr,)), dma((n_out,)), dma((n_out,)), dma((n_out,)), dma((n_out,)),
            dma((nr - 1,)), dma((nr - 1,)), dma((2, nr)), dma((nr,)),
            dma((nc - 1,)), dma((nc - 1,)), dma((nc - 1,)), dma((nc - 1,)),
        ],
        compiler_params=pltpu.CompilerParams(
            collective_id=0, has_side_effects=True, vmem_limit_bytes=56 * MIB
        ),
        cost_estimate=pl.CostEstimate(
            flops=tile_flops, bytes_accessed=adjacency.size * 2, transcendentals=rows * feat
        ),
    )(
        tile_cols.T, row_counts.T, features.reshape(own_rows // tile, tile, feat), adjacency, weight,
        bias.reshape(1, -1), out_grad,
    )

    partial, activations = pl.pallas_call(
        backward_kernel,
        out_shape=(
            jax.ShapeDtypeStruct((col_blocks, tile, feat), BF16),
            jax.ShapeDtypeStruct((rows, feat), BF16),
        ),
        in_specs=[smem, smem, vmem, vmem],
        out_specs=(vmem, hbm),
        scratch_shapes=[dma] + [pltpu.VMEM((col_blocks + 1, tile, feat), F32) for unused in range(4)],
        compiler_params=pltpu.CompilerParams(vmem_limit_bytes=32 * MIB),
        cost_estimate=pl.CostEstimate(
            flops=tile_flops * 8, bytes_accessed=adjacency.size * 2, transcendentals=0
        ),
    )(tile_cols.T, row_counts.T, adjacency, grads)

    feature_grad, weight_grad, bias_grad = pl.pallas_call(
        functools.partial(scatter_kernel, nc, nr),
        out_shape=(
            jax.ShapeDtypeStruct((own_rows, feat), BF16),
            jax.ShapeDtypeStruct((feat, feat), F32),
            jax.ShapeDtypeStruct((1, feat), F32),
        ),
        in_specs=[vmem, vmem],
        out_specs=(vmem, vmem, vmem),
        scratch_shapes=[
            pltpu.VMEM((n_out, own_rows, feat), BF16),
            pltpu.VMEM((n_out - 1, own_rows, feat), BF16),
            pltpu.VMEM((n_out - 1, own_rows, feat), BF16),
            pltpu.VMEM((nr, feat + 8, feat), F32),
            dma((n_out,)), dma((n_out,)), dma((n_out - 1,)), dma((n_out - 1,)),
            dma((nr - 1,)), dma((nr - 1,)),
        ],
        compiler_params=pltpu.CompilerParams(
            collective_id=1, has_side_effects=True, vmem_limit_bytes=20 * MIB
        ),
        cost_estimate=pl.CostEstimate(
            flops=own_rows * nc * feat, bytes_accessed=8 * own_rows * nc * feat, transcendentals=0
        ),
    )(partial.reshape(nc, own_rows, feat), wb)
    return (activations, feature_grad, weight_grad, bias_grad.reshape(-1))


GROUP = 4


def slot_tables(cols_ref, counts_ref, col_blocks, mine, tab_ref):
    per_row, blocks = cols_ref.shape
    slots = per_row * blocks
    groups = half_groups(slots, col_blocks)
    keys = 2 * col_blocks

    def iota(shape, axis):
        return lax.broadcasted_iota(jnp.int32, shape, axis)

    def upright(row):
        n = row.shape[1]
        return jnp.sum(jnp.where(iota((n, n), 0) == iota((n, n), 1), row, 0), axis=1, keepdims=True)

    lane = iota((blocks, keys), 1)
    block = iota((blocks, 1), 0)
    late = jnp.where((block >= mine) & (block < mine + blocks // 2), 0, col_blocks)
    counts = upright(counts_ref[...])
    seen = jnp.zeros((blocks, keys), jnp.int32)
    hits, ranks = [], []
    for s in range(per_row):
        hit = jnp.where((upright(cols_ref[pl.ds(s, 1), :]) + late == lane) & (counts > s), 1, 0)
        hits.append(hit)
        ranks.append(seen)
        seen = seen + hit
    earlier = jnp.zeros((blocks, keys), jnp.int32)
    for b in range(blocks - 1):
        earlier = earlier + jnp.where(block > b, seen[b : b + 1, :], 0)
    sizes = lax.shift_right_logical(jnp.sum(seen, axis=0, keepdims=True) + (GROUP - 1), 2)
    square = (keys, keys)
    first, second = iota(square, 0), iota(square, 1)
    lower = (first < second) & ((first < col_blocks) == (second < col_blocks))
    starts = jnp.sum(jnp.where(lower, upright(sizes), 0), axis=0, keepdims=True)
    starts = starts + jnp.where(iota((1, keys), 1) < col_blocks, 0, groups)
    places = -(-2 * GROUP * groups // 128) * 128
    heads = -(-2 * groups // 128) * 128
    place = iota((blocks, places), 1)
    head = iota((blocks, heads), 1) * GROUP
    found = jnp.zeros((blocks, places), jnp.int32)
    fresh = jnp.zeros((blocks, heads), jnp.int32)
    for s in range(per_row):
        rank = jnp.sum(hits[s] * (ranks[s] + earlier), axis=1, keepdims=True)
        at = jnp.sum(hits[s] * (GROUP * starts), axis=1, keepdims=True) + rank
        at = jnp.where(counts > s, at, -1)
        found = found + jnp.where(at == place, slots - (block * per_row + s), 0)
        fresh = fresh + jnp.where((at == head) & (rank == 0), 1, 0)
    found = slots - jnp.sum(found, axis=0, keepdims=True)
    fresh = jnp.sum(fresh, axis=0, keepdims=True)
    last = jnp.where(sizes > 0, starts + sizes - 1, 2 * groups)
    n = 0
    for value in (found, fresh):
        for k in range(value.shape[1] // 128):
            tab_ref[pl.ds(n, 1), :] = value[:, k * 128 : (k + 1) * 128]
            n += 1
    tab_ref[pl.ds(n, 1), pl.ds(0, keys)] = last


def square_peers():
    c = lax.axis_index("col")
    y, x, core = c // 4, c // 2 % 2, c % 2

    def at(dy, dx):
        return (y + dy) % 2 * 4 + (x + dx) % 2 * 2 + core

    return c, c + 1 - 2 * core, [c, at(1, 1), at(0, 1), at(1, 0)]


def half_groups(slots, col_blocks):
    most = (slots // 2 + (GROUP - 1) * min(col_blocks, slots // 2)) // GROUP
    return -(-most // 8) * 8


def layer_kernel(
    nc, nr, scale, cols_hbm, counts_hbm, feat_hbm, adj_hbm, weight_hbm, bias_hbm, og_hbm,
    fg_ref, act_ref, wb_ref,
    cols_s, counts_s, tab_s, cols_v, counts_v, tab_v,
    xg, adj, weight_ref, bias_ref, og_ref, pf, part, near, far, hid, half, bias_sum, gg,
    contrib, runs, pair_out, pair_in, chip_out, chip_in, kept,
    w_out, w_in, w_row, w_all,
    in_sem, a_sem, f_send, f_recv, n_send, n_recv, r_send, r_recv,
    g_send, g_recv, gp_send, gp_recv, gc_send, gc_recv,
    w_send, w_recv, wr_send, wr_recv, wa_send, wa_recv,
):
    blocks, tile, slot_width = adj.shape
    per_row = slot_width // tile
    slots = blocks * per_row
    chunk = blocks // nr
    rows = chunk * tile
    n_out = nc // 2
    own_blocks = feat_hbm.shape[0]
    col_blocks = nc * own_blocks
    feat = weight_ref.shape[0]
    groups = half_groups(slots, col_blocks)
    cuts = 4
    fresh_at = -(-2 * GROUP * groups // 128)
    last_at = fresh_at + -(-2 * groups // 128)
    step = rows // cuts
    c, partner, ahead = square_peers()
    r = lax.axis_index("row")

    barrier = pltpu.get_barrier_semaphore()
    for d in range(1, nc):
        pl.semaphore_signal(barrier, inc=1, device_id={"col": lax.rem(c + d, nc)}, device_id_type=MESH)
    for e in range(1, nr):
        pl.semaphore_signal(barrier, inc=1, device_id={"row": lax.rem(r + e, nr)}, device_id_type=MESH)

    half_blocks = own_blocks // 2
    odd, even = c % 2 == 1, c % 2 == 0
    chip_x, chip_y, chip_d = [ahead[n] - c % 2 for n in (2, 3, 1)]

    def feat_part(col, h):
        return xg.at[pl.ds(col * own_blocks + h * half_blocks, half_blocks)]

    def give(slot, src, col, h, there):
        return send(src, feat_part(col, h), f_send.at[slot], f_recv.at[col, h], {"col": there})

    first = []
    for h in range(2):
        mine = feat_hbm.at[pl.ds(h * half_blocks, half_blocks)]
        first.append((h, give(h, mine, c, h, chip_x + 1)))
        first.append((1 - h, give(2 + h, mine, c, h, chip_y + 1)))
        first.append((2 + h, give(4 + h, mine, c, h, partner)))
    first = [copy for unused, copy in sorted(first, key=lambda pair: pair[0])]

    relays, keeps, last_ones = [], [], []
    for k in (1, 0):
        relays.append((chip_x + k, 0, chip_y + 1))
        relays.append((chip_y + k, 1, chip_x + 1))
        keeps += [(chip_x + k, 1), (chip_y + k, 0)]
        last_ones += [(chip_d + k, 0), (chip_d + k, 1)]
    inside = [(col, h) for col, h, unused in relays] + keeps + last_ones
    relays = [give(6 + n, feat_part(col, h), col, h, there) for n, (col, h, there) in enumerate(relays)]
    inside = [give(10 + n, feat_part(col, h), col, h, partner) for n, (col, h) in enumerate(inside)]

    pl.semaphore_wait(barrier, nc - 1 + nr - 1)
    for copy in first:
        copy.start()

    loads = {}
    for n, (name, src, dst) in enumerate((
        ("cols_v", cols_hbm, cols_v), ("counts_v", counts_hbm, counts_v),
        ("feat", feat_hbm, xg.at[pl.ds(c * own_blocks, own_blocks)]), ("cols_s", cols_hbm, cols_s),
        ("counts_s", counts_hbm, counts_s),
        ("weight", weight_hbm, weight_ref), ("bias", bias_hbm, bias_ref), ("og", og_hbm, og_ref),
    )):
        loads[name] = pltpu.make_async_copy(src, dst, in_sem.at[n])
        loads[name].start()

    mirrored = r >= 2
    inner = (r == 1) | (r == 2)
    outer = (r == 0) | (r == 3)

    def place(d):
        return jnp.where(mirrored, 3 - d, d)

    mate = jnp.where(r % 2 == 0, r + 1, r - 1)
    targets = [place(3), place(2), mate, r]
    for e in range(nr):
        cut = pl.ds(targets[e] * chunk, chunk)
        load = pltpu.make_async_copy(adj_hbm.at[cut], adj.at[cut], a_sem.at[e])
        load.start()
        loads[e] = load

    xg[col_blocks] = jnp.zeros(xg.shape[1:], xg.dtype)
    contrib[slots] = jnp.zeros(contrib.shape[1:], F32)
    runs[2 * groups] = jnp.zeros(runs.shape[1:], F32)

    @pl.when(odd)
    def relay():
        for n in range(4):
            inside[n].wait_recv()
            relays[n].start()
            inside[n].start()

    loads["cols_v"].wait()
    loads["counts_v"].wait()
    slot_tables(cols_v, counts_v, col_blocks, r // 2 * (blocks // 2), tab_v)
    table = pltpu.make_async_copy(tab_v, tab_s, in_sem.at[8])
    table.start()

    @pl.when(odd)
    def pass_inside():
        for n in range(4, 12):
            inside[n].wait_recv()
            inside[n].start()

    @pl.when(even)
    def take_inside():
        for n in range(12):
            inside[n].wait_recv()

    for name in ("feat", "cols_s", "counts_s"):
        loads[name].wait()
    table.wait()
    for h in range(2):
        give(4 + h, feat_part(partner, h), partner, h, partner).wait_recv()

    def piece(q):
        return pl.ds(q * step, step)

    def to_near(e, q):
        return send(part.at[e, piece(q)], near.at[e, piece(q)], n_send.at[e, q], n_recv.at[e, q], {"row": mate})

    def to_far(e, q):
        return send(part.at[e, piece(q)], far.at[piece(q)], r_send.at[e, q], r_recv.at[q], {"row": targets[e]})

    def products(e, q):
        def block_rows(n, carry):
            for i in range(2):
                i = q * (chunk // cuts) + n * 2 + i
                b = targets[e] * chunk + i
                count = counts_s[0, b]
                picked = [xg[jnp.where(s < count, cols_s[s, b], col_blocks)] for s in range(per_row)]
                got = jnp.dot(adj[b], jnp.concatenate(picked, axis=0), preferred_element_type=F32)
                cut = pl.ds(pl.multiple_of(i * tile, tile), tile)
                pf[e, cut, :] = got
                if e < 3:
                    part[e, cut, :] = got.astype(BF16)
            return carry

        lax.fori_loop(0, chunk // cuts // 2, block_rows, 0)

    loads[0].wait()
    loads[1].wait()
    for e in range(2):
        for q in range(cuts):
            products(e, q)

            @pl.when(outer)
            def hand_in(e=e, q=q):
                to_near(e, q).start()
    for e in (2, 3):
        loads[e].wait()
        for q in range(cuts):
            products(e, q)
            if e == 2:
                to_near(e, q).start()
    for e in range(2):
        for q in range(cuts):
            @pl.when(inner)
            def join(e=e, q=q):
                to_near(e, q).wait_recv()
                part[e, piece(q), :] = (pf[e, piece(q), :] + near[e, piece(q), :].astype(F32)).astype(BF16)
                to_far(e, q).start()

    def to_mate(t, q):
        return send(gg.at[t, piece(q)], gg.at[t, piece(q)], g_send.at[0, t, q], g_recv.at[t, q], {"row": mate})

    def to_other(q):
        return send(gg.at[r, piece(q)], gg.at[r, piece(q)], g_send.at[1, r, q], g_recv.at[r, q], {"row": place(2)})

    for name in ("weight", "bias", "og"):
        loads[name].wait()
    bias_part = jnp.zeros((1, feat), F32)
    for q in range(cuts):
        cut = piece(q)
        to_near(2, q).wait_recv()
        to_far(0, q).wait_recv()
        hidden = (pf[3, cut, :] + near[2, cut, :].astype(F32) + far[cut, :].astype(F32)).astype(BF16)
        preact = jnp.dot(hidden, weight_ref[...], preferred_element_type=F32) + bias_ref[...]
        sig = jax.nn.sigmoid(preact)
        pre_grad = og_ref[cut, :].astype(F32) * (sig * (1.0 + preact * (1.0 - sig)))
        small = pre_grad.astype(BF16)
        dest = lax.dot_general(small, weight_ref[...], (((1,), (1,)), ((), ())), preferred_element_type=F32)
        gg[r, cut, :] = dest.astype(BF16)
        to_mate(r, q).start()
        to_other(q).start()
        act_ref[cut, :] = (preact * sig).astype(BF16)
        hid[cut, :] = hidden
        half[cut, :] = small
        bias_part = bias_part + jnp.sum(pre_grad, axis=0, keepdims=True)
    bias_sum[...] = bias_part

    wcut = feat // nc

    def to_col(src, dst, sems, d):
        return send(src, dst, sems[0].at[d - 1], sems[1].at[d - 1], {"col": lax.rem(c + d, nc)})

    def w_first(d):
        return to_col(w_out.at[lax.rem(c + d, nc)], w_in.at[d - 1], (w_send, w_recv), d)

    def w_second(e):
        return send(w_row.at[r], w_row.at[r], wr_send.at[e - 1], wr_recv.at[e - 1], {"row": lax.rem(r + e, nr)})

    def w_third(d):
        return to_col(w_all.at[c], w_all.at[c], (wa_send, wa_recv), d)

    def weight_terms():
        w_out[:, pl.ds(0, wcut), :] = scale * lax.dot_general(
            hid[...], half[...], (((0,), (0,)), ((), ())), preferred_element_type=F32
        ).reshape(nc, wcut, feat)
        w_out[:, pl.ds(wcut, 8), :] = jnp.broadcast_to(scale * bias_sum[...], (nc, 8, feat))
        for d in range(1, nc):
            w_first(d).start()

    def weight_rows():
        total = w_out[c]
        for d in range(1, nc):
            w_first(d).wait_recv()
            total = total + w_in[d - 1]
        w_row[r] = total
        for e in range(1, nr):
            w_second(e).start()

    def weight_whole():
        for e in range(1, nr):
            w_second(e).wait_recv()
        total = w_row[0]
        for n in range(1, nr):
            total = total + w_row[n]
        w_all[c] = total
        for d in range(1, nc):
            w_third(d).start()

    def contribute(t, q):
        def pairs(n, carry):
            b = t * chunk + q * (chunk // cuts) + n * 2
            lhs = adj[pl.ds(b, 2)].reshape(2 * tile, slot_width)
            g = gg[t, pl.ds(pl.multiple_of(q * step + n * 2 * tile, 2 * tile), 2 * tile), :]
            upper = lax.broadcasted_iota(jnp.int32, g.shape, 0) < tile
            zero = jnp.zeros_like(g)
            rhs = jnp.concatenate([jnp.where(upper, g, zero), jnp.where(upper, zero, g)], axis=1)
            got = lax.dot_general(lhs, rhs, (((0,), (0,)), ((), ())), preferred_element_type=F32)
            contrib[pl.ds(b * per_row, per_row)] = got[:, :feat].reshape(per_row, tile, feat)
            contrib[pl.ds(b * per_row + per_row, per_row)] = got[:, feat:].reshape(per_row, tile, feat)
            return carry

        lax.fori_loop(0, chunk // cuts // 2, pairs, 0)

    def gather(part_of, low=0, high=tile):
        span = pl.ds(low, high - low)

        def add_up(n, acc):
            spot = part_of * GROUP * groups + n * 8 * GROUP
            head = part_of * groups + n * 8
            for u in range(8):
                terms = [contrib[tab_s[spot // 128, spot % 128 + u * GROUP + k], span, :] for k in range(GROUP)]
                new = tab_s[fresh_at + head // 128, head % 128 + u]
                acc = jnp.where(new > 0, 0.0, acc) + ((terms[0] + terms[1]) + (terms[2] + terms[3]))
                runs[head + u, span, :] = acc
            return acc

        lax.fori_loop(0, groups // 8, add_up, jnp.zeros((high - low, feat), F32))

    near_in, far_in = place(2), place(3)
    from_in = [(r, q) for q in range(cuts)]
    from_out = from_in + [(mate, q) for q in range(cuts)]
    passed = []
    for q in range(cuts):
        from_in += [(mate, q), (near_in, q), (far_in, q)]
        from_out += [(near_in, q), (far_in, q)]
        passed += [(near_in, q), (far_in, q)]
    for k in range(4 * cuts):
        if 2 <= k < 2 + len(passed):
            @pl.when(inner)
            def pass_on(t=passed[k - 2][0], q=passed[k - 2][1]):
                to_mate(t, q).wait_recv()
                to_mate(t, q).start()
        if k == 0:
            weight_terms()
        if k == 2 + len(passed):
            pl.when(inner)(weight_rows)
        if k == 2 * cuts:
            @pl.when(outer)
            def early():
                weight_rows()
                gather(0)
        if k >= cuts:
            @pl.when(outer)
            def came(k=k):
                to_mate(*from_out[k]).wait_recv()
        if from_in[k][0] is mate:
            @pl.when(inner)
            def mate_came(k=k):
                to_mate(*from_in[k]).wait_recv()
        contribute(
            jnp.where(inner, from_in[k][0], from_out[k][0]), jnp.where(inner, from_in[k][1], from_out[k][1])
        )

    hrows = tile // 2
    order = list(range(1, n_out)) + [0]

    def to_pair(h, d):
        return send(pair_out.at[h, d], pair_in.at[h, d], gp_send.at[h, d], gp_recv.at[h, d], {"col": partner})

    def to_chip(h, d):
        return send(
            chip_out.at[h, d - 1], chip_in.at[h, d - 1], gc_send.at[h, d - 1], gc_recv.at[h, d - 1], {"col": ahead[d]}
        )

    def totals(col, h):
        lines = [(tab_s[last_at, col * own_blocks + n], tab_s[last_at, col_blocks + col * own_blocks + n])
                 for n in range(own_blocks)]
        cut = pl.ds(h * hrows, hrows)
        return jnp.concatenate([runs[a, cut, :] + runs[b, cut, :] for a, b in lines], axis=0)

    def hand_over(h):
        for d in order:
            pair_out[h, d] = totals(ahead[d] + partner - c, h).astype(BF16)
            to_pair(h, d).start()

    def combine(h):
        for d in order:
            mine = totals(ahead[d], h)
            to_pair(h, d).wait_recv()
            both = mine + pair_in[h, d].astype(F32)
            if d:
                chip_out[h, d - 1] = both.astype(BF16)
                to_chip(h, d).start()
            else:
                kept[h] = both

    @pl.when(inner)
    def late():
        gather(0)

    gather(1)
    hand_over(0)
    weight_whole()
    combine(0)
    hand_over(1)
    combine(1)
    for copy in first:
        copy.wait_send()

    @pl.when(odd)
    def odd_sent():
        for copy in relays + inside:
            copy.wait_send()

    for d in range(1, nc):
        w_first(d).wait_send()
    for e in range(1, nr):
        w_second(e).wait_send()
    for q in range(cuts):
        to_near(2, q).wait_send()
        to_other(q).wait_send()
        to_mate(r, q).wait_send()

    @pl.when(outer)
    def outer_sent():
        for e in range(2):
            for q in range(cuts):
                to_near(e, q).wait_send()

    @pl.when(inner)
    def inner_sent():
        for e in range(2):
            for q in range(cuts):
                to_far(e, q).wait_send()
                to_mate(targets[e], q).wait_send()

    for h in range(2):
        for d in range(n_out):
            to_pair(h, d).wait_send()
    for d in range(1, nc):
        w_third(d).wait_recv()
    for n in range(nc):
        wb_ref[pl.ds(n * wcut, wcut), :] = w_all[n, pl.ds(0, wcut), :]
    wb_ref[pl.ds(feat, 8), :] = w_all[0, pl.ds(wcut, 8), :]
    for h in range(2):
        for d in range(1, n_out):
            to_chip(h, d).wait_recv()
        both = kept[h]
        for d in range(1, n_out):
            both = both + chip_in[h, d - 1].astype(F32)
        both = both.astype(BF16)
        for n in range(own_blocks):
            fg_ref[pl.ds(n * tile + h * hrows, hrows), :] = both[n * hrows : (n + 1) * hrows]
    for h in range(2):
        for d in range(1, n_out):
            to_chip(h, d).wait_send()
    for d in range(1, nc):
        w_third(d).wait_send()


def finish_kernel(fg_in, act_in, wb_in, act_out, fg_out, wg_out, bg_out, sem):
    feat = wg_out.shape[0]
    copies = []
    for n, (src, dst) in enumerate((
        (fg_in, fg_out), (act_in, act_out), (wb_in.at[pl.ds(0, feat)], wg_out), (wb_in.at[pl.ds(feat, 1)], bg_out),
    )):
        copy = pltpu.make_async_copy(src, dst, sem.at[n])
        copy.start()
        copies.append(copy)
    for copy in copies:
        copy.wait()


def whole_layer(mesh, features, adjacency, tile_cols, row_counts, weight, bias, out_grad):
    blocks, tile, slot_width = adjacency.shape
    own_rows, feat = features.shape
    nc, nr = mesh.shape["col"], mesh.shape["row"]
    n_out = nc // 2
    own_blocks = own_rows // tile
    col_blocks = nc * own_blocks
    per_row = slot_width // tile
    slots = blocks * per_row
    scale = 1.0 / math.sqrt(own_rows * nc * nr)
    cut = feat // nc
    rows = blocks * tile // nr
    groups = half_groups(slots, col_blocks)
    table_rows = -(-2 * GROUP * groups // 128) + -(-2 * groups // 128) + 1
    table_rows = -(-table_rows // 8) * 8

    vmem = pl.BlockSpec(memory_space=pltpu.VMEM)
    hbm = pl.BlockSpec(memory_space=pltpu.HBM)
    dma = pltpu.SemaphoreType.DMA
    tile_flops = 2 * blocks * tile * slot_width * feat
    fg, act, wb = pl.pallas_call(
        functools.partial(layer_kernel, nc, nr, scale),
        out_shape=(
            pltpu.VMEM((own_rows, feat), BF16),
            pltpu.VMEM((rows, feat), BF16),
            pltpu.VMEM((feat + 8, feat), F32),
        ),
        in_specs=[hbm] * 7,
        out_specs=(vmem, vmem, vmem),
        scratch_shapes=[
            pltpu.SMEM((per_row, blocks), jnp.int32),
            pltpu.SMEM((1, blocks), jnp.int32),
            pltpu.SMEM((table_rows, 128), jnp.int32),
            pltpu.VMEM((per_row, blocks), jnp.int32),
            pltpu.VMEM((1, blocks), jnp.int32),
            pltpu.VMEM((table_rows, 128), jnp.int32),
            pltpu.VMEM((col_blocks + 1, tile, feat), BF16),
            pltpu.VMEM(adjacency.shape, BF16),
            pltpu.VMEM((feat, feat), BF16),
            pltpu.VMEM((1, feat), F32),
            pltpu.VMEM((rows, feat), BF16),
            pltpu.VMEM((nr, rows, feat), F32),
            pltpu.VMEM((3, rows, feat), BF16),
            pltpu.VMEM((3, rows, feat), BF16),
            pltpu.VMEM((rows, feat), BF16),
            pltpu.VMEM((rows, feat), BF16),
            pltpu.VMEM((rows, feat), BF16),
            pltpu.VMEM((1, feat), F32),
            pltpu.VMEM((nr, rows, feat), BF16),
            pltpu.VMEM((slots + 1, tile, feat), F32),
            pltpu.VMEM((2 * groups + 1, tile, feat), F32),
            pltpu.VMEM((2, n_out, own_rows // 2, feat), BF16),
            pltpu.VMEM((2, n_out, own_rows // 2, feat), BF16),
            pltpu.VMEM((2, n_out - 1, own_rows // 2, feat), BF16),
            pltpu.VMEM((2, n_out - 1, own_rows // 2, feat), BF16),
            pltpu.VMEM((2, own_rows // 2, feat), F32),
            pltpu.VMEM((nc, cut + 8, feat), F32),
            pltpu.VMEM((nc - 1, cut + 8, feat), F32),
            pltpu.VMEM((nr, cut + 8, feat), F32),
            pltpu.VMEM((nc, cut + 8, feat), F32),
            dma((9,)), dma((nr,)), dma((22,)), dma((nc, 2)),
            dma((3, 4)), dma((3, 4)), dma((2, 4)), dma((4,)),
            dma((2, nr, 4)), dma((nr, 4)),
            dma((2, n_out)), dma((2, n_out)), dma((2, n_out - 1)), dma((2, n_out - 1)),
            dma((nc - 1,)), dma((nc - 1,)), dma((nr - 1,)), dma((nr - 1,)), dma((nc - 1,)), dma((nc - 1,)),
        ],
        compiler_params=pltpu.CompilerParams(
            collective_id=0, has_side_effects=True, vmem_limit_bytes=56 * MIB
        ),
        cost_estimate=pl.CostEstimate(
            flops=2 * tile_flops, bytes_accessed=adjacency.size * 2, transcendentals=rows * feat
        ),
    )(
        tile_cols.T, row_counts.T, features.reshape(own_blocks, tile, feat), adjacency, weight,
        bias.reshape(1, -1), out_grad,
    )
    activations, feature_grad, weight_grad, bias_grad = pl.pallas_call(
        finish_kernel,
        out_shape=(
            jax.ShapeDtypeStruct((rows, feat), BF16),
            jax.ShapeDtypeStruct((own_rows, feat), BF16),
            jax.ShapeDtypeStruct((feat, feat), F32),
            jax.ShapeDtypeStruct((1, feat), F32),
        ),
        in_specs=[vmem] * 3,
        out_specs=(hbm,) * 4,
        scratch_shapes=[dma((4,))],
        compiler_params=pltpu.CompilerParams(vmem_limit_bytes=2 * MIB),
    )(fg, act, wb)
    return (activations, feature_grad, weight_grad, bias_grad.reshape(-1))


def solution(mesh):
    small = mesh.shape["row"] == 4 and mesh.shape["col"] == 8
    placed = (
        P(("groups", "row", "col"), None),
        P(("groups", "col"), None, "row"),
        P(("groups", "col"), "row"),
        P(("groups", "col"), "row"),
        P(),
        P(),
        P(("groups", "col", "row"), None),
    )
    return jax.shard_map(
        functools.partial(whole_layer if small else on_device, mesh),
        mesh=mesh,
        in_specs=placed,
        out_specs=(
            P(("groups", "col", "row"), None),
            P(("groups", "row", "col"), None),
            P("groups", None),
            P("groups"),
        ),
        check_vma=False,
    )
```

```python
import functools
import math

import jax
import jax.numpy as jnp
from jax import lax
from jax.experimental import pallas as pl
from jax.experimental.pallas import tpu as pltpu
from jax.sharding import PartitionSpec as P

MESH = pl.DeviceIdType.MESH
F32, BF16 = jnp.float32, jnp.bfloat16
MIB = 1024 * 1024


def col_peers(nc):
    c = lax.axis_index("col")
    outer, core, n_out = c // 2, c % 2, nc // 2
    partner = outer * 2 + (1 - core)
    ahead = [lax.rem(outer + d, n_out) * 2 + core for d in range(n_out)]
    behind = [lax.rem(outer - d + n_out, n_out) * 2 + core for d in range(n_out)]
    return c, partner, ahead, behind


def send(src, dst, send_sem, recv_sem, where):
    return pltpu.make_async_remote_copy(
        src_ref=src, dst_ref=dst, send_sem=send_sem, recv_sem=recv_sem,
        device_id=where, device_id_type=MESH,
    )


def enter(nc, nr):
    c, r = lax.axis_index("col"), lax.axis_index("row")
    barrier = pltpu.get_barrier_semaphore()
    for d in range(1, nc):
        pl.semaphore_signal(barrier, inc=1, device_id={"col": lax.rem(c + d, nc)}, device_id_type=MESH)
    for e in range(1, nr):
        pl.semaphore_signal(barrier, inc=1, device_id={"row": lax.rem(r + e, nr)}, device_id_type=MESH)
    pl.semaphore_wait(barrier, nc - 1 + nr - 1)


def forward_kernel(
    nc, nr, scale, cols_ref, counts_ref, feat_hbm, adj_hbm, weight_hbm, bias_hbm, og_hbm,
    grads_ref, wb_ref,
    xg, adj, weight_ref, bias_ref, og_ref, own, part, rbuf, gg, w_out, w_in, w_all,
    in_sem, a_sem, f_send, f_recv, p_send, p_recv, r_send, r_recv, g_send, g_recv, w_send, w_recv, wa_send, wa_recv,
):
    blocks, tile, slot_width = adj.shape
    per_row = slot_width // tile
    chunk = blocks // nr
    rows = chunk * tile
    n_out = nc // 2
    own_blocks = feat_hbm.shape[0]
    c, partner, ahead, behind = col_peers(nc)
    r = lax.axis_index("row")
    row_at = [lax.rem(r + e, nr) for e in range(nr)]

    mine = xg.at[pl.ds(c * own_blocks, own_blocks)]
    first = pltpu.make_async_copy(feat_hbm, mine, in_sem.at[0])
    first.start()
    loads = []
    for e in range(nr):
        t = row_at[(e + 1) % nr]
        cut = pl.ds(t * chunk, chunk)
        load = pltpu.make_async_copy(adj_hbm.at[cut], adj.at[cut], a_sem.at[e])
        load.start()
        loads.append(load)
    small = []
    for n, (src, dst) in enumerate(((weight_hbm, weight_ref), (bias_hbm, bias_ref), (og_hbm, og_ref))):
        load = pltpu.make_async_copy(src, dst, in_sem.at[n + 1])
        load.start()
        small.append(load)

    def blocks_of(col):
        return xg.at[pl.ds(col * own_blocks, own_blocks)]

    xg[nc * own_blocks] = jnp.zeros(xg.shape[1:], xg.dtype)
    first.wait()
    enter(nc, nr)

    copies = []
    for d in range(1, n_out):
        copy = send(blocks_of(c), blocks_of(c), f_send.at[d], f_recv.at[d], {"col": ahead[d]})
        copy.start()
        copies.append(copy)
    pair = []
    copy = send(blocks_of(c), blocks_of(c), p_send.at[0], p_recv.at[0], {"col": partner})
    copy.start()
    pair.append(copy)
    for d in range(1, n_out):
        copies[d - 1].wait_recv()
        came = blocks_of(behind[d])
        copy = send(came, came, p_send.at[d], p_recv.at[d], {"col": partner})
        copy.start()
        pair.append(copy)
    for copy in pair:
        copy.wait_recv()
    for copy in copies + pair:
        copy.wait_send()

    pace = math.gcd(chunk, 4)
    row_copies = []
    for e in range(nr):
        far = (e + 1) % nr
        t = row_at[far]
        loads[e].wait()

        def block_rows(n, carry, t=t, far=far):
            for i in range(pace):
                i = n * pace + i
                b = t * chunk + i
                count = counts_ref[0, b]
                picked = [
                    xg[jnp.where(s < count, cols_ref[s, b], nc * own_blocks)] for s in range(per_row)
                ]
                got = jnp.dot(adj[b], jnp.concatenate(picked, axis=0), preferred_element_type=F32)
                cut = pl.ds(pl.multiple_of(i * tile, tile), tile)
                if far:
                    part[far - 1, cut, :] = got.astype(BF16)
                else:
                    own[cut, :] = got
            return carry

        lax.fori_loop(0, chunk // pace, block_rows, 0)
        if far:
            copy = send(
                part.at[far - 1], rbuf.at[far - 1], r_send.at[far - 1], r_recv.at[far - 1], {"row": t}
            )
            copy.start()
            row_copies.append(copy)
    summed = own[...]
    for copy in row_copies:
        copy.wait_recv()
    for e in range(nr - 1):
        summed = summed + rbuf[e].astype(F32)
    hidden = summed.astype(BF16)
    for load in small:
        load.wait()
    preact = jnp.dot(hidden, weight_ref[...], preferred_element_type=F32) + bias_ref[...]
    sig = jax.nn.sigmoid(preact)
    pre_grad = og_ref[...].astype(F32) * (sig * (1.0 + preact * (1.0 - sig)))
    half = pre_grad.astype(BF16)
    dest = lax.dot_general(
        half, weight_ref[...], (((1,), (1,)), ((), ())), preferred_element_type=F32
    )
    gg[r] = dest.astype(BF16)

    def hop(t, step):
        way = 0 if step > 0 else 1
        return send(gg.at[t], gg.at[t], g_send.at[way, t], g_recv.at[t], {"row": r + step})

    for step in (1, -1):
        @pl.when((r + step >= 0) & (r + step < nr))
        def start_chain(step=step):
            hop(r, step).start()
    grads_ref[pl.ds(nr * rows, rows), :] = (preact * sig).astype(BF16)
    feat = hidden.shape[1]
    cut = feat // nc
    w_out[:, pl.ds(0, cut), :] = scale * lax.dot_general(
        hidden, half, (((0,), (0,)), ((), ())), preferred_element_type=F32
    ).reshape(nc, cut, feat)
    w_out[:, pl.ds(cut, 8), :] = jnp.broadcast_to(
        scale * jnp.sum(pre_grad, axis=0, keepdims=True), (nc, 8, feat)
    )
    w_copies = []
    for d in range(1, nc):
        there = lax.rem(c + d, nc)
        copy = send(w_out.at[there], w_in.at[d - 1], w_send.at[d - 1], w_recv.at[d - 1], {"col": there})
        copy.start()
        w_copies.append(copy)
    for k in range(1, nr):
        if k == min(2, nr - 1):
            total = w_out[c]
            for d in range(1, nc):
                w_copies[d - 1].wait_recv()
                total = total + w_in[d - 1]
            w_all[c] = total
            for d in range(1, nc):
                there = lax.rem(c + d, nc)
                copy = send(w_all.at[c], w_all.at[c], wa_send.at[d - 1], wa_recv.at[d - 1], {"col": there})
                copy.start()
                w_copies.append(copy)
        for step in (1, -1):
            t = r - k * step
            came = (t >= 0) & (t < nr)

            @pl.when(came)
            def arrive(t=t, step=step):
                hop(t, step).wait_recv()

            @pl.when(came & (r + step >= 0) & (r + step < nr))
            def pass_on(t=t, step=step):
                hop(t, step).start()
    for k in range(nr):
        for step in (1, -1):
            t = r - k * step

            @pl.when((t >= 0) & (t < nr) & (r + step >= 0) & (r + step < nr))
            def sent(t=t, step=step):
                hop(t, step).wait_send()
    for copy in w_copies[nc - 1 :]:
        copy.wait_recv()
    for n in range(nc):
        wb_ref[pl.ds(n * cut, cut), :] = w_all[n, pl.ds(0, cut), :]
    wb_ref[pl.ds(feat, 8), :] = w_all[0, pl.ds(cut, 8), :]
    grads_ref[pl.ds(0, nr * rows), :] = gg[...].reshape(nr * rows, feat)
    for copy in row_copies + w_copies:
        copy.wait_send()


def backward_kernel(cols_ref, counts_ref, adj_ref, grad_ref, out_ref, act_out, sem, *accs):
    blocks, tile, slot_width = adj_ref.shape
    per_row = slot_width // tile
    dead = out_ref.shape[0]
    hand_out = pltpu.make_async_copy(grad_ref.at[pl.ds(blocks * tile, act_out.shape[0])], act_out, sem)
    hand_out.start()
    for acc in accs:
        acc[...] = jnp.zeros_like(acc)

    pace = math.gcd(blocks, 4)

    def block_rows(n, carry):
        contribs = []
        for i in range(pace):
            b = n * pace + i
            contribs.append(lax.dot_general(
                adj_ref[b], grad_ref[pl.ds(pl.multiple_of(b * tile, tile), tile), :],
                (((0,), (0,)), ((), ())), preferred_element_type=F32,
            ))
        for s in range(per_row):
            for i in range(pace):
                b = n * pace + i
                acc = accs[i]
                j = jnp.where(s < counts_ref[0, b], cols_ref[s, b], dead)
                acc[j] = acc[j] + contribs[i][s * tile : (s + 1) * tile]
        return carry

    lax.fori_loop(0, blocks // pace, block_rows, 0)
    total = accs[0][pl.ds(0, dead)]
    for acc in accs[1:]:
        total = total + acc[pl.ds(0, dead)]
    out_ref[...] = total.astype(BF16)
    hand_out.wait()


def scatter_kernel(
    nc, nr, part_ref, wb_ref, out_ref, wg_ref, bg_ref,
    from_pair, send_buf, from_chip, w_row,
    p_send, p_recv, s_send, s_recv, wr_send, wr_recv,
):
    n_out = nc // 2
    c, partner, ahead, behind = col_peers(nc)
    r = lax.axis_index("row")
    row_at = [lax.rem(r + e, nr) for e in range(nr)]
    partner_ahead = [x + partner - c for x in ahead]
    enter(nc, nr)

    started = []

    def go(*args):
        copy = send(*args)
        copy.start()
        started.append(copy)
        return copy

    order = list(range(1, n_out)) + [0]
    pair = {}
    for d in order:
        pair[d] = go(part_ref.at[partner_ahead[d]], from_pair.at[d], p_send.at[d], p_recv.at[d], {"col": partner})
    w_row[r] = wb_ref[...]
    w_copies = [
        go(w_row.at[r], w_row.at[r], wr_send.at[e - 1], wr_recv.at[e - 1], {"row": row_at[e]})
        for e in range(1, nr)
    ]
    copies = []
    for d in order:
        pair[d].wait_recv()
        both = part_ref[ahead[d]].astype(F32) + from_pair[d].astype(F32)
        if d:
            send_buf[d - 1] = both.astype(BF16)
            copies.append(go(
                send_buf.at[d - 1], from_chip.at[d - 1], s_send.at[d - 1], s_recv.at[d - 1], {"col": ahead[d]}
            ))
    for copy in copies:
        copy.wait_recv()
    for d in range(1, n_out):
        both = both + from_chip[d - 1].astype(F32)
    out_ref[...] = both.astype(BF16)
    for copy in w_copies:
        copy.wait_recv()
    total = w_row[0]
    for n in range(1, nr):
        total = total + w_row[n]
    feat = wg_ref.shape[0]
    wg_ref[...] = total[:feat]
    bg_ref[...] = total[feat : feat + 1]
    for copy in started:
        copy.wait_send()


def on_device(mesh, features, adjacency, tile_cols, row_counts, weight, bias, out_grad):
    blocks, tile, slot_width = adjacency.shape
    own_rows, feat = features.shape
    nc, nr = mesh.shape["col"], mesh.shape["row"]
    n_out = nc // 2
    col_blocks = nc * own_rows // tile
    scale = 1.0 / math.sqrt(own_rows * nc * nr)
    cut = feat // nc

    vmem = pl.BlockSpec(memory_space=pltpu.VMEM)
    smem = pl.BlockSpec(memory_space=pltpu.SMEM)
    hbm = pl.BlockSpec(memory_space=pltpu.HBM)
    dma = pltpu.SemaphoreType.DMA
    rows = blocks * tile // nr
    tile_flops = 2 * blocks * tile * slot_width * feat
    grads, wb = pl.pallas_call(
        functools.partial(forward_kernel, nc, nr, scale),
        out_shape=(
            jax.ShapeDtypeStruct((blocks * tile + rows, feat), BF16),
            jax.ShapeDtypeStruct((feat + 8, feat), F32),
        ),
        in_specs=[smem, smem, hbm, hbm, hbm, hbm, hbm],
        out_specs=(vmem, vmem),
        scratch_shapes=[
            pltpu.VMEM((col_blocks + 1, tile, feat), BF16),
            pltpu.VMEM(adjacency.shape, BF16),
            pltpu.VMEM((feat, feat), BF16),
            pltpu.VMEM((1, feat), F32),
            pltpu.VMEM((rows, feat), BF16),
            pltpu.VMEM((rows, feat), F32),
            pltpu.VMEM((nr - 1, rows, feat), BF16),
            pltpu.VMEM((nr - 1, rows, feat), BF16),
            pltpu.VMEM((nr, rows, feat), BF16),
            pltpu.VMEM((nc, cut + 8, feat), F32),
            pltpu.VMEM((nc - 1, cut + 8, feat), F32),
            pltpu.VMEM((nc, cut + 8, feat), F32),
            dma((4,)), dma((nr,)), dma((n_out,)), dma((n_out,)), dma((n_out,)), dma((n_out,)),
            dma((nr - 1,)), dma((nr - 1,)), dma((2, nr)), dma((nr,)),
            dma((nc - 1,)), dma((nc - 1,)), dma((nc - 1,)), dma((nc - 1,)),
        ],
        compiler_params=pltpu.CompilerParams(
            collective_id=0, has_side_effects=True, vmem_limit_bytes=56 * MIB
        ),
        cost_estimate=pl.CostEstimate(
            flops=tile_flops, bytes_accessed=adjacency.size * 2, transcendentals=rows * feat
        ),
    )(
        tile_cols.T, row_counts.T, features.reshape(own_rows // tile, tile, feat), adjacency, weight,
        bias.reshape(1, -1), out_grad,
    )

    partial, activations = pl.pallas_call(
        backward_kernel,
        out_shape=(
            jax.ShapeDtypeStruct((col_blocks, tile, feat), BF16),
            jax.ShapeDtypeStruct((rows, feat), BF16),
        ),
        in_specs=[smem, smem, vmem, vmem],
        out_specs=(vmem, hbm),
        scratch_shapes=[dma] + [pltpu.VMEM((col_blocks + 1, tile, feat), F32) for unused in range(4)],
        compiler_params=pltpu.CompilerParams(vmem_limit_bytes=32 * MIB),
        cost_estimate=pl.CostEstimate(
            flops=tile_flops * 8, bytes_accessed=adjacency.size * 2, transcendentals=0
        ),
    )(tile_cols.T, row_counts.T, adjacency, grads)

    feature_grad, weight_grad, bias_grad = pl.pallas_call(
        functools.partial(scatter_kernel, nc, nr),
        out_shape=(
            jax.ShapeDtypeStruct((own_rows, feat), BF16),
            jax.ShapeDtypeStruct((feat, feat), F32),
            jax.ShapeDtypeStruct((1, feat), F32),
        ),
        in_specs=[vmem, vmem],
        out_specs=(vmem, vmem, vmem),
        scratch_shapes=[
            pltpu.VMEM((n_out, own_rows, feat), BF16),
            pltpu.VMEM((n_out - 1, own_rows, feat), BF16),
            pltpu.VMEM((n_out - 1, own_rows, feat), BF16),
            pltpu.VMEM((nr, feat + 8, feat), F32),
            dma((n_out,)), dma((n_out,)), dma((n_out - 1,)), dma((n_out - 1,)),
            dma((nr - 1,)), dma((nr - 1,)),
        ],
        compiler_params=pltpu.CompilerParams(
            collective_id=1, has_side_effects=True, vmem_limit_bytes=20 * MIB
        ),
        cost_estimate=pl.CostEstimate(
            flops=own_rows * nc * feat, bytes_accessed=8 * own_rows * nc * feat, transcendentals=0
        ),
    )(partial.reshape(nc, own_rows, feat), wb)
    return (activations, feature_grad, weight_grad, bias_grad.reshape(-1))


GROUP = 4


def slot_tables(cols_ref, counts_ref, col_blocks, mine, tab_ref):
    per_row, blocks = cols_ref.shape
    slots = per_row * blocks
    groups = half_groups(slots, col_blocks)
    keys = 2 * col_blocks

    def iota(shape, axis):
        return lax.broadcasted_iota(jnp.int32, shape, axis)

    def upright(row):
        n = row.shape[1]
        return jnp.sum(jnp.where(iota((n, n), 0) == iota((n, n), 1), row, 0), axis=1, keepdims=True)

    lane = iota((blocks, keys), 1)
    block = iota((blocks, 1), 0)
    late = jnp.where((block >= mine) & (block < mine + blocks // 2), 0, col_blocks)
    counts = upright(counts_ref[...])
    seen = jnp.zeros((blocks, keys), jnp.int32)
    hits, ranks = [], []
    for s in range(per_row):
        hit = jnp.where((upright(cols_ref[pl.ds(s, 1), :]) + late == lane) & (counts > s), 1, 0)
        hits.append(hit)
        ranks.append(seen)
        seen = seen + hit
    earlier = jnp.zeros((blocks, keys), jnp.int32)
    for b in range(blocks - 1):
        earlier = earlier + jnp.where(block > b, seen[b : b + 1, :], 0)
    sizes = lax.shift_right_logical(jnp.sum(seen, axis=0, keepdims=True) + (GROUP - 1), 2)
    square = (keys, keys)
    first, second = iota(square, 0), iota(square, 1)
    lower = (first < second) & ((first < col_blocks) == (second < col_blocks))
    starts = jnp.sum(jnp.where(lower, upright(sizes), 0), axis=0, keepdims=True)
    starts = starts + jnp.where(iota((1, keys), 1) < col_blocks, 0, groups)
    places = -(-2 * GROUP * groups // 128) * 128
    heads = -(-2 * groups // 128) * 128
    place = iota((blocks, places), 1)
    head = iota((blocks, heads), 1) * GROUP
    found = jnp.zeros((blocks, places), jnp.int32)
    fresh = jnp.zeros((blocks, heads), jnp.int32)
    for s in range(per_row):
        rank = jnp.sum(hits[s] * (ranks[s] + earlier), axis=1, keepdims=True)
        at = jnp.sum(hits[s] * (GROUP * starts), axis=1, keepdims=True) + rank
        at = jnp.where(counts > s, at, -1)
        found = found + jnp.where(at == place, slots - (block * per_row + s), 0)
        fresh = fresh + jnp.where((at == head) & (rank == 0), 1, 0)
    found = slots - jnp.sum(found, axis=0, keepdims=True)
    fresh = jnp.sum(fresh, axis=0, keepdims=True)
    last = jnp.where(sizes > 0, starts + sizes - 1, 2 * groups)
    n = 0
    for value in (found, fresh):
        for k in range(value.shape[1] // 128):
            tab_ref[pl.ds(n, 1), :] = value[:, k * 128 : (k + 1) * 128]
            n += 1
    tab_ref[pl.ds(n, 1), pl.ds(0, keys)] = last


def square_peers():
    c = lax.axis_index("col")
    y, x, core = c // 4, c // 2 % 2, c % 2

    def at(dy, dx):
        return (y + dy) % 2 * 4 + (x + dx) % 2 * 2 + core

    return c, c + 1 - 2 * core, [c, at(1, 1), at(0, 1), at(1, 0)]


def half_groups(slots, col_blocks):
    most = (slots // 2 + (GROUP - 1) * min(col_blocks, slots // 2)) // GROUP
    return -(-most // 8) * 8


def layer_kernel(
    nc, nr, scale, cols_hbm, counts_hbm, feat_hbm, adj_hbm, weight_hbm, bias_hbm, og_hbm,
    fg_ref, act_ref, wb_ref,
    cols_s, counts_s, tab_s, cols_v, counts_v, tab_v,
    xg, adj, weight_ref, bias_ref, og_ref, pf, part, near, far, hid, half, bias_sum, gg,
    contrib, runs, pair_out, pair_in, chip_out, chip_in, kept,
    w_out, w_in, w_row, w_all,
    in_sem, a_sem, f_send, f_recv, n_send, n_recv, r_send, r_recv,
    g_send, g_recv, gp_send, gp_recv, gc_send, gc_recv,
    w_send, w_recv, wr_send, wr_recv, wa_send, wa_recv,
):
    blocks, tile, slot_width = adj.shape
    per_row = slot_width // tile
    slots = blocks * per_row
    chunk = blocks // nr
    rows = chunk * tile
    n_out = nc // 2
    own_blocks = feat_hbm.shape[0]
    col_blocks = nc * own_blocks
    feat = weight_ref.shape[0]
    groups = half_groups(slots, col_blocks)
    cuts = 4
    fresh_at = -(-2 * GROUP * groups // 128)
    last_at = fresh_at + -(-2 * groups // 128)
    step = rows // cuts
    c, partner, ahead = square_peers()
    r = lax.axis_index("row")

    barrier = pltpu.get_barrier_semaphore()
    for d in range(1, nc):
        pl.semaphore_signal(barrier, inc=1, device_id={"col": lax.rem(c + d, nc)}, device_id_type=MESH)
    for e in range(1, nr):
        pl.semaphore_signal(barrier, inc=1, device_id={"row": lax.rem(r + e, nr)}, device_id_type=MESH)

    half_blocks = own_blocks // 2
    odd, even = c % 2 == 1, c % 2 == 0
    chip_x, chip_y, chip_d = [ahead[n] - c % 2 for n in (2, 3, 1)]

    def feat_part(col, h):
        return xg.at[pl.ds(col * own_blocks + h * half_blocks, half_blocks)]

    def give(slot, src, col, h, there):
        return send(src, feat_part(col, h), f_send.at[slot], f_recv.at[col, h], {"col": there})

    first = []
    for h in range(2):
        mine = feat_hbm.at[pl.ds(h * half_blocks, half_blocks)]
        first.append((h, give(h, mine, c, h, chip_x + 1)))
        first.append((1 - h, give(2 + h, mine, c, h, chip_y + 1)))
        first.append((2 + h, give(4 + h, mine, c, h, partner)))
    first = [copy for unused, copy in sorted(first, key=lambda pair: pair[0])]

    relays, keeps, last_ones = [], [], []
    for k in (1, 0):
        relays.append((chip_x + k, 0, chip_y + 1))
        relays.append((chip_y + k, 1, chip_x + 1))
        keeps += [(chip_x + k, 1), (chip_y + k, 0)]
        last_ones += [(chip_d + k, 0), (chip_d + k, 1)]
    inside = [(col, h) for col, h, unused in relays] + keeps + last_ones
    relays = [give(6 + n, feat_part(col, h), col, h, there) for n, (col, h, there) in enumerate(relays)]
    inside = [give(10 + n, feat_part(col, h), col, h, partner) for n, (col, h) in enumerate(inside)]

    pl.semaphore_wait(barrier, nc - 1 + nr - 1)
    for copy in first:
        copy.start()

    loads = {}
    for n, (name, src, dst) in enumerate((
        ("cols_v", cols_hbm, cols_v), ("counts_v", counts_hbm, counts_v),
        ("feat", feat_hbm, xg.at[pl.ds(c * own_blocks, own_blocks)]), ("cols_s", cols_hbm, cols_s),
        ("counts_s", counts_hbm, counts_s),
        ("weight", weight_hbm, weight_ref), ("bias", bias_hbm, bias_ref), ("og", og_hbm, og_ref),
    )):
        loads[name] = pltpu.make_async_copy(src, dst, in_sem.at[n])
        loads[name].start()

    mirrored = r >= 2
    inner = (r == 1) | (r == 2)
    outer = (r == 0) | (r == 3)

    def place(d):
        return jnp.where(mirrored, 3 - d, d)

    mate = jnp.where(r % 2 == 0, r + 1, r - 1)
    targets = [place(3), place(2), mate, r]
    for e in range(nr):
        cut = pl.ds(targets[e] * chunk, chunk)
        load = pltpu.make_async_copy(adj_hbm.at[cut], adj.at[cut], a_sem.at[e])
        load.start()
        loads[e] = load

    xg[col_blocks] = jnp.zeros(xg.shape[1:], xg.dtype)
    contrib[slots] = jnp.zeros(contrib.shape[1:], F32)
    runs[2 * groups] = jnp.zeros(runs.shape[1:], F32)

    @pl.when(odd)
    def relay():
        for n in range(4):
            inside[n].wait_recv()
            relays[n].start()
            inside[n].start()

    loads["cols_v"].wait()
    loads["counts_v"].wait()
    slot_tables(cols_v, counts_v, col_blocks, r // 2 * (blocks // 2), tab_v)
    table = pltpu.make_async_copy(tab_v, tab_s, in_sem.at[8])
    table.start()

    @pl.when(odd)
    def pass_inside():
        for n in range(4, 12):
            inside[n].wait_recv()
            inside[n].start()

    @pl.when(even)
    def take_inside():
        for n in range(12):
            inside[n].wait_recv()

    for name in ("feat", "cols_s", "counts_s"):
        loads[name].wait()
    table.wait()
    for h in range(2):
        give(4 + h, feat_part(partner, h), partner, h, partner).wait_recv()

    def piece(q):
        return pl.ds(q * step, step)

    def to_near(e, q):
        return send(part.at[e, piece(q)], near.at[e, piece(q)], n_send.at[e, q], n_recv.at[e, q], {"row": mate})

    def to_far(e, q):
        return send(part.at[e, piece(q)], far.at[piece(q)], r_send.at[e, q], r_recv.at[q], {"row": targets[e]})

    def products(e, q):
        def block_rows(n, carry):
            for i in range(2):
                i = q * (chunk // cuts) + n * 2 + i
                b = targets[e] * chunk + i
                count = counts_s[0, b]
                picked = [xg[jnp.where(s < count, cols_s[s, b], col_blocks)] for s in range(per_row)]
                got = jnp.dot(adj[b], jnp.concatenate(picked, axis=0), preferred_element_type=F32)
                cut = pl.ds(pl.multiple_of(i * tile, tile), tile)
                pf[e, cut, :] = got
                if e < 3:
                    part[e, cut, :] = got.astype(BF16)
            return carry

        lax.fori_loop(0, chunk // cuts // 2, block_rows, 0)

    loads[0].wait()
    loads[1].wait()
    for e in range(2):
        for q in range(cuts):
            products(e, q)

            @pl.when(outer)
            def hand_in(e=e, q=q):
                to_near(e, q).start()
    for e in (2, 3):
        loads[e].wait()
        for q in range(cuts):
            products(e, q)
            if e == 2:
                to_near(e, q).start()
    for e in range(2):
        for q in range(cuts):
            @pl.when(inner)
            def join(e=e, q=q):
                to_near(e, q).wait_recv()
                part[e, piece(q), :] = (pf[e, piece(q), :] + near[e, piece(q), :].astype(F32)).astype(BF16)
                to_far(e, q).start()

    def to_mate(t, q):
        return send(gg.at[t, piece(q)], gg.at[t, piece(q)], g_send.at[0, t, q], g_recv.at[t, q], {"row": mate})

    def to_other(q):
        return send(gg.at[r, piece(q)], gg.at[r, piece(q)], g_send.at[1, r, q], g_recv.at[r, q], {"row": place(2)})

    for name in ("weight", "bias", "og"):
        loads[name].wait()
    bias_part = jnp.zeros((1, feat), F32)
    for q in range(cuts):
        cut = piece(q)
        to_near(2, q).wait_recv()
        to_far(0, q).wait_recv()
        hidden = (pf[3, cut, :] + near[2, cut, :].astype(F32) + far[cut, :].astype(F32)).astype(BF16)
        preact = jnp.dot(hidden, weight_ref[...], preferred_element_type=F32) + bias_ref[...]
        sig = jax.nn.sigmoid(preact)
        pre_grad = og_ref[cut, :].astype(F32) * (sig * (1.0 + preact * (1.0 - sig)))
        small = pre_grad.astype(BF16)
        dest = lax.dot_general(small, weight_ref[...], (((1,), (1,)), ((), ())), preferred_element_type=F32)
        gg[r, cut, :] = dest.astype(BF16)
        to_mate(r, q).start()
        to_other(q).start()
        act_ref[cut, :] = (preact * sig).astype(BF16)
        hid[cut, :] = hidden
        half[cut, :] = small
        bias_part = bias_part + jnp.sum(pre_grad, axis=0, keepdims=True)
    bias_sum[...] = bias_part

    wcut = feat // nc

    def to_col(src, dst, sems, d):
        return send(src, dst, sems[0].at[d - 1], sems[1].at[d - 1], {"col": lax.rem(c + d, nc)})

    def w_first(d):
        return to_col(w_out.at[lax.rem(c + d, nc)], w_in.at[d - 1], (w_send, w_recv), d)

    def w_second(e):
        return send(w_row.at[r], w_row.at[r], wr_send.at[e - 1], wr_recv.at[e - 1], {"row": lax.rem(r + e, nr)})

    def w_third(d):
        return to_col(w_all.at[c], w_all.at[c], (wa_send, wa_recv), d)

    def weight_terms():
        w_out[:, pl.ds(0, wcut), :] = scale * lax.dot_general(
            hid[...], half[...], (((0,), (0,)), ((), ())), preferred_element_type=F32
        ).reshape(nc, wcut, feat)
        w_out[:, pl.ds(wcut, 8), :] = jnp.broadcast_to(scale * bias_sum[...], (nc, 8, feat))
        for d in range(1, nc):
            w_first(d).start()

    def weight_rows():
        total = w_out[c]
        for d in range(1, nc):
            w_first(d).wait_recv()
            total = total + w_in[d - 1]
        w_row[r] = total
        for e in range(1, nr):
            w_second(e).start()

    def weight_whole():
        for e in range(1, nr):
            w_second(e).wait_recv()
        total = w_row[0]
        for n in range(1, nr):
            total = total + w_row[n]
        w_all[c] = total
        for d in range(1, nc):
            w_third(d).start()

    def contribute(t, q):
        def pairs(n, carry):
            b = t * chunk + q * (chunk // cuts) + n * 2
            lhs = adj[pl.ds(b, 2)].reshape(2 * tile, slot_width)
            g = gg[t, pl.ds(pl.multiple_of(q * step + n * 2 * tile, 2 * tile), 2 * tile), :]
            upper = lax.broadcasted_iota(jnp.int32, g.shape, 0) < tile
            zero = jnp.zeros_like(g)
            rhs = jnp.concatenate([jnp.where(upper, g, zero), jnp.where(upper, zero, g)], axis=1)
            got = lax.dot_general(lhs, rhs, (((0,), (0,)), ((), ())), preferred_element_type=F32)
            contrib[pl.ds(b * per_row, per_row)] = got[:, :feat].reshape(per_row, tile, feat)
            contrib[pl.ds(b * per_row + per_row, per_row)] = got[:, feat:].reshape(per_row, tile, feat)
            return carry

        lax.fori_loop(0, chunk // cuts // 2, pairs, 0)

    def gather(part_of, low=0, high=tile):
        span = pl.ds(low, high - low)

        def add_up(n, acc):
            spot = part_of * GROUP * groups + n * 8 * GROUP
            head = part_of * groups + n * 8
            for u in range(8):
                terms = [contrib[tab_s[spot // 128, spot % 128 + u * GROUP + k], span, :] for k in range(GROUP)]
                new = tab_s[fresh_at + head // 128, head % 128 + u]
                acc = jnp.where(new > 0, 0.0, acc) + ((terms[0] + terms[1]) + (terms[2] + terms[3]))
                runs[head + u, span, :] = acc
            return acc

        lax.fori_loop(0, groups // 8, add_up, jnp.zeros((high - low, feat), F32))

    near_in, far_in = place(2), place(3)
    from_in = [(r, q) for q in range(cuts)]
    from_out = from_in + [(mate, q) for q in range(cuts)]
    passed = []
    for q in range(cuts):
        from_in += [(mate, q), (near_in, q), (far_in, q)]
        from_out += [(near_in, q), (far_in, q)]
        passed += [(near_in, q), (far_in, q)]
    for k in range(4 * cuts):
        if 2 <= k < 2 + len(passed):
            @pl.when(inner)
            def pass_on(t=passed[k - 2][0], q=passed[k - 2][1]):
                to_mate(t, q).wait_recv()
                to_mate(t, q).start()
        if k == 0:
            weight_terms()
        if k == 2 + len(passed):
            pl.when(inner)(weight_rows)
        if k == 2 * cuts:
            @pl.when(outer)
            def early():
                weight_rows()
                gather(0)
        if k >= cuts:
            @pl.when(outer)
            def came(k=k):
                to_mate(*from_out[k]).wait_recv()
        if from_in[k][0] is mate:
            @pl.when(inner)
            def mate_came(k=k):
                to_mate(*from_in[k]).wait_recv()
        contribute(
            jnp.where(inner, from_in[k][0], from_out[k][0]), jnp.where(inner, from_in[k][1], from_out[k][1])
        )

    hrows = tile // 2
    order = list(range(1, n_out)) + [0]

    def to_pair(h, d):
        return send(pair_out.at[h, d], pair_in.at[h, d], gp_send.at[h, d], gp_recv.at[h, d], {"col": partner})

    def to_chip(h, d):
        return send(
            chip_out.at[h, d - 1], chip_in.at[h, d - 1], gc_send.at[h, d - 1], gc_recv.at[h, d - 1], {"col": ahead[d]}
        )

    def totals(col, h):
        lines = [(tab_s[last_at, col * own_blocks + n], tab_s[last_at, col_blocks + col * own_blocks + n])
                 for n in range(own_blocks)]
        cut = pl.ds(h * hrows, hrows)
        return jnp.concatenate([runs[a, cut, :] + runs[b, cut, :] for a, b in lines], axis=0)

    def hand_over(h):
        for d in order:
            pair_out[h, d] = totals(ahead[d] + partner - c, h).astype(BF16)
            to_pair(h, d).start()

    def combine(h):
        for d in order:
            mine = totals(ahead[d], h)
            to_pair(h, d).wait_recv()
            both = mine + pair_in[h, d].astype(F32)
            if d:
                chip_out[h, d - 1] = both.astype(BF16)
                to_chip(h, d).start()
            else:
                kept[h] = both

    @pl.when(inner)
    def late():
        gather(0)

    weight_whole()
    gather(1)
    hand_over(0)
    hand_over(1)
    combine(0)
    combine(1)
    for copy in first:
        copy.wait_send()

    @pl.when(odd)
    def odd_sent():
        for copy in relays + inside:
            copy.wait_send()

    for d in range(1, nc):
        w_first(d).wait_send()
    for e in range(1, nr):
        w_second(e).wait_send()
    for q in range(cuts):
        to_near(2, q).wait_send()
        to_other(q).wait_send()
        to_mate(r, q).wait_send()

    @pl.when(outer)
    def outer_sent():
        for e in range(2):
            for q in range(cuts):
                to_near(e, q).wait_send()

    @pl.when(inner)
    def inner_sent():
        for e in range(2):
            for q in range(cuts):
                to_far(e, q).wait_send()
                to_mate(targets[e], q).wait_send()

    for h in range(2):
        for d in range(n_out):
            to_pair(h, d).wait_send()
    for d in range(1, nc):
        w_third(d).wait_recv()
    for n in range(nc):
        wb_ref[pl.ds(n * wcut, wcut), :] = w_all[n, pl.ds(0, wcut), :]
    wb_ref[pl.ds(feat, 8), :] = w_all[0, pl.ds(wcut, 8), :]
    for h in range(2):
        for d in range(1, n_out):
            to_chip(h, d).wait_recv()
        both = kept[h]
        for d in range(1, n_out):
            both = both + chip_in[h, d - 1].astype(F32)
        both = both.astype(BF16)
        for n in range(own_blocks):
            fg_ref[pl.ds(n * tile + h * hrows, hrows), :] = both[n * hrows : (n + 1) * hrows]
    for h in range(2):
        for d in range(1, n_out):
            to_chip(h, d).wait_send()
    for d in range(1, nc):
        w_third(d).wait_send()


def finish_kernel(fg_in, act_in, wb_in, act_out, fg_out, wg_out, bg_out, sem):
    feat = wg_out.shape[0]
    copies = []
    for n, (src, dst) in enumerate((
        (fg_in, fg_out), (act_in, act_out), (wb_in.at[pl.ds(0, feat)], wg_out), (wb_in.at[pl.ds(feat, 1)], bg_out),
    )):
        copy = pltpu.make_async_copy(src, dst, sem.at[n])
        copy.start()
        copies.append(copy)
    for copy in copies:
        copy.wait()


def whole_layer(mesh, features, adjacency, tile_cols, row_counts, weight, bias, out_grad):
    blocks, tile, slot_width = adjacency.shape
    own_rows, feat = features.shape
    nc, nr = mesh.shape["col"], mesh.shape["row"]
    n_out = nc // 2
    own_blocks = own_rows // tile
    col_blocks = nc * own_blocks
    per_row = slot_width // tile
    slots = blocks * per_row
    scale = 1.0 / math.sqrt(own_rows * nc * nr)
    cut = feat // nc
    rows = blocks * tile // nr
    groups = half_groups(slots, col_blocks)
    table_rows = -(-2 * GROUP * groups // 128) + -(-2 * groups // 128) + 1
    table_rows = -(-table_rows // 8) * 8

    vmem = pl.BlockSpec(memory_space=pltpu.VMEM)
    hbm = pl.BlockSpec(memory_space=pltpu.HBM)
    dma = pltpu.SemaphoreType.DMA
    tile_flops = 2 * blocks * tile * slot_width * feat
    fg, act, wb = pl.pallas_call(
        functools.partial(layer_kernel, nc, nr, scale),
        out_shape=(
            pltpu.VMEM((own_rows, feat), BF16),
            pltpu.VMEM((rows, feat), BF16),
            pltpu.VMEM((feat + 8, feat), F32),
        ),
        in_specs=[hbm] * 7,
        out_specs=(vmem, vmem, vmem),
        scratch_shapes=[
            pltpu.SMEM((per_row, blocks), jnp.int32),
            pltpu.SMEM((1, blocks), jnp.int32),
            pltpu.SMEM((table_rows, 128), jnp.int32),
            pltpu.VMEM((per_row, blocks), jnp.int32),
            pltpu.VMEM((1, blocks), jnp.int32),
            pltpu.VMEM((table_rows, 128), jnp.int32),
            pltpu.VMEM((col_blocks + 1, tile, feat), BF16),
            pltpu.VMEM(adjacency.shape, BF16),
            pltpu.VMEM((feat, feat), BF16),
            pltpu.VMEM((1, feat), F32),
            pltpu.VMEM((rows, feat), BF16),
            pltpu.VMEM((nr, rows, feat), F32),
            pltpu.VMEM((3, rows, feat), BF16),
            pltpu.VMEM((3, rows, feat), BF16),
            pltpu.VMEM((rows, feat), BF16),
            pltpu.VMEM((rows, feat), BF16),
            pltpu.VMEM((rows, feat), BF16),
            pltpu.VMEM((1, feat), F32),
            pltpu.VMEM((nr, rows, feat), BF16),
            pltpu.VMEM((slots + 1, tile, feat), F32),
            pltpu.VMEM((2 * groups + 1, tile, feat), F32),
            pltpu.VMEM((2, n_out, own_rows // 2, feat), BF16),
            pltpu.VMEM((2, n_out, own_rows // 2, feat), BF16),
            pltpu.VMEM((2, n_out - 1, own_rows // 2, feat), BF16),
            pltpu.VMEM((2, n_out - 1, own_rows // 2, feat), BF16),
            pltpu.VMEM((2, own_rows // 2, feat), F32),
            pltpu.VMEM((nc, cut + 8, feat), F32),
            pltpu.VMEM((nc - 1, cut + 8, feat), F32),
            pltpu.VMEM((nr, cut + 8, feat), F32),
            pltpu.VMEM((nc, cut + 8, feat), F32),
            dma((9,)), dma((nr,)), dma((22,)), dma((nc, 2)),
            dma((3, 4)), dma((3, 4)), dma((2, 4)), dma((4,)),
            dma((2, nr, 4)), dma((nr, 4)),
            dma((2, n_out)), dma((2, n_out)), dma((2, n_out - 1)), dma((2, n_out - 1)),
            dma((nc - 1,)), dma((nc - 1,)), dma((nr - 1,)), dma((nr - 1,)), dma((nc - 1,)), dma((nc - 1,)),
        ],
        compiler_params=pltpu.CompilerParams(
            collective_id=0, has_side_effects=True, vmem_limit_bytes=56 * MIB
        ),
        cost_estimate=pl.CostEstimate(
            flops=2 * tile_flops, bytes_accessed=adjacency.size * 2, transcendentals=rows * feat
        ),
    )(
        tile_cols.T, row_counts.T, features.reshape(own_blocks, tile, feat), adjacency, weight,
        bias.reshape(1, -1), out_grad,
    )
    activations, feature_grad, weight_grad, bias_grad = pl.pallas_call(
        finish_kernel,
        out_shape=(
            jax.ShapeDtypeStruct((rows, feat), BF16),
            jax.ShapeDtypeStruct((own_rows, feat), BF16),
            jax.ShapeDtypeStruct((feat, feat), F32),
            jax.ShapeDtypeStruct((1, feat), F32),
        ),
        in_specs=[vmem] * 3,
        out_specs=(hbm,) * 4,
        scratch_shapes=[dma((4,))],
        compiler_params=pltpu.CompilerParams(vmem_limit_bytes=2 * MIB),
    )(fg, act, wb)
    return (activations, feature_grad, weight_grad, bias_grad.reshape(-1))


def solution(mesh):
    small = mesh.shape["row"] == 4 and mesh.shape["col"] == 8
    placed = (
        P(("groups", "row", "col"), None),
        P(("groups", "col"), None, "row"),
        P(("groups", "col"), "row"),
        P(("groups", "col"), "row"),
        P(),
        P(),
        P(("groups", "col", "row"), None),
    )
    return jax.shard_map(
        functools.partial(whole_layer if small else on_device, mesh),
        mesh=mesh,
        in_specs=placed,
        out_specs=(
            P(("groups", "col", "row"), None),
            P(("groups", "row", "col"), None),
            P("groups", None),
            P("groups"),
        ),
        check_vma=False,
    )
```
